256 devices in a mesh: seq: 2 (over z_lo), shard: 128 (over x, z_hi, y, core).
Axes of the slice: x: 4, y: 4, z: 8 (z_hi: 4, z_lo: 2; z = z_hi * 2 + z_lo), core: 2. Of those that a mesh axis runs over, the one named last changes fastest.
Arguments:
- tokens: bfloat16 [65536, 768], P(('shard', 'seq')), may hold values from -24 to 24
- w_qkv: bfloat16 [768, 2304], P('shard'), may hold values from -0.3125 to 0.3125
- bias_q: bfloat16 [768], P('shard'), may hold values from -1.1953125 to 1.1953125
- bias_v: bfloat16 [768], P('shard'), may hold values from -1.1953125 to 1.1953125
- w_out: bfloat16 [768, 768], P('shard'), may hold values from -0.4375 to 0.4375
- bias_out: bfloat16 [768], P('shard'), may hold values from -1.1953125 to 1.1953125
- gain_one: bfloat16 [768], P('shard'), may hold values from 0.5 to 1.5
- shift_one: bfloat16 [768], P('shard'), may hold values from -1.1953125 to 1.1953125
- w_in: bfloat16 [768, 3072], P('shard'), may hold values from -0.21875 to 0.21875
- bias_in: bfloat16 [3072], P('shard'), may hold values from -1.1953125 to 1.1953125
- w_down: bfloat16 [3072, 768], P('shard'), may hold values from -0.15625 to 0.15625
- bias_down: bfloat16 [768], P('shard'), may hold values from -1.1953125 to 1.1953125
- gain_two: bfloat16 [768], P('shard'), may hold values from 0.5 to 1.5
- shift_two: bfloat16 [768], P('shard'), may hold values from -1.1953125 to 1.1953125
- doc_lengths: int32 [128], replicated, may hold values from 1 to 1024, 65536 in all
- cotangent: bfloat16 [65536, 768], P(('shard', 'seq')), may hold values from -6 to 6
Outputs:
- layer_out: bfloat16 [65536, 768], P(('shard', 'seq'))
- grad_tokens: float32 [65536, 768], P(('shard', 'seq'))
- grad_w_qkv: float32 [768, 2304], P('shard')
- grad_bias_q: float32 [768], P('shard')
- grad_bias_v: float32 [768], P('shard')
- grad_w_out: float32 [768, 768], P('shard')
- grad_bias_out: float32 [768], P('shard')
- grad_gain_one: float32 [768], P('shard')
- grad_shift_one: float32 [768], P('shard')
- grad_w_in: float32 [768, 3072], P('shard')
- grad_bias_in: float32 [3072], P('shard')
- grad_w_down: float32 [3072, 768], P('shard')
- grad_bias_down: float32 [768], P('shard')
- grad_gain_two: float32 [768], P('shard')
- grad_shift_two: float32 [768], P('shard')
The draws below stay inside these ranges and needn't reach their ends.
Inputs may be any that keep to these rules, and one draw needn't show every extreme that they name: `doc_lengths`: document lengths in stream order; the documents fill the 65536 tokens end to end, and the longest has exactly 1024 tokens.
All inputs are finite; a program needn't handle non-finite values.
Results may differ from the reference program's by a relative error of at most 0.025.
Values may be sent and summed in bfloat16 or wider, within the bound.
A program may use at most 192 MiB of HBM per device.

```python
import math
import jax
import jax.numpy as jnp
import numpy as np
from jax import lax

D = 768
HEADS = 12
HEAD_DIM = 64
FF = 3072
DOC_MAX = 1024
TOKENS = 65536
GROUP = 512
REACH = 2
DOCS = 128


def raised(array, own_key, source, target, shards_of, factor):
    def block_of(axis_at):
        return (jnp.arange(array.shape[axis_at]) // (array.shape[axis_at] // shards_of)).reshape((-1,) + (1,) * (array.ndim - 1 - axis_at))

    one_side = jax.random.permutation(own_key, shards_of)[block_of(target)]
    far = (block_of(target) + shards_of // 2) % shards_of
    return jnp.where((block_of(source) == one_side) | (block_of(source) == far), factor * array, array)


def shard_levels(key, shape, shards, smallest, largest):
    factor_of, own = 1.0, jax.random.fold_in(key, 6)
    for dim, shards_of in shards:
        draws = jnp.exp(jax.random.uniform(jax.random.fold_in(own, dim), (shards_of,), jnp.float32, smallest / len(shards), largest / len(shards)))
        factor_of = factor_of * jnp.repeat(draws, shape[dim] // shards_of).reshape([-1 if axis == dim else 1 for axis in range(len(shape))])
    return factor_of


def length_profile(count, total, most, lean):
    portions = [(1 << 20) // math.isqrt(standing ** lean) + 1 for standing in range(2, count + 1)]
    surplus, counts = total - most - (count - 1), [1] * (count - 1)
    while surplus > 0:
        free = [i for i in range(count - 1) if counts[i] < most]
        mass, budget = sum([portions[i] for i in free]), surplus
        for i in free:
            more = min(most - counts[i], max(1, budget * portions[i] // mass), surplus)
            counts[i] = counts[i] + more
            surplus = surplus - more
    return np.array([most] + counts)


def ragged(rng, number_of, total, reach, slope):
    if number_of == 2:
        one = jax.random.randint(rng, (), max(1, total - reach), min(reach, total - 1) + 1)
        return jnp.stack([one, total - one])
    sizes = jnp.asarray(length_profile(number_of, total, reach, slope), jnp.int32)
    twos = (number_of - 1) // 2
    giver, receiver = sizes[1:1 + 2 * twos:2], sizes[2:2 + 2 * twos:2]
    margin = jnp.minimum(giver - 1, reach - receiver)
    moved = jax.random.randint(jax.random.fold_in(rng, 1), (twos,), 0, 1 << 20) % (margin + 1)
    sizes = sizes.at[1:1 + 2 * twos:2].set(giver - moved).at[2:2 + 2 * twos:2].set(receiver + moved)
    return sizes[jax.random.permutation(jax.random.fold_in(rng, 2), number_of)]


def bell_draw(own_key, extent, scale, limit, cuts=(), kind=jnp.bfloat16):
    array = scale * jax.random.normal(own_key, extent, jnp.float32)
    if cuts:
        array = array * shard_levels(own_key, extent, cuts, -0.22, 0.18)
    return jnp.clip(array, -limit, limit).astype(kind)


def gaussian_with(rng, extent, width, limit, pieces, heavy, kind=jnp.bfloat16):
    array = width * jax.random.normal(rng, extent, jnp.float32)
    if pieces:
        array = array * shard_levels(rng, extent, pieces, -0.22, 0.18)
    return jnp.clip(raised(array, jax.random.fold_in(rng, 3), *heavy), -limit, limit).astype(kind)


def setup_inputs(seed: int = 0) -> dict:
    arg_keys = jax.random.split(jax.random.key(seed), 17)
    return {
        "tokens": gaussian_with(arg_keys[0], (TOKENS, D), 1.0, 24.0, ((0, 256),), (0, 1, 256, 6.0)),
        "w_qkv": bell_draw(arg_keys[1], (D, 3 * D), (D // 2) ** -0.5, 0.3125, ((0, 128),)),
        "bias_q": bell_draw(arg_keys[2], (D,), 0.2, 1.1953125, ((0, 128),)),
        "bias_v": bell_draw(arg_keys[3], (D,), 0.2, 1.1953125, ((0, 128),)),
        "w_out": bell_draw(arg_keys[4], (D, D), (D // 4) ** -0.5, 0.4375, ((0, 128),)),
        "bias_out": bell_draw(arg_keys[5], (D,), 0.2, 1.1953125, ((0, 128),)),
        "gain_one": jnp.clip(1.0 + 0.1 * jax.random.normal(arg_keys[6], (D,), jnp.float32), 0.5, 1.5).astype(jnp.bfloat16),
        "shift_one": bell_draw(arg_keys[7], (D,), 0.2, 1.1953125, ((0, 128),)),
        "w_in": bell_draw(arg_keys[8], (D, FF), D ** -0.5, 0.21875, ((0, 128),)),
        "bias_in": bell_draw(arg_keys[9], (FF,), 0.2, 1.1953125, ((0, 128),)),
        "w_down": bell_draw(arg_keys[10], (FF, D), (FF // 2) ** -0.5, 0.15625, ((0, 128),)),
        "bias_down": bell_draw(arg_keys[11], (D,), 0.2, 1.1953125, ((0, 128),)),
        "gain_two": jnp.clip(1.0 + 0.1 * jax.random.normal(arg_keys[12], (D,), jnp.float32), 0.5, 1.5).astype(jnp.bfloat16),
        "shift_two": bell_draw(arg_keys[13], (D,), 0.2, 1.1953125, ((0, 128),)),
        "doc_lengths": ragged(arg_keys[14], DOCS, TOKENS, DOC_MAX, 2).astype(jnp.int32),
        "cotangent": bell_draw(arg_keys[15], (TOKENS, D), 1.0, 6.0, ((0, 256),)),
    }


@jax.custom_vjp
def low(v):
    return lax.optimization_barrier(v.astype(jnp.bfloat16)).astype(jnp.float32)

@jax.custom_vjp
def low_back(v):
    return v

def low_keep(v):
    return (low(v), None)

def low_pass(kept, grad):
    return (grad,)

def back_keep(v):
    return (v, None)

def back_low(kept, grad):
    return (low(grad),)
low.defvjp(low_keep, low_pass)
low_back.defvjp(back_keep, back_low)
HIGHEST_PREC = lax.Precision.HIGHEST
MASKED_SCORE = -1e+30
NORM_EPS = 1e-12

def layer_norm(resid, gain_vec, shift_vec):
    row_mean = lax.optimization_barrier(jnp.mean(resid, axis=-1, keepdims=True))
    centred = resid - row_mean
    variance = lax.optimization_barrier(jnp.mean(centred * centred, axis=-1, keepdims=True))
    return centred * lax.rsqrt(variance + NORM_EPS) * gain_vec + shift_vec

def doc_index(doc_lengths, positions, stream_len):
    doc_ends = jnp.cumsum(doc_lengths, dtype=jnp.int32)
    starts = doc_ends - doc_lengths
    counted = lax.optimization_barrier(jnp.sum((positions[:, None] >= starts[None, :]).astype(jnp.int32), axis=1, dtype=jnp.int32)) - 1
    inside = (positions >= 0) & (positions < stream_len)
    return jnp.where(inside, counted, -1).astype(jnp.int32)

def reference(tokens, w_qkv, bias_q, bias_v, w_out, bias_out, gain_one, shift_one, w_in, bias_in, w_down, bias_down, gain_two, shift_two, doc_lengths, cotangent):
    group_rows = GROUP
    window = (2 * REACH + 1) * group_rows
    pad_rows = REACH * group_rows
    block_count = TOKENS // group_rows
    score_scale = HEAD_DIM ** (-0.5)
    positions = jnp.arange(TOKENS + 2 * pad_rows, dtype=jnp.int32) - pad_rows
    doc_all = doc_index(doc_lengths, positions, TOKENS)

    def forward(tok_in, qkv_w, q_bias, v_bias, out_w, out_bias, gain_a, shift_a, in_w, in_bias, down_w, down_bias, gain_b, shift_b):
        projected = jnp.dot(tok_in, qkv_w, precision=HIGHEST_PREC)
        queries = low(low_back(projected[:, :D] + q_bias))
        keys_all = low(low_back(projected[:, D:2 * D]))
        values_all = low(low_back(projected[:, 2 * D:] + v_bias))
        keys_pad = jnp.pad(keys_all, ((pad_rows, pad_rows), (0, 0)))
        values_pad = jnp.pad(values_all, ((pad_rows, pad_rows), (0, 0)))

        def one_block(block_num):
            row_start = block_num * group_rows
            q_block = lax.dynamic_slice_in_dim(queries, row_start, group_rows, 0).reshape(group_rows, HEADS, HEAD_DIM)
            k_window = lax.dynamic_slice_in_dim(keys_pad, row_start, window, 0).reshape(window, HEADS, HEAD_DIM)
            v_window = lax.dynamic_slice_in_dim(values_pad, row_start, window, 0).reshape(window, HEADS, HEAD_DIM)
            q_docs = lax.dynamic_slice_in_dim(doc_all, row_start + pad_rows, group_rows, 0)
            k_docs = lax.dynamic_slice_in_dim(doc_all, row_start, window, 0)
            allowed = (q_docs[:, None] == k_docs[None, :])[None]
            scores = low_back(score_scale * jnp.einsum('qhd,khd->hqk', q_block, k_window, precision=HIGHEST_PREC))
            scores = jnp.where(allowed, scores, MASKED_SCORE)
            row_top = lax.optimization_barrier(jnp.max(scores, axis=-1, keepdims=True))
            exp_terms = jnp.exp(scores - row_top)
            prob_rows = low(exp_terms / lax.optimization_barrier(jnp.sum(exp_terms, axis=-1, keepdims=True)))
            attended = jnp.einsum('hqk,khd->qhd', prob_rows, v_window, precision=HIGHEST_PREC).reshape(group_rows, D)
            attended = low(low_back(attended))
            branch = low_back(jnp.dot(attended, out_w, precision=HIGHEST_PREC)) + out_bias
            tok_block = lax.dynamic_slice_in_dim(tok_in, row_start, group_rows, 0)
            normed = layer_norm(tok_block + branch, gain_a, shift_a)
            hidden = low_back(jnp.dot(low(normed), in_w, precision=HIGHEST_PREC) + in_bias)
            active = low(jax.nn.gelu(hidden, approximate=False))
            branch_two = low_back(jnp.dot(active, down_w, precision=HIGHEST_PREC)) + down_bias
            return layer_norm(normed + branch_two, gain_b, shift_b)
        outputs = lax.map(jax.checkpoint(one_block), jnp.arange(block_count, dtype=jnp.int32))
        return outputs.reshape(TOKENS, D)
    floats = tuple((array_in.astype(jnp.float32) for array_in in (tokens, w_qkv, bias_q, bias_v, w_out, bias_out, gain_one, shift_one, w_in, bias_in, w_down, bias_down, gain_two, shift_two)))
    layer_value, pullback = jax.vjp(forward, *floats)
    gradients = pullback(cotangent.astype(jnp.float32))
    return (layer_value.astype(jnp.bfloat16), gradients[0], gradients[1], gradients[2], gradients[3], gradients[4], gradients[5], gradients[6], gradients[7], gradients[8], gradients[9], gradients[10], gradients[11], gradients[12], gradients[13])
```

```python
import functools
import jax
import jax.numpy as jnp
from jax import lax
from jax.experimental import pallas as pl
from jax.experimental.pallas import tpu as pltpu

MESH = pl.DeviceIdType.MESH
EXTENT = {"x": 4, "y": 4, "z": 8}
ORDERS = (("x", "y", "z"), ("y", "z", "x"), ("z", "x", "y"))
HALVES = (((0, 384), (384, 384)), ((0, 256), (256, 128)))
WHOLE = ((0, 768), (0, 384))


def place():
    s = lax.axis_index("shard")
    q = lax.axis_index("seq")
    return {
        "c": lax.rem(s, 2),
        "y": lax.rem(s // 2, 4),
        "x": s // 32,
        "z": lax.rem(s // 8, 4) * 2 + q,
    }


def device_at(at):
    return {
        "shard": ((at["x"] * 4 + at["z"] // 2) * 4 + at["y"]) * 2 + at["c"],
        "seq": lax.rem(at["z"], 2),
    }


def moved(at, **steps):
    new = dict(at)
    for dim, step in steps.items():
        size = 2 if dim == "c" else EXTENT[dim]
        new[dim] = lax.rem(at[dim] + step + size, size)
    return new


def greet(partners):
    barrier = pltpu.get_barrier_semaphore()
    for partner in partners:
        pl.semaphore_signal(barrier, inc=1, device_id=device_at(partner), device_id_type=MESH)
    pl.semaphore_wait(barrier, len(partners))


def remote(src, dst, send, recv, to):
    return pltpu.make_async_remote_copy(
        src_ref=src, dst_ref=dst, send_sem=send, recv_sem=recv,
        device_id=device_at(to), device_id_type=MESH,
    )


def neighbours(at):
    return [moved(at, **{d: step}) for d in ("x", "y", "z") for step in (1, -1)]


def octet_mates(me):
    across = dict(me)
    across["y"] = me["y"] + 1 - 2 * lax.rem(me["y"], 2)
    twin = moved(me, c=1)
    diagonal = dict(across)
    diagonal["c"] = twin["c"]
    return twin, across, diagonal


def ring_events(orders):
    events = []
    for part, order in enumerate(orders):
        clock, size, slot = 0.0, 1, part * 8
        for phase, dim in enumerate(order):
            half = EXTENT[dim] // 2
            for step in range(1, half + 1):
                clock += size * (0.5 if step == half else 1.0)
                events.append((clock, part, phase, dim, step, slot))
                slot += 1
            size *= EXTENT[dim]
    return sorted(events)


def span(index):
    return slice(None) if index is None else pl.ds(index, 1)


def views(wide, tall, core, part, sets, half=None):
    x, y, z = sets["x"], sets["y"], sets["z"]
    m, yp = (None, None) if y is None else (y // 2, lax.rem(y, 2))
    zh, q = (None, None) if z is None else (z // 2, lax.rem(z, 2))
    cuts = WHOLE if half is None else (HALVES[0][half], HALVES[1][half])
    return (
        wide.at[core, span(yp), span(q), span(x), span(zh), span(m), part, :, pl.ds(*cuts[0])],
        tall.at[core, span(x), span(zh), span(m), span(yp), span(q), part, :, pl.ds(*cuts[1])],
    )


def gather_kernel(
    cat_ref, down_ref, vec_ref, wide, tall, vecs,
    land, stage, own, odown, oct_s, oct_r, local, send, recv, core_s, core_r, vec_s, vec_r,
):
    me = place()
    c, x, y, z = me["c"], me["x"], me["y"], me["z"]
    yp, q, m, zh = lax.rem(y, 2), lax.rem(z, 2), y // 2, z // 2
    twin, across, diagonal = octet_mates(me)
    vec_rounds = (
        ("x", (1, 2, 3)), ("y", (1, 2, 3)), ("z", (2, 4, 6)), ("c", (1,)),
    )
    far = [moved(me, x=2), moved(me, y=2), moved(me, z=2), moved(me, z=4), moved(me, z=6)]
    greet(neighbours(me) + [twin, diagonal] + far)

    def chunk_of(at):
        cols = (at["c"] * 4 + lax.rem(at["y"], 2) * 2 + q) * 768
        return cat_ref.at[:, pl.ds(pl.multiple_of(cols, 128), 768)]

    index = yp * 2 + c
    out = [remote(chunk_of(mate), land.at[index], oct_s.at[k], oct_r.at[k], mate)
           for k, mate in enumerate((twin, across, diagonal))]
    for cp in out:
        cp.start()
    kept = pltpu.make_async_copy(chunk_of(me), land.at[index], local.at[0])
    kept.start()
    gives = q == c
    down_out = remote(down_ref.at[:, :, pl.ds(pl.multiple_of((1 - c) * 384, 128), 384)], odown,
                      oct_s.at[3], oct_r.at[3], twin)
    down_kept = pltpu.make_async_copy(
        down_ref.at[:, :, pl.ds(pl.multiple_of(c * 384, 128), 384)], odown, local.at[1])

    @pl.when(gives)
    def _():
        down_out.start()
        down_kept.start()

    vec_kept = pltpu.make_async_copy(vec_ref, vecs.at[c, x, zh, y], local.at[2])
    vec_kept.start()
    vec_kept.wait()

    def vec_copies(round_at, arriving):
        dim, steps = vec_rounds[round_at]
        done = [d for d, _ in vec_rounds[:round_at]]
        at = {"x": x, "y": y, "z": z, "c": c}
        copies = []
        for k, step in enumerate(steps):
            source = dict(at)
            if arriving:
                source = moved(at, **{dim: -step if dim != "c" else 1})
            pick = [None if d in done else (source["z"] // 2 if d == "z" else source[d]) for d in ("c", "x", "z", "y")]
            ref = vecs.at[tuple(span(p) for p in pick)]
            copies.append(remote(ref, ref, vec_s.at[round_at, k], vec_r.at[round_at, k], moved(at, **{dim: step})))
        return copies

    vec_sent = []

    def vec_start(round_at):
        for cp in vec_copies(round_at, False):
            cp.start()
            vec_sent.append(cp)

    def vec_wait(round_at):
        for cp in vec_copies(round_at, True):
            cp.wait_recv()

    vec_start(0)

    kept.wait()
    for k, mate in enumerate((twin, across, diagonal)):
        mate_index = lax.rem(mate["y"], 2) * 2 + mate["c"]
        remote(chunk_of(me), land.at[mate_index], oct_s.at[k], oct_r.at[k], mate).wait_recv()
    for owner in range(4):
        stage[pl.ds(6 * owner, 6), :] = land[owner].astype(jnp.float32)
    for part in range(3):
        own[part] = stage[pl.ds(8 * part, 8), :].astype(jnp.bfloat16)
    flush = [pltpu.make_async_copy(own, wide.at[c, yp, q, x, zh, m], local.at[3])]
    flush[0].start()

    @pl.when(gives)
    def _():
        down_kept.wait()

    @pl.when(jnp.logical_not(gives))
    def _():
        down_out.wait_recv()

    flush.append(pltpu.make_async_copy(odown, tall.at[c, x, zh, m, yp, q], local.at[4]))
    flush[1].start()
    for cp in flush:
        cp.wait()

    sent, twins = [], []

    def share(part, sets, half, slot):
        mine = views(wide, tall, c, part, sets, half)
        theirs = views(wide, tall, 1 - c, part, sets, half)
        for k in range(2):
            cp = remote(mine[k], mine[k], core_s.at[slot, k], core_r.at[slot, k], twin)
            cp.start()
            sent.append(cp)
            twins.append(remote(theirs[k], theirs[k], core_s.at[slot, k], core_r.at[slot, k], twin))

    def ring_copies(part, phase, dim, step, slot, direction, arriving):
        sign = 1 if direction == 0 else -1
        size = EXTENT[dim]
        behind = step if arriving else step - 1
        sets = {"x": x, "y": y, "z": z}
        for earlier in ORDERS[part][:phase]:
            sets[earlier] = None
        sets[dim] = lax.rem(me[dim] - sign * behind + size, size)
        half = direction if step == size // 2 else None
        both = views(wide, tall, c, part, sets, half)
        return [
            remote(both[k], both[k], send.at[slot, direction, k], recv.at[slot, direction, k], moved(me, **{dim: sign}))
            for k in range(2)
        ], sets, half

    def ring_start(part, phase, dim, step, slot):
        for direction in (0, 1):
            copies, _, _ = ring_copies(part, phase, dim, step, slot, direction, False)
            for cp in copies:
                cp.start()
                sent.append(cp)

    follow = {}
    for part, order in enumerate(ORDERS):
        steps = [(part, phase, dim, step) for phase, dim in enumerate(order) for step in range(1, EXTENT[dim] // 2 + 1)]
        steps = [(*s, part * 8 + i) for i, s in enumerate(steps)]
        ring_start(*steps[0])
        share(part, {"x": x, "y": y, "z": z}, None, 48 + part)
        for one, two in zip(steps, steps[1:]):
            follow[one] = two
    for number, (_, part, phase, dim, step, slot) in enumerate(ring_events(ORDERS)):
        arrived = []
        for direction in (0, 1):
            copies, sets, half = ring_copies(part, phase, dim, step, slot, direction, True)
            for cp in copies:
                cp.wait_recv()
            arrived.append((sets, half))
        after = follow.get((part, phase, dim, step, slot))
        if after is not None:
            ring_start(*after)
        for direction, (sets, half) in enumerate(arrived):
            share(part, sets, half, slot * 2 + direction)
        if number in (2, 5, 8):
            vec_wait((number - 2) // 3)
            vec_start((number - 2) // 3 + 1)
    vec_wait(3)
    for cp in twins:
        cp.wait_recv()
    for cp in out + vec_sent + sent:
        cp.wait_send()

    @pl.when(gives)
    def _():
        down_out.wait_send()


def gather_weights(cat, down, vec):
    any_space = pl.BlockSpec(memory_space=pl.ANY)
    wide, tall, vecs = pl.pallas_call(
        gather_kernel,
        name="gather_weights",
        out_shape=(
            jax.ShapeDtypeStruct((2, 2, 2, 4, 4, 2, 3, 8, 768), jnp.bfloat16),
            jax.ShapeDtypeStruct((2, 4, 4, 2, 2, 2, 3, 8, 384), jnp.bfloat16),
            jax.ShapeDtypeStruct((2, 4, 4, 4, 8, 128), jnp.float32),
        ),
        in_specs=[any_space] * 3,
        out_specs=(any_space,) * 3,
        scratch_shapes=[
            pltpu.VMEM((4, 6, 768), jnp.bfloat16),
            pltpu.VMEM((24, 768), jnp.float32),
            pltpu.VMEM((3, 8, 768), jnp.bfloat16),
            pltpu.VMEM((3, 8, 384), jnp.bfloat16),
            pltpu.SemaphoreType.DMA((4,)),
            pltpu.SemaphoreType.DMA((4,)),
            pltpu.SemaphoreType.DMA((5,)),
            pltpu.SemaphoreType.DMA((24, 2, 2)),
            pltpu.SemaphoreType.DMA((24, 2, 2)),
            pltpu.SemaphoreType.DMA((51, 2)),
            pltpu.SemaphoreType.DMA((51, 2)),
            pltpu.SemaphoreType.DMA((4, 3)),
            pltpu.SemaphoreType.DMA((4, 3)),
        ],
        compiler_params=pltpu.CompilerParams(collective_id=1, has_side_effects=True),
    )(cat, down, vec)
    return wide, tall, vecs


def flat_region(count, fn):
    if count == 1:
        fn(0)
    else:
        lax.fori_loop(0, count, lambda i, _: (fn(i), 0)[1], 0)


def reduce_kernel(
    gw, gt, gv, out_w, out_t, out_v,
    acc_w, acc_t, twin_w, twin_t,
    l0w, l0t, l1w, l1t, l2w, l2t, stage, rows, tall_f,
    v_c, v_x, v_y, v_z,
    local, core_s, core_r, send, recv, fin_s, fin_r, t_s, t_r, vec_s, vec_r,
):
    me = place()
    c, x, y, z = me["c"], me["x"], me["y"], me["z"]
    yp, q, m, zh = lax.rem(y, 2), lax.rem(z, 2), y // 2, z // 2
    twin, across, diagonal = octet_mates(me)

    def other_q(at):
        new = dict(at)
        new["z"] = at["z"] + 1 - 2 * lax.rem(at["z"], 2)
        return new

    ring_mates = [moved(me, **{d: k}) for d in ("x", "y", "z") for k in range(1, EXTENT[d])]
    mates = [twin, across, diagonal] + [other_q(a) for a in (me, twin, across, diagonal)]
    greet(ring_mates + [twin, diagonal] + [other_q(a) for a in (twin, across, diagonal)])

    lands_w = {(p, f, d): (l0w, l1w, l2w)[p][f][d] for p in range(3) for f in range(3) for d in range(2)}
    lands_t = {(p, f, d): (l0t, l1t, l2t)[p][f][d] for p in range(3) for f in range(3) for d in range(2)}

    def sets_of(part, phase, index):
        sets = {"x": x, "y": y, "z": z}
        order = ORDERS[part]
        for later in order[phase + 1:]:
            sets[later] = None
        sets[order[phase]] = index
        return sets

    def parts_of(sets, gone=()):
        a, b, d = sets["x"], sets["y"], sets["z"]
        pick = {
            "x": a, "m": None if b is None else b // 2, "yp": None if b is None else lax.rem(b, 2),
            "zh": None if d is None else d // 2, "q": None if d is None else lax.rem(d, 2),
        }
        for dim in gone:
            for name in {"x": ("x",), "y": ("m", "yp"), "z": ("zh", "q")}[dim]:
                pick[name] = 0
        return pick

    SIZES = {"yp": 2, "q": 2, "x": 4, "zh": 4, "m": 2}

    def acc_views(pair, part, sets, half=None, gone=()):
        pick = parts_of(sets, gone)
        cuts = WHOLE if half is None else (HALVES[0][half], HALVES[1][half])
        s = {k: span(v) for k, v in pick.items()}
        w, t = pair
        if part is None:
            return (w.at[s["yp"], s["q"], s["x"], s["zh"], s["m"], :, pl.ds(*cuts[0])],
                    t.at[s["x"], s["zh"], s["m"], s["yp"], s["q"], :, pl.ds(*cuts[1])])
        return (w.at[s["yp"], s["q"], s["x"], s["zh"], s["m"], part, :, pl.ds(*cuts[0])],
                t.at[s["x"], s["zh"], s["m"], s["yp"], s["q"], part, :, pl.ds(*cuts[1])])

    def add_region(part, sets, src, half=None, gone=()):
        pick, from_pick = parts_of(sets), parts_of(sets, gone)
        free = [k for k in ("yp", "q", "x", "zh", "m") if pick[k] is None]
        count = 1
        for k in free:
            count *= SIZES[k]
        cuts = WHOLE if half is None else (HALVES[0][half], HALVES[1][half])

        def one(i):
            at = {}
            for k in reversed(free):
                at[k] = lax.rem(i, SIZES[k]) if count > 1 else 0
                i = i // SIZES[k]
            to = {k: (at[k] if v is None else v) for k, v in pick.items()}
            fr = {k: (at[k] if v is None else v) for k, v in from_pick.items()}
            cw, ct = (pl.ds(*cut) for cut in cuts)
            wi = (to["yp"], to["q"], to["x"], to["zh"], to["m"], part, slice(None), cw)
            ti = (to["x"], to["zh"], to["m"], to["yp"], to["q"], part, slice(None), ct)
            wf = (fr["yp"], fr["q"], fr["x"], fr["zh"], fr["m"], slice(None), cw)
            tf = (fr["x"], fr["zh"], fr["m"], fr["yp"], fr["q"], slice(None), ct)
            acc_w[wi] = (acc_w[wi].astype(jnp.float32) + src[0][wf].astype(jnp.float32)).astype(jnp.bfloat16)
            acc_t[ti] = (acc_t[ti].astype(jnp.float32) + src[1][tf].astype(jnp.float32)).astype(jnp.bfloat16)

        flat_region(count, one)

    def hop(part, k):
        dim = ORDERS[part][0]
        half = EXTENT[dim] // 2
        offset = [half]
        for step in range(2, half + 1):
            offset += [half - step + 1, -(half - step + 1)]
        offset.append(0)
        return lax.rem(me[dim] + offset[k] + EXTENT[dim], EXTENT[dim])

    first = {}
    tops = [EXTENT[ORDERS[p][0]] for p in range(3)]
    starts = (0, tops[0], tops[0] + tops[1])
    sent = []
    for k in range(max(tops)):
        for part in range(3):
            if k >= tops[part]:
                continue
            slot = starts[part] + k
            sets = sets_of(part, 0, hop(part, k))
            src = acc_views((gw.at[1 - c], gt.at[1 - c]), part, sets)
            dst = acc_views((twin_w, twin_t), part, sets)
            mine = acc_views((gw.at[c], gt.at[c]), part, sets)
            keep = acc_views((acc_w, acc_t), part, sets)
            for j in range(2):
                cp = remote(src[j], dst[j], core_s.at[slot, j], core_r.at[slot, j], twin)
                cp.start()
                sent.append(cp)
                own = pltpu.make_async_copy(mine[j], keep[j], local.at[slot, j])
                own.start()
                first[part, k, j] = (cp, own)

    vec_lands = (v_c, v_x, v_y, v_z)
    vec_dims = ("c", "x", "y", "z")
    vec_sent = []

    def vec_start(number):
        dim, land = vec_dims[number], vec_lands[number]
        size = 2 if dim == "c" else EXTENT[dim]
        for k in range(1, size):
            cp = remote(land.at[me[dim]], land.at[me[dim]], vec_s.at[number, k], vec_r.at[number, k], moved(me, **{dim: k}))
            cp.start()
            vec_sent.append(cp)

    def vec_finish(number):
        dim, land = vec_dims[number], vec_lands[number]
        size = 2 if dim == "c" else EXTENT[dim]
        for k in range(1, size):
            src = lax.rem(me[dim] - k + size, size)
            remote(land.at[src], land.at[src], vec_s.at[number, k], vec_r.at[number, k], moved(me, **{dim: k})).wait_recv()
        total = land[0]
        for k in range(1, size):
            total = total + land[k]
        return total

    v_c[c] = gv[...]
    vec_start(0)

    def meet_twin(part, k):
        for j in range(2):
            cp, own = first[part, k, j]
            own.wait()
            cp.wait_recv()
        pick = sets_of(part, 0, hop(part, k))
        add_region(part, pick, (twin_w.at[:, :, :, :, :, part], twin_t.at[:, :, :, :, :, part]))

    def step_copies(part, phase, dim, step, slot, direction):
        sign = 1 if direction == 0 else -1
        size = EXTENT[dim]
        half = direction if step == 1 else None
        ahead = size // 2 - step + 1
        gone = ORDERS[part][:phase]

        def region(index):
            return sets_of(part, phase, lax.rem(index + 2 * size, size))

        going = region(me[dim] + sign * ahead)
        landing = (lands_w[part, phase, direction], lands_t[part, phase, direction])
        src = acc_views((acc_w, acc_t), part, going, half)
        dst = acc_views(landing, None, going, half, gone)
        to = moved(me, **{dim: sign})
        out = [remote(src[j], dst[j], send.at[slot, direction, j], recv.at[slot, direction, j], to) for j in range(2)]
        coming = region(me[dim] + sign * (ahead - 1))
        here = acc_views(landing, None, coming, half, gone)
        into = [remote(here[j], here[j], send.at[slot, direction, j], recv.at[slot, direction, j], to) for j in range(2)]
        return out, into, coming, landing, half, gone

    def ring_start(part, phase, dim, step, slot):
        for direction in (0, 1):
            for cp in step_copies(part, phase, dim, step, slot, direction)[0]:
                cp.start()
                sent.append(cp)

    def ring_finish(part, phase, dim, step, slot):
        for direction in (0, 1):
            _, into, coming, landing, half, gone = step_copies(part, phase, dim, step, slot, direction)
            for cp in into:
                cp.wait_recv()
            add_region(part, coming, landing, half, gone)

    plan, follow, events = {}, {}, []
    for part, order in enumerate(ORDERS):
        steps, size = [], 128
        clock = 0.0
        for phase, dim in enumerate(order):
            size //= EXTENT[dim]
            for step in range(1, EXTENT[dim] // 2 + 1):
                clock += size * (0.5 if step == 1 else 1.0)
                item = (part, phase, dim, step, part * 8 + len(steps))
                events.append((clock, item))
                steps.append(item)
        plan[part] = steps
        for one, two in zip(steps, steps[1:]):
            follow[one] = two
    events.sort()
    for part in range(3):
        meet_twin(part, 0)
        ring_start(*plan[part][0])
    met = [1, 1, 1]
    for part in range(3):
        for _ in range(2):
            meet_twin(part, met[part])
            met[part] += 1
    for number, (_, item) in enumerate(events):
        part, phase, dim, step, slot = item
        if phase == 0:
            while met[part] < min(2 * step + 1, tops[part]):
                meet_twin(part, met[part])
                met[part] += 1
            if step == EXTENT[dim] // 2:
                while met[part] < tops[part]:
                    meet_twin(part, met[part])
                    met[part] += 1
        ring_finish(*item)
        after = follow.get(item)
        if after is not None:
            ring_start(*after)
        if number in (3, 7, 11, 15):
            n = (number - 3) // 4
            total = vec_finish(n)
            if n < 3:
                vec_lands[n + 1][me[vec_dims[n + 1]]] = total
                vec_start(n + 1)
            else:
                out_v[...] = total

    for part in range(3):
        stage[pl.ds(8 * part, 8), :] = acc_w[yp, q, x, zh, m, part].astype(jnp.float32)
        tall_f[part] = acc_t[x, zh, m, yp, q, part].astype(jnp.float32)
    for owner in range(4):
        rows[owner] = stage[pl.ds(6 * owner, 6), :]
    cols = pl.ds(pl.multiple_of((c * 4 + yp * 2 + q) * 768, 128), 768)
    mine_at = yp * 2 + c
    ends = []
    for k, mate in enumerate(mates):
        o = lax.rem(mate["y"], 2) * 2 + mate["c"]
        cp = remote(rows.at[o], out_w.at[:, cols], fin_s.at[k], fin_r.at[k], mate)
        cp.start()
        ends.append(cp)
    kept = pltpu.make_async_copy(rows.at[mine_at], out_w.at[:, cols], fin_s.at[7])
    kept.start()
    half_cols = pl.ds(pl.multiple_of(c * 384, 128), 384)
    stays = c == q
    t_self = pltpu.make_async_copy(tall_f, out_t.at[:, :, half_cols], t_s.at[0])
    owner_here, owner_there = dict(me), other_q(me)
    t_twin = remote(tall_f, out_t.at[:, :, half_cols], t_s.at[0], t_r.at[0], twin)
    owner_there["c"] = q
    there_same = other_q(me)
    there_cross = other_q(twin)
    t_same = remote(tall_f, out_t.at[:, :, half_cols], t_s.at[1], t_r.at[1], there_same)
    t_cross = remote(tall_f, out_t.at[:, :, half_cols], t_s.at[1], t_r.at[2], there_cross)

    @pl.when(stays)
    def _():
        t_self.start()
        t_same.start()

    @pl.when(jnp.logical_not(stays))
    def _():
        t_twin.start()
        t_cross.start()

    for k, mate in enumerate(mates):
        from_cols = pl.ds(pl.multiple_of((mate["c"] * 4 + lax.rem(mate["y"], 2) * 2 + lax.rem(mate["z"], 2)) * 768, 128), 768)
        remote(rows.at[0], out_w.at[:, from_cols], fin_s.at[k], fin_r.at[k], mate).wait_recv()

    @pl.when(stays)
    def _():
        remote(tall_f, out_t.at[:, :, pl.ds(pl.multiple_of((1 - c) * 384, 128), 384)], t_s.at[0], t_r.at[0], twin).wait_recv()
        t_self.wait()
        t_same.wait_send()

    @pl.when(jnp.logical_not(stays))
    def _():
        remote(tall_f, out_t.at[:, :, half_cols], t_s.at[1], t_r.at[1], there_same).wait_recv()
        remote(tall_f, out_t.at[:, :, pl.ds(pl.multiple_of((1 - c) * 384, 128), 384)], t_s.at[1], t_r.at[2], there_cross).wait_recv()
        t_twin.wait_send()
        t_cross.wait_send()

    kept.wait()
    for cp in ends + vec_sent + sent:
        cp.wait_send()


def reduce_grads(gw, gt, gv):
    any_space = pl.BlockSpec(memory_space=pl.ANY)
    vmem = pl.BlockSpec(memory_space=pltpu.VMEM)

    def lands(part):
        order = ORDERS[part]
        wides, talls = [], []
        for phase in range(3):
            gone = order[:phase]
            sx = 1 if "x" in gone else 4
            sm, syp = (1, 1) if "y" in gone else (2, 2)
            szh, sq = (1, 1) if "z" in gone else (4, 2)
            wides.append([pltpu.VMEM((syp, sq, sx, szh, sm, 8, 768), jnp.bfloat16)] * 2)
            talls.append([pltpu.VMEM((sx, szh, sm, syp, sq, 8, 384), jnp.bfloat16)] * 2)
        return [wides, talls]

    return pl.pallas_call(
        reduce_kernel,
        name="reduce_grads",
        out_shape=(
            jax.ShapeDtypeStruct((6, 6144), jnp.float32),
            jax.ShapeDtypeStruct((3, 8, 768), jnp.float32),
            jax.ShapeDtypeStruct((16, 768), jnp.float32),
        ),
        in_specs=[any_space, any_space, vmem],
        out_specs=(any_space, any_space, vmem),
        scratch_shapes=[
            pltpu.VMEM((2, 2, 4, 4, 2, 3, 8, 768), jnp.bfloat16),
            pltpu.VMEM((4, 4, 2, 2, 2, 3, 8, 384), jnp.bfloat16),
            pltpu.VMEM((2, 2, 4, 4, 2, 3, 8, 768), jnp.bfloat16),
            pltpu.VMEM((4, 4, 2, 2, 2, 3, 8, 384), jnp.bfloat16),
            *lands(0), *lands(1), *lands(2),
            pltpu.VMEM((24, 768), jnp.float32),
            pltpu.VMEM((4, 6, 768), jnp.float32),
            pltpu.VMEM((3, 8, 384), jnp.float32),
            pltpu.VMEM((2, 16, 768), jnp.float32),
            pltpu.VMEM((4, 16, 768), jnp.float32),
            pltpu.VMEM((4, 16, 768), jnp.float32),
            pltpu.VMEM((8, 16, 768), jnp.float32),
            pltpu.SemaphoreType.DMA((16, 2)),
            pltpu.SemaphoreType.DMA((16, 2)),
            pltpu.SemaphoreType.DMA((16, 2)),
            pltpu.SemaphoreType.DMA((24, 2, 2)),
            pltpu.SemaphoreType.DMA((24, 2, 2)),
            pltpu.SemaphoreType.DMA((8,)),
            pltpu.SemaphoreType.DMA((7,)),
            pltpu.SemaphoreType.DMA((2,)),
            pltpu.SemaphoreType.DMA((3,)),
            pltpu.SemaphoreType.DMA((4, 8)),
            pltpu.SemaphoreType.DMA((4, 8)),
        ],
        compiler_params=pltpu.CompilerParams(
            collective_id=2, has_side_effects=True, vmem_limit_bytes=58 << 20
        ),
    )(gw, gt, gv)


from jax.sharding import PartitionSpec as P

HEAD_DIM = 64
DOC_MAX = 1024
MASKED_SCORE = -1e30
NORM_EPS = 1e-12


def passed_along(block, axis, distance):
    devices = range(lax.axis_size(axis))
    route = [(i - distance, i) for i in devices if i - distance in devices]
    return lax.ppermute(block, axis, route)


def layer_norm(resid, gain_vec, shift_vec):
    row_mean = jnp.mean(resid, axis=-1, keepdims=True)
    centred = resid - row_mean
    variance = jnp.mean(centred * centred, axis=-1, keepdims=True)
    return centred * lax.rsqrt(variance + NORM_EPS) * gain_vec + shift_vec


def doc_index(doc_lengths, positions, stream_len):
    doc_ends = jnp.cumsum(doc_lengths, dtype=jnp.int32)
    starts = doc_ends - doc_lengths
    counted = jnp.sum((positions[:, None] >= starts[None, :]).astype(jnp.int32), axis=1, dtype=jnp.int32) - 1
    inside = (positions >= 0) & (positions < stream_len)
    return jnp.where(inside, counted, -1)


def head_scores(q_head, k_window, allowed, score_scale):
    scores = jnp.einsum("qd,kd->qk", q_head, k_window, preferred_element_type=jnp.float32) * score_scale
    return jnp.where(allowed, scores, MASKED_SCORE)


def dot32(spec, a, b):
    return jnp.einsum(spec, a, b, preferred_element_type=jnp.float32)


def body(
    tokens, w_qkv, bias_q, bias_v, w_out, bias_out, gain_one, shift_one, w_in, bias_in,
    w_down, bias_down, gain_two, shift_two, doc_lengths, cotangent,
):
    seq_count = lax.axis_size("seq")
    shard_count = lax.axis_size("shard")
    shard_place = lax.axis_index("shard")
    tok_rows, model_width = tokens.shape
    half_width = model_width // seq_count
    heads_local = half_width // HEAD_DIM
    group_rows = tok_rows * seq_count
    reach_groups = 1 + (DOC_MAX - 2) // group_rows
    window = (2 * reach_groups + 1) * group_rows
    stream_len = group_rows * shard_count
    score_scale = HEAD_DIM ** (-0.5)
    query_pos = shard_place * group_rows + jnp.arange(group_rows, dtype=jnp.int32)
    key_pos = (shard_place - reach_groups) * group_rows + jnp.arange(window, dtype=jnp.int32)
    query_docs = doc_index(doc_lengths, query_pos, stream_len)
    key_docs = doc_index(doc_lengths, key_pos, stream_len)
    allowed = query_docs[:, None] == key_docs[None, :]

    vectors = (bias_q, bias_v, bias_out, gain_one, shift_one, bias_down, gain_two, shift_two)
    vec = jnp.concatenate(
        [
            jnp.stack(vectors).astype(jnp.float32),
            jnp.pad(bias_in.astype(jnp.float32).reshape(1, 24), ((0, 7), (0, 0))),
            jnp.zeros((8, 98), jnp.float32),
        ],
        axis=1,
    )
    cat = jnp.concatenate([w_qkv, w_out, w_in], axis=1)
    wide, tall, vecs = gather_weights(cat, w_down.reshape(3, 8, model_width), vec)
    wide = wide.reshape(8, model_width, model_width)
    tall = tall.reshape(2, 4 * model_width, model_width // 2)
    vecs = jnp.transpose(vecs, (4, 1, 2, 3, 0, 5)).reshape(8, 128, 128)
    rows = vecs[:, :, :6].reshape(8, 1, model_width)
    bias_q_all, bias_v_all, bias_out_all, gain_one_all, shift_one_all, bias_down_all, gain_two_all, shift_two_all = rows
    bias_in_all = vecs[0, :, 6:30].reshape(4, 1, model_width)

    qkv = dot32("td,cdn->ctn", tokens, wide[:3])
    queries = (qkv[0] + bias_q_all).astype(jnp.bfloat16)
    keys_all = qkv[1].astype(jnp.bfloat16)
    values_all = (qkv[2] + bias_v_all).astype(jnp.bfloat16)
    q_heads, k_heads, v_heads = (
        lax.all_to_all(a, "seq", split_axis=1, concat_axis=0, tiled=True) for a in (queries, keys_all, values_all)
    )
    k_parts, v_parts = [], []
    for offset in range(-reach_groups, reach_groups + 1):
        if offset == 0:
            k_piece, v_piece = k_heads, v_heads
        else:
            k_piece, v_piece = passed_along((k_heads, v_heads), "shard", -offset)
        k_parts.append(k_piece)
        v_parts.append(v_piece)
    k_window = jnp.concatenate(k_parts, axis=0)
    v_window = jnp.concatenate(v_parts, axis=0)
    head_parts, top_parts, total_parts = [], [], []
    for head_num in range(heads_local):
        cols = slice(head_num * HEAD_DIM, (head_num + 1) * HEAD_DIM)
        scores = head_scores(q_heads[:, cols], k_window[:, cols], allowed, score_scale)
        row_top = jnp.max(scores, axis=1, keepdims=True)
        exp_terms = jnp.exp(scores - row_top)
        row_total = jnp.sum(exp_terms, axis=1, keepdims=True)
        prob_low = (exp_terms / row_total).astype(jnp.bfloat16)
        head_parts.append(jnp.dot(prob_low, v_window[:, cols], preferred_element_type=jnp.float32))
        top_parts.append(row_top)
        total_parts.append(row_total)
    attended = jnp.concatenate(head_parts, axis=1).astype(jnp.bfloat16)
    back_tokens = lax.all_to_all(attended, "seq", split_axis=0, concat_axis=1, tiled=True)
    branch = jnp.dot(back_tokens, wide[3], preferred_element_type=jnp.float32) + bias_out_all
    resid_one = tokens.astype(jnp.float32) + branch
    normed, norm_one_pull = jax.vjp(layer_norm, resid_one, gain_one_all, shift_one_all)
    normed_low = normed.astype(jnp.bfloat16)
    hidden = dot32("td,cdn->ctn", normed_low, wide[4:]) + bias_in_all
    active, gelu_pull = jax.vjp(lambda h: jax.nn.gelu(h, approximate=False), hidden)
    active_low = active.astype(jnp.bfloat16)
    tall4 = tall.reshape(2, 4, model_width, model_width // 2)
    branch_two = jnp.concatenate([dot32("ctf,cfn->tn", active_low, tall4[j]) for j in range(2)], axis=1) + bias_down_all
    resid_two = normed + branch_two
    layer_value, norm_two_pull = jax.vjp(layer_norm, resid_two, gain_two_all, shift_two_all)
    layer_out = layer_value.astype(jnp.bfloat16)

    d_resid_two, d_gain_two, d_shift_two = norm_two_pull(cotangent.astype(jnp.float32))
    d_branch_two = d_resid_two.astype(jnp.bfloat16)
    d_bias_down = jnp.sum(d_resid_two, axis=0, keepdims=True)
    grads_down = [
        dot32("ctf,tn->cfn", active_low, d_branch_two[:, j * half_width : (j + 1) * half_width]).astype(jnp.bfloat16)
        for j in range(2)
    ]
    d_active = sum(
        dot32("tn,cfn->ctf", d_branch_two[:, j * half_width : (j + 1) * half_width], tall4[j]) for j in range(2)
    )
    d_hidden = gelu_pull(d_active)[0].astype(jnp.bfloat16)
    d_bias_in = jnp.sum(d_hidden.astype(jnp.float32), axis=1)
    grad_in = dot32("td,ctn->cdn", normed_low, d_hidden).astype(jnp.bfloat16)
    d_normed = d_resid_two + dot32("ctn,cdn->td", d_hidden, wide[4:])
    d_resid_one, d_gain_one, d_shift_one = norm_one_pull(d_normed)
    d_branch = d_resid_one.astype(jnp.bfloat16)
    d_bias_out = jnp.sum(d_resid_one, axis=0, keepdims=True)
    grad_out = dot32("tc,td->cd", back_tokens, d_branch).astype(jnp.bfloat16)
    d_attended = dot32("td,cd->tc", d_branch, wide[3]).astype(jnp.bfloat16)
    d_heads = lax.all_to_all(d_attended, "seq", split_axis=1, concat_axis=0, tiled=True)
    dq_parts, dk_parts, dv_parts = [], [], []
    for head_num in range(heads_local):
        cols = slice(head_num * HEAD_DIM, (head_num + 1) * HEAD_DIM)
        q_head, k_head, v_head, d_out_head = q_heads[:, cols], k_window[:, cols], v_window[:, cols], d_heads[:, cols]
        scores = head_scores(q_head, k_head, allowed, score_scale)
        prob_rows = jnp.exp(scores - top_parts[head_num]) / total_parts[head_num]
        prob_low = prob_rows.astype(jnp.bfloat16)
        d_probs = dot32("qd,kd->qk", d_out_head, v_head)
        row_delta = jnp.sum(prob_rows * d_probs, axis=1, keepdims=True)
        d_scores = (prob_rows * (d_probs - row_delta)).astype(jnp.bfloat16)
        dq_parts.append(jnp.dot(d_scores, k_head, preferred_element_type=jnp.float32) * score_scale)
        dk_parts.append(dot32("qk,qd->kd", d_scores, q_head) * score_scale)
        dv_parts.append(dot32("qk,qd->kd", prob_low, d_out_head))
    d_query_heads = jnp.concatenate(dq_parts, axis=1).astype(jnp.bfloat16)
    dk_window = jnp.concatenate(dk_parts, axis=1)
    dv_window = jnp.concatenate(dv_parts, axis=1)
    own_start = reach_groups * group_rows
    dk_total = dk_window[own_start : own_start + group_rows]
    dv_total = dv_window[own_start : own_start + group_rows]
    for offset in range(-reach_groups, reach_groups + 1):
        if offset != 0:
            row_start = (offset + reach_groups) * group_rows
            k_return, v_return = (
                passed_along(a[row_start : row_start + group_rows].astype(jnp.bfloat16), "shard", offset).astype(jnp.float32)
                for a in (dk_window, dv_window)
            )
            dk_total = dk_total + k_return
            dv_total = dv_total + v_return
    d_qkv = jnp.stack([
        lax.all_to_all(a.astype(jnp.bfloat16), "seq", split_axis=0, concat_axis=1, tiled=True)
        for a in (d_query_heads, dk_total, dv_total)
    ])
    d_bias_q = jnp.sum(d_qkv[0].astype(jnp.float32), axis=0, keepdims=True)
    d_bias_v = jnp.sum(d_qkv[2].astype(jnp.float32), axis=0, keepdims=True)
    grad_qkv = dot32("td,ctn->cdn", tokens, d_qkv).astype(jnp.bfloat16)
    grad_tokens = d_resid_one + dot32("ctn,cdn->td", d_qkv, wide[:3])

    gw = jnp.concatenate([grad_qkv, grad_out[None], grad_in], axis=0).reshape(2, 2, 2, 4, 4, 2, 3, 8, model_width)
    gt = jnp.stack(grads_down).reshape(2, 4, 4, 2, 2, 2, 3, 8, half_width)
    gv = jnp.concatenate(
        [d_bias_q, d_bias_v, d_bias_out, d_gain_one, d_shift_one, d_bias_down, d_gain_two, d_shift_two, d_bias_in,
         jnp.zeros((4, model_width), jnp.float32)], axis=0)
    sum_w, sum_t, sum_v = reduce_grads(gw, gt, gv)
    mine = lax.dynamic_slice(sum_v, (0, 6 * shard_place), (8, 6))
    in_mine = lax.dynamic_slice(sum_v[8:12].reshape(-1), (24 * shard_place,), (24,))
    return (
        layer_out, grad_tokens, sum_w[:, : 3 * model_width], mine[0], mine[1],
        sum_w[:, 3 * model_width : 4 * model_width], mine[2], mine[3], mine[4],
        sum_w[:, 4 * model_width :], in_mine, sum_t.reshape(24, model_width), mine[5], mine[6], mine[7],
    )


def solution(mesh):
    both, own = P(("shard", "seq"), None), P("shard")
    rows = P("shard", None)
    return jax.shard_map(
        body,
        mesh=mesh,
        in_specs=(both, rows, own, own, rows, own, own, own, rows, own, rows, own, own, own, P(), both),
        out_specs=(both, both, rows, own, own, rows, own, own, own, rows, own, rows, own, own, own),
        check_vma=False,
    )
```

```python
import functools
import jax
import jax.numpy as jnp
from jax import lax
from jax.experimental import pallas as pl
from jax.experimental.pallas import tpu as pltpu

HEAD_DIM = 64
MESH = pl.DeviceIdType.MESH
EXTENT = {"x": 4, "y": 4, "z": 8}
ORDERS = (("x", "y", "z"), ("y", "z", "x"), ("z", "x", "y"))
HALVES = (((0, 384), (384, 384)), ((0, 256), (256, 128)))
WHOLE = ((0, 768), (0, 384))


def place():
    s = lax.axis_index("shard")
    q = lax.axis_index("seq")
    return {
        "c": lax.rem(s, 2),
        "y": lax.rem(s // 2, 4),
        "x": s // 32,
        "z": lax.rem(s // 8, 4) * 2 + q,
    }


def device_at(at):
    return {
        "shard": ((at["x"] * 4 + at["z"] // 2) * 4 + at["y"]) * 2 + at["c"],
        "seq": lax.rem(at["z"], 2),
    }


def moved(at, **steps):
    new = dict(at)
    for dim, step in steps.items():
        size = 2 if dim == "c" else EXTENT[dim]
        new[dim] = lax.rem(at[dim] + step + size, size)
    return new


def greet(partners):
    barrier = pltpu.get_barrier_semaphore()
    for partner in partners:
        pl.semaphore_signal(barrier, inc=1, device_id=device_at(partner), device_id_type=MESH)
    pl.semaphore_wait(barrier, len(partners))


def remote(src, dst, send, recv, to):
    return pltpu.make_async_remote_copy(
        src_ref=src, dst_ref=dst, send_sem=send, recv_sem=recv,
        device_id=device_at(to), device_id_type=MESH,
    )


def neighbours(at):
    return [moved(at, **{d: step}) for d in ("x", "y", "z") for step in (1, -1)]


def octet_mates(me):
    across = dict(me)
    across["y"] = me["y"] + 1 - 2 * lax.rem(me["y"], 2)
    twin = moved(me, c=1)
    diagonal = dict(across)
    diagonal["c"] = twin["c"]
    return twin, across, diagonal


def ring_events(orders):
    events = []
    for part, order in enumerate(orders):
        clock, size, slot = 0.0, 1, part * 8
        for phase, dim in enumerate(order):
            half = EXTENT[dim] // 2
            for step in range(1, half + 1):
                clock += size * (0.5 if step == half else 1.0)
                events.append((clock, part, phase, dim, step, slot))
                slot += 1
            size *= EXTENT[dim]
    return sorted(events)


def span(index):
    return slice(None) if index is None else pl.ds(index, 1)


def views(wide, tall, core, part, sets, half=None):
    x, y, z = sets["x"], sets["y"], sets["z"]
    m, yp = (None, None) if y is None else (y // 2, lax.rem(y, 2))
    zh, q = (None, None) if z is None else (z // 2, lax.rem(z, 2))
    cuts = WHOLE if half is None else (HALVES[0][half], HALVES[1][half])
    return (
        wide.at[core, span(yp), span(q), span(x), span(zh), span(m), part, :, pl.ds(*cuts[0])],
        tall.at[core, span(x), span(zh), span(m), span(yp), span(q), part, :, pl.ds(*cuts[1])],
    )


def gather_kernel(
    cat_ref, down_ref, vec_ref, wide, tall, vecs,
    land, stage, own, odown, oct_s, oct_r, local, send, recv, core_s, core_r, vec_s, vec_r,
):
    me = place()
    c, x, y, z = me["c"], me["x"], me["y"], me["z"]
    yp, q, m, zh = lax.rem(y, 2), lax.rem(z, 2), y // 2, z // 2
    twin, across, diagonal = octet_mates(me)
    vec_rounds = (
        ("x", (1, 2, 3)), ("y", (1, 2, 3)), ("z", (2, 4, 6)), ("c", (1,)),
    )
    far = [moved(me, x=2), moved(me, y=2), moved(me, z=2), moved(me, z=4), moved(me, z=6)]
    greet(neighbours(me) + [twin, diagonal] + far)

    def chunk_of(at):
        cols = (at["c"] * 4 + lax.rem(at["y"], 2) * 2 + q) * 768
        return cat_ref.at[:, pl.ds(pl.multiple_of(cols, 128), 768)]

    index = yp * 2 + c
    out = [remote(chunk_of(mate), land.at[index], oct_s.at[k], oct_r.at[k], mate)
           for k, mate in enumerate((twin, across, diagonal))]
    for cp in out:
        cp.start()
    kept = pltpu.make_async_copy(chunk_of(me), land.at[index], local.at[0])
    kept.start()
    gives = q == c
    down_out = remote(down_ref.at[:, :, pl.ds(pl.multiple_of((1 - c) * 384, 128), 384)], odown,
                      oct_s.at[3], oct_r.at[3], twin)
    down_kept = pltpu.make_async_copy(
        down_ref.at[:, :, pl.ds(pl.multiple_of(c * 384, 128), 384)], odown, local.at[1])

    @pl.when(gives)
    def _():
        down_out.start()
        down_kept.start()

    vec_kept = pltpu.make_async_copy(vec_ref, vecs.at[c, x, zh, y], local.at[2])
    vec_kept.start()
    vec_kept.wait()

    def vec_copies(round_at, arriving):
        dim, steps = vec_rounds[round_at]
        done = [d for d, _ in vec_rounds[:round_at]]
        at = {"x": x, "y": y, "z": z, "c": c}
        copies = []
        for k, step in enumerate(steps):
            source = dict(at)
            if arriving:
                source = moved(at, **{dim: -step if dim != "c" else 1})
            pick = [None if d in done else (source["z"] // 2 if d == "z" else source[d]) for d in ("c", "x", "z", "y")]
            ref = vecs.at[tuple(span(p) for p in pick)]
            copies.append(remote(ref, ref, vec_s.at[round_at, k], vec_r.at[round_at, k], moved(at, **{dim: step})))
        return copies

    vec_sent = []

    def vec_start(round_at):
        for cp in vec_copies(round_at, False):
            cp.start()
            vec_sent.append(cp)

    def vec_wait(round_at):
        for cp in vec_copies(round_at, True):
            cp.wait_recv()

    vec_start(0)

    kept.wait()
    for k, mate in enumerate((twin, across, diagonal)):
        mate_index = lax.rem(mate["y"], 2) * 2 + mate["c"]
        remote(chunk_of(me), land.at[mate_index], oct_s.at[k], oct_r.at[k], mate).wait_recv()
    for owner in range(4):
        stage[pl.ds(6 * owner, 6), :] = land[owner].astype(jnp.float32)
    for part in range(3):
        own[part] = stage[pl.ds(8 * part, 8), :].astype(jnp.bfloat16)
    flush = [pltpu.make_async_copy(own, wide.at[c, yp, q, x, zh, m], local.at[3])]
    flush[0].start()

    @pl.when(gives)
    def _():
        down_kept.wait()

    @pl.when(jnp.logical_not(gives))
    def _():
        down_out.wait_recv()

    flush.append(pltpu.make_async_copy(odown, tall.at[c, x, zh, m, yp, q], local.at[4]))
    flush[1].start()
    for cp in flush:
        cp.wait()

    sent, twins = [], []

    def share(part, sets, half, slot):
        mine = views(wide, tall, c, part, sets, half)
        theirs = views(wide, tall, 1 - c, part, sets, half)
        for k in range(2):
            cp = remote(mine[k], mine[k], core_s.at[slot, k], core_r.at[slot, k], twin)
            cp.start()
            sent.append(cp)
            twins.append(remote(theirs[k], theirs[k], core_s.at[slot, k], core_r.at[slot, k], twin))

    def ring_copies(part, phase, dim, step, slot, direction, arriving):
        sign = 1 if direction == 0 else -1
        size = EXTENT[dim]
        behind = step if arriving else step - 1
        sets = {"x": x, "y": y, "z": z}
        for earlier in ORDERS[part][:phase]:
            sets[earlier] = None
        sets[dim] = lax.rem(me[dim] - sign * behind + size, size)
        half = direction if step == size // 2 else None
        both = views(wide, tall, c, part, sets, half)
        return [
            remote(both[k], both[k], send.at[slot, direction, k], recv.at[slot, direction, k], moved(me, **{dim: sign}))
            for k in range(2)
        ], sets, half

    def ring_start(part, phase, dim, step, slot):
        for direction in (0, 1):
            copies, _, _ = ring_copies(part, phase, dim, step, slot, direction, False)
            for cp in copies:
                cp.start()
                sent.append(cp)

    follow = {}
    for part, order in enumerate(ORDERS):
        steps = [(part, phase, dim, step) for phase, dim in enumerate(order) for step in range(1, EXTENT[dim] // 2 + 1)]
        steps = [(*s, part * 8 + i) for i, s in enumerate(steps)]
        ring_start(*steps[0])
        share(part, {"x": x, "y": y, "z": z}, None, 48 + part)
        for one, two in zip(steps, steps[1:]):
            follow[one] = two
    for number, (_, part, phase, dim, step, slot) in enumerate(ring_events(ORDERS)):
        arrived = []
        for direction in (0, 1):
            copies, sets, half = ring_copies(part, phase, dim, step, slot, direction, True)
            for cp in copies:
                cp.wait_recv()
            arrived.append((sets, half))
        after = follow.get((part, phase, dim, step, slot))
        if after is not None:
            ring_start(*after)
        for direction, (sets, half) in enumerate(arrived):
            share(part, sets, half, slot * 2 + direction)
        if number in (2, 5, 8):
            vec_wait((number - 2) // 3)
            vec_start((number - 2) // 3 + 1)
    vec_wait(3)
    for cp in twins:
        cp.wait_recv()
    for cp in out + vec_sent + sent:
        cp.wait_send()

    @pl.when(gives)
    def _():
        down_out.wait_send()


def gather_weights(cat, down, vec):
    any_space = pl.BlockSpec(memory_space=pl.ANY)
    wide, tall, vecs = pl.pallas_call(
        gather_kernel,
        name="gather_weights",
        out_shape=(
            jax.ShapeDtypeStruct((2, 2, 2, 4, 4, 2, 3, 8, 768), jnp.bfloat16),
            jax.ShapeDtypeStruct((2, 4, 4, 2, 2, 2, 3, 8, 384), jnp.bfloat16),
            jax.ShapeDtypeStruct((2, 4, 4, 4, 8, 128), jnp.float32),
        ),
        in_specs=[any_space] * 3,
        out_specs=(any_space,) * 3,
        scratch_shapes=[
            pltpu.VMEM((4, 6, 768), jnp.bfloat16),
            pltpu.VMEM((24, 768), jnp.float32),
            pltpu.VMEM((3, 8, 768), jnp.bfloat16),
            pltpu.VMEM((3, 8, 384), jnp.bfloat16),
            pltpu.SemaphoreType.DMA((4,)),
            pltpu.SemaphoreType.DMA((4,)),
            pltpu.SemaphoreType.DMA((5,)),
            pltpu.SemaphoreType.DMA((24, 2, 2)),
            pltpu.SemaphoreType.DMA((24, 2, 2)),
            pltpu.SemaphoreType.DMA((51, 2)),
            pltpu.SemaphoreType.DMA((51, 2)),
            pltpu.SemaphoreType.DMA((4, 3)),
            pltpu.SemaphoreType.DMA((4, 3)),
        ],
        compiler_params=pltpu.CompilerParams(collective_id=1, has_side_effects=True),
    )(cat, down, vec)
    return wide, tall, vecs


def flat_region(count, fn):
    if count == 1:
        fn(0)
    else:
        lax.fori_loop(0, count, lambda i, _: (fn(i), 0)[1], 0)


def reduce_kernel(
    gw, gt, gv, out_w, out_t, out_v,
    acc_w, acc_t, twin_w, twin_t,
    l0w, l0t, l1w, l1t, l2w, l2t, stage, rows, tall_f,
    v_c, v_x, v_y, v_z,
    local, core_s, core_r, send, recv, fin_s, fin_r, t_s, t_r, vec_s, vec_r,
):
    me = place()
    c, x, y, z = me["c"], me["x"], me["y"], me["z"]
    yp, q, m, zh = lax.rem(y, 2), lax.rem(z, 2), y // 2, z // 2
    twin, across, diagonal = octet_mates(me)

    def other_q(at):
        new = dict(at)
        new["z"] = at["z"] + 1 - 2 * lax.rem(at["z"], 2)
        return new

    ring_mates = [moved(me, **{d: k}) for d in ("x", "y", "z") for k in range(1, EXTENT[d])]
    mates = [twin, across, diagonal] + [other_q(a) for a in (me, twin, across, diagonal)]
    greet(ring_mates + [twin, diagonal] + [other_q(a) for a in (twin, across, diagonal)])

    lands_w = {(p, f, d): (l0w, l1w, l2w)[p][f][d] for p in range(3) for f in range(3) for d in range(2)}
    lands_t = {(p, f, d): (l0t, l1t, l2t)[p][f][d] for p in range(3) for f in range(3) for d in range(2)}

    def sets_of(part, phase, index):
        sets = {"x": x, "y": y, "z": z}
        order = ORDERS[part]
        for later in order[phase + 1:]:
            sets[later] = None
        sets[order[phase]] = index
        return sets

    def parts_of(sets, gone=()):
        a, b, d = sets["x"], sets["y"], sets["z"]
        pick = {
            "x": a, "m": None if b is None else b // 2, "yp": None if b is None else lax.rem(b, 2),
            "zh": None if d is None else d // 2, "q": None if d is None else lax.rem(d, 2),
        }
        for dim in gone:
            for name in {"x": ("x",), "y": ("m", "yp"), "z": ("zh", "q")}[dim]:
                pick[name] = 0
        return pick

    SIZES = {"yp": 2, "q": 2, "x": 4, "zh": 4, "m": 2}

    def acc_views(pair, part, sets, half=None, gone=()):
        pick = parts_of(sets, gone)
        cuts = WHOLE if half is None else (HALVES[0][half], HALVES[1][half])
        s = {k: span(v) for k, v in pick.items()}
        w, t = pair
        if part is None:
            return (w.at[s["yp"], s["q"], s["x"], s["zh"], s["m"], :, pl.ds(*cuts[0])],
                    t.at[s["x"], s["zh"], s["m"], s["yp"], s["q"], :, pl.ds(*cuts[1])])
        return (w.at[s["yp"], s["q"], s["x"], s["zh"], s["m"], part, :, pl.ds(*cuts[0])],
                t.at[s["x"], s["zh"], s["m"], s["yp"], s["q"], part, :, pl.ds(*cuts[1])])

    def add_region(part, sets, src, half=None, gone=()):
        pick, from_pick = parts_of(sets), parts_of(sets, gone)
        free = [k for k in ("yp", "q", "x", "zh", "m") if pick[k] is None]
        count = 1
        for k in free:
            count *= SIZES[k]
        cuts = WHOLE if half is None else (HALVES[0][half], HALVES[1][half])

        def one(i):
            at = {}
            for k in reversed(free):
                at[k] = lax.rem(i, SIZES[k]) if count > 1 else 0
                i = i // SIZES[k]
            to = {k: (at[k] if v is None else v) for k, v in pick.items()}
            fr = {k: (at[k] if v is None else v) for k, v in from_pick.items()}
            cw, ct = (pl.ds(*cut) for cut in cuts)
            wi = (to["yp"], to["q"], to["x"], to["zh"], to["m"], part, slice(None), cw)
            ti = (to["x"], to["zh"], to["m"], to["yp"], to["q"], part, slice(None), ct)
            wf = (fr["yp"], fr["q"], fr["x"], fr["zh"], fr["m"], slice(None), cw)
            tf = (fr["x"], fr["zh"], fr["m"], fr["yp"], fr["q"], slice(None), ct)
            acc_w[wi] = (acc_w[wi].astype(jnp.float32) + src[0][wf].astype(jnp.float32)).astype(jnp.bfloat16)
            acc_t[ti] = (acc_t[ti].astype(jnp.float32) + src[1][tf].astype(jnp.float32)).astype(jnp.bfloat16)

        flat_region(count, one)

    def hop(part, k):
        dim = ORDERS[part][0]
        half = EXTENT[dim] // 2
        offset = [half]
        for step in range(2, half + 1):
            offset += [half - step + 1, -(half - step + 1)]
        offset.append(0)
        return lax.rem(me[dim] + offset[k] + EXTENT[dim], EXTENT[dim])

    first = {}
    tops = [EXTENT[ORDERS[p][0]] for p in range(3)]
    starts = (0, tops[0], tops[0] + tops[1])
    sent = []
    for k in range(max(tops)):
        for part in range(3):
            if k >= tops[part]:
                continue
            slot = starts[part] + k
            sets = sets_of(part, 0, hop(part, k))
            src = acc_views((gw.at[1 - c], gt.at[1 - c]), part, sets)
            dst = acc_views((twin_w, twin_t), part, sets)
            mine = acc_views((gw.at[c], gt.at[c]), part, sets)
            keep = acc_views((acc_w, acc_t), part, sets)
            for j in range(2):
                cp = remote(src[j], dst[j], core_s.at[slot, j], core_r.at[slot, j], twin)
                cp.start()
                sent.append(cp)
                own = pltpu.make_async_copy(mine[j], keep[j], local.at[slot, j])
                own.start()
                first[part, k, j] = (cp, own)

    vec_lands = (v_c, v_x, v_y, v_z)
    vec_dims = ("c", "x", "y", "z")
    vec_sent = []

    def vec_start(number):
        dim, land = vec_dims[number], vec_lands[number]
        size = 2 if dim == "c" else EXTENT[dim]
        for k in range(1, size):
            cp = remote(land.at[me[dim]], land.at[me[dim]], vec_s.at[number, k], vec_r.at[number, k], moved(me, **{dim: k}))
            cp.start()
            vec_sent.append(cp)

    def vec_finish(number):
        dim, land = vec_dims[number], vec_lands[number]
        size = 2 if dim == "c" else EXTENT[dim]
        for k in range(1, size):
            src = lax.rem(me[dim] - k + size, size)
            remote(land.at[src], land.at[src], vec_s.at[number, k], vec_r.at[number, k], moved(me, **{dim: k})).wait_recv()
        total = land[0]
        for k in range(1, size):
            total = total + land[k]
        return total

    v_c[c] = gv[...]
    vec_start(0)

    def meet_twin(part, k):
        for j in range(2):
            cp, own = first[part, k, j]
            own.wait()
            cp.wait_recv()
        pick = sets_of(part, 0, hop(part, k))
        add_region(part, pick, (twin_w.at[:, :, :, :, :, part], twin_t.at[:, :, :, :, :, part]))

    def step_copies(part, phase, dim, step, slot, direction):
        sign = 1 if direction == 0 else -1
        size = EXTENT[dim]
        half = direction if step == 1 else None
        ahead = size // 2 - step + 1
        gone = ORDERS[part][:phase]

        def region(index):
            return sets_of(part, phase, lax.rem(index + 2 * size, size))

        going = region(me[dim] + sign * ahead)
        landing = (lands_w[part, phase, direction], lands_t[part, phase, direction])
        src = acc_views((acc_w, acc_t), part, going, half)
        dst = acc_views(landing, None, going, half, gone)
        to = moved(me, **{dim: sign})
        out = [remote(src[j], dst[j], send.at[slot, direction, j], recv.at[slot, direction, j], to) for j in range(2)]
        coming = region(me[dim] + sign * (ahead - 1))
        here = acc_views(landing, None, coming, half, gone)
        into = [remote(here[j], here[j], send.at[slot, direction, j], recv.at[slot, direction, j], to) for j in range(2)]
        return out, into, coming, landing, half, gone

    def ring_start(part, phase, dim, step, slot):
        for direction in (0, 1):
            for cp in step_copies(part, phase, dim, step, slot, direction)[0]:
                cp.start()
                sent.append(cp)

    def ring_finish(part, phase, dim, step, slot):
        for direction in (0, 1):
            _, into, coming, landing, half, gone = step_copies(part, phase, dim, step, slot, direction)
            for cp in into:
                cp.wait_recv()
            add_region(part, coming, landing, half, gone)

    plan, follow, events = {}, {}, []
    for part, order in enumerate(ORDERS):
        steps, size = [], 128
        clock = 0.0
        for phase, dim in enumerate(order):
            size //= EXTENT[dim]
            for step in range(1, EXTENT[dim] // 2 + 1):
                clock += size * (0.5 if step == 1 else 1.0)
                item = (part, phase, dim, step, part * 8 + len(steps))
                events.append((clock, item))
                steps.append(item)
        plan[part] = steps
        for one, two in zip(steps, steps[1:]):
            follow[one] = two
    events.sort()
    for part in range(3):
        meet_twin(part, 0)
        ring_start(*plan[part][0])
    met = [1, 1, 1]
    for part in range(3):
        for _ in range(2):
            meet_twin(part, met[part])
            met[part] += 1
    for number, (_, item) in enumerate(events):
        part, phase, dim, step, slot = item
        if phase == 0:
            while met[part] < min(2 * step + 1, tops[part]):
                meet_twin(part, met[part])
                met[part] += 1
            if step == EXTENT[dim] // 2:
                while met[part] < tops[part]:
                    meet_twin(part, met[part])
                    met[part] += 1
        ring_finish(*item)
        after = follow.get(item)
        if after is not None:
            ring_start(*after)
        if number in (3, 7, 11, 15):
            n = (number - 3) // 4
            total = vec_finish(n)
            if n < 3:
                vec_lands[n + 1][me[vec_dims[n + 1]]] = total
                vec_start(n + 1)
            else:
                out_v[...] = total

    for part in range(3):
        stage[pl.ds(8 * part, 8), :] = acc_w[yp, q, x, zh, m, part].astype(jnp.float32)
        tall_f[part] = acc_t[x, zh, m, yp, q, part].astype(jnp.float32)
    for owner in range(4):
        rows[owner] = stage[pl.ds(6 * owner, 6), :]
    cols = pl.ds(pl.multiple_of((c * 4 + yp * 2 + q) * 768, 128), 768)
    mine_at = yp * 2 + c
    ends = []
    for k, mate in enumerate(mates):
        o = lax.rem(mate["y"], 2) * 2 + mate["c"]
        cp = remote(rows.at[o], out_w.at[:, cols], fin_s.at[k], fin_r.at[k], mate)
        cp.start()
        ends.append(cp)
    kept = pltpu.make_async_copy(rows.at[mine_at], out_w.at[:, cols], fin_s.at[7])
    kept.start()
    half_cols = pl.ds(pl.multiple_of(c * 384, 128), 384)
    stays = c == q
    t_self = pltpu.make_async_copy(tall_f, out_t.at[:, :, half_cols], t_s.at[0])
    owner_here, owner_there = dict(me), other_q(me)
    t_twin = remote(tall_f, out_t.at[:, :, half_cols], t_s.at[0], t_r.at[0], twin)
    owner_there["c"] = q
    there_same = other_q(me)
    there_cross = other_q(twin)
    t_same = remote(tall_f, out_t.at[:, :, half_cols], t_s.at[1], t_r.at[1], there_same)
    t_cross = remote(tall_f, out_t.at[:, :, half_cols], t_s.at[1], t_r.at[2], there_cross)

    @pl.when(stays)
    def _():
        t_self.start()
        t_same.start()

    @pl.when(jnp.logical_not(stays))
    def _():
        t_twin.start()
        t_cross.start()

    for k, mate in enumerate(mates):
        from_cols = pl.ds(pl.multiple_of((mate["c"] * 4 + lax.rem(mate["y"], 2) * 2 + lax.rem(mate["z"], 2)) * 768, 128), 768)
        remote(rows.at[0], out_w.at[:, from_cols], fin_s.at[k], fin_r.at[k], mate).wait_recv()

    @pl.when(stays)
    def _():
        remote(tall_f, out_t.at[:, :, pl.ds(pl.multiple_of((1 - c) * 384, 128), 384)], t_s.at[0], t_r.at[0], twin).wait_recv()
        t_self.wait()
        t_same.wait_send()

    @pl.when(jnp.logical_not(stays))
    def _():
        remote(tall_f, out_t.at[:, :, half_cols], t_s.at[1], t_r.at[1], there_same).wait_recv()
        remote(tall_f, out_t.at[:, :, pl.ds(pl.multiple_of((1 - c) * 384, 128), 384)], t_s.at[1], t_r.at[2], there_cross).wait_recv()
        t_twin.wait_send()
        t_cross.wait_send()

    kept.wait()
    for cp in ends + vec_sent + sent:
        cp.wait_send()


def reduce_grads(gw, gt, gv):
    any_space = pl.BlockSpec(memory_space=pl.ANY)
    vmem = pl.BlockSpec(memory_space=pltpu.VMEM)

    def lands(part):
        order = ORDERS[part]
        wides, talls = [], []
        for phase in range(3):
            gone = order[:phase]
            sx = 1 if "x" in gone else 4
            sm, syp = (1, 1) if "y" in gone else (2, 2)
            szh, sq = (1, 1) if "z" in gone else (4, 2)
            wides.append([pltpu.VMEM((syp, sq, sx, szh, sm, 8, 768), jnp.bfloat16)] * 2)
            talls.append([pltpu.VMEM((sx, szh, sm, syp, sq, 8, 384), jnp.bfloat16)] * 2)
        return [wides, talls]

    return pl.pallas_call(
        reduce_kernel,
        name="reduce_grads",
        out_shape=(
            jax.ShapeDtypeStruct((6, 6144), jnp.float32),
            jax.ShapeDtypeStruct((3, 8, 768), jnp.float32),
            jax.ShapeDtypeStruct((16, 768), jnp.float32),
        ),
        in_specs=[any_space, any_space, vmem],
        out_specs=(any_space, any_space, vmem),
        scratch_shapes=[
            pltpu.VMEM((2, 2, 4, 4, 2, 3, 8, 768), jnp.bfloat16),
            pltpu.VMEM((4, 4, 2, 2, 2, 3, 8, 384), jnp.bfloat16),
            pltpu.VMEM((2, 2, 4, 4, 2, 3, 8, 768), jnp.bfloat16),
            pltpu.VMEM((4, 4, 2, 2, 2, 3, 8, 384), jnp.bfloat16),
            *lands(0), *lands(1), *lands(2),
            pltpu.VMEM((24, 768), jnp.float32),
            pltpu.VMEM((4, 6, 768), jnp.float32),
            pltpu.VMEM((3, 8, 384), jnp.float32),
            pltpu.VMEM((2, 16, 768), jnp.float32),
            pltpu.VMEM((4, 16, 768), jnp.float32),
            pltpu.VMEM((4, 16, 768), jnp.float32),
            pltpu.VMEM((8, 16, 768), jnp.float32),
            pltpu.SemaphoreType.DMA((16, 2)),
            pltpu.SemaphoreType.DMA((16, 2)),
            pltpu.SemaphoreType.DMA((16, 2)),
            pltpu.SemaphoreType.DMA((24, 2, 2)),
            pltpu.SemaphoreType.DMA((24, 2, 2)),
            pltpu.SemaphoreType.DMA((8,)),
            pltpu.SemaphoreType.DMA((7,)),
            pltpu.SemaphoreType.DMA((2,)),
            pltpu.SemaphoreType.DMA((3,)),
            pltpu.SemaphoreType.DMA((4, 8)),
            pltpu.SemaphoreType.DMA((4, 8)),
        ],
        compiler_params=pltpu.CompilerParams(
            collective_id=2, has_side_effects=True, vmem_limit_bytes=58 << 20
        ),
    )(gw, gt, gv)


ANY_SPACE = pl.BlockSpec(memory_space=pl.ANY)
LOG2E = 1.4426950408889634
TILE = 256
HALF = 384
BOTTOM = -1e30


def stream_place():
    s = lax.axis_index("shard")
    q = lax.axis_index("seq")
    return s, q, lax.rem(s, 2)


def greet_at(targets):
    barrier = pltpu.get_barrier_semaphore()
    for target in targets:
        pl.semaphore_signal(barrier, inc=1, device_id=target, device_id_type=MESH)
    pl.semaphore_wait(barrier, len(targets))


def sending(src, dst, send, recv, target):
    return pltpu.make_async_remote_copy(
        src_ref=src, dst_ref=dst, send_sem=send, recv_sem=recv, device_id=target, device_id_type=MESH
    )


def cols_of(q):
    return pl.ds(pl.multiple_of(q * HALF, 128), HALF)


def stream_mates():
    s, q, c = stream_place()
    partner = {"shard": s, "seq": 1 - q}
    twin = {"shard": s + 1 - 2 * c, "seq": q}
    after = {"shard": lax.rem(s + 2, 128), "seq": q}
    before = {"shard": lax.rem(s + 126, 128), "seq": q}
    return s, q, c, partner, twin, after, before


def spread_kernel(qkv, q_out, kv, send, recv, local):
    s, q, c, partner, twin, after, before = stream_mates()
    greet_at((partner, twin, after, before))
    mine, other = cols_of(q), cols_of(1 - q)
    beside = 2 + 4 * c
    src = qkv.at[pl.ds(1, 2), :, mine]
    out = []

    def go(src, dst, at, target):
        cp = sending(src, dst, send.at[at], recv.at[at], target)
        cp.start()
        out.append(cp)

    go(qkv.at[pl.ds(1, 2), :, other], kv.at[:, 4 + q], 0, partner)
    go(src, kv.at[:, q], 1, after)
    go(src, kv.at[:, 8 + q], 2, before)
    go(src, kv.at[:, beside + q], 3, twin)
    go(qkv.at[0, :, other], q_out.at[q], 4, partner)
    kept = [
        pltpu.make_async_copy(src, kv.at[:, 4 + q], local.at[0]),
        pltpu.make_async_copy(qkv.at[0, :, mine], q_out.at[q], local.at[1]),
    ]
    for cp in kept:
        cp.start()

    def arrive(dst, at, target):
        sending(dst, dst, send.at[at], recv.at[at], target).wait_recv()

    theirs = kv.at[:, 4 + 1 - q]
    arrive(theirs, 0, partner)
    go(theirs, kv.at[:, 1 - q], 5, after)
    go(theirs, kv.at[:, 8 + 1 - q], 6, before)
    go(theirs, kv.at[:, beside + 1 - q], 7, twin)
    edge, inner = 8 * (1 - c), 6 - 4 * c
    for h, first, at in ((q, 1, 8), (1 - q, 5, 9)):
        arrive(kv.at[:, h], first, before)
        arrive(kv.at[:, 8 + h], first + 1, after)
        go(kv.at[:, edge + h], kv.at[:, inner + h], at, twin)
    for cp in kept:
        cp.wait()
    arrive(q_out.at[1 - q], 4, partner)
    for h, at, target in ((q, 3, twin), (1 - q, 7, twin)):
        arrive(kv.at[:, 6 - 4 * c + h], at, target)
    for h, at in ((q, 8), (1 - q, 9)):
        arrive(kv.at[:, 2 + 4 * c + h], at, twin)
    for cp in out:
        cp.wait_send()


def spread(qkv):
    return pl.pallas_call(
        spread_kernel,
        name="spread",
        out_shape=(
            jax.ShapeDtypeStruct((2, TILE, HALF), jnp.bfloat16),
            jax.ShapeDtypeStruct((2, 10, TILE, HALF), jnp.bfloat16),
        ),
        in_specs=[ANY_SPACE],
        out_specs=(ANY_SPACE, ANY_SPACE),
        scratch_shapes=[
            pltpu.SemaphoreType.DMA((10,)), pltpu.SemaphoreType.DMA((10,)), pltpu.SemaphoreType.DMA((2,)),
        ],
        compiler_params=pltpu.CompilerParams(collective_id=3, has_side_effects=True),
    )(qkv)


def to_tokens_kernel(heads, rows, send, recv, local):
    s, q, c, partner, *_ = stream_mates()
    greet_at((partner,))
    kept = pltpu.make_async_copy(heads.at[q], rows.at[:, cols_of(q)], local.at[0])
    out = sending(heads.at[1 - q], rows.at[:, cols_of(q)], send.at[0], recv.at[0], partner)
    out.start()
    kept.start()
    kept.wait()
    sending(heads.at[q], rows.at[:, cols_of(1 - q)], send.at[0], recv.at[0], partner).wait_recv()
    out.wait_send()


def to_heads_kernel(rows, heads, send, recv, local):
    s, q, c, partner, *_ = stream_mates()
    greet_at((partner,))
    kept = pltpu.make_async_copy(rows.at[:, cols_of(q)], heads.at[q], local.at[0])
    out = sending(rows.at[:, cols_of(1 - q)], heads.at[q], send.at[0], recv.at[0], partner)
    out.start()
    kept.start()
    kept.wait()
    sending(rows.at[:, cols_of(q)], heads.at[1 - q], send.at[0], recv.at[0], partner).wait_recv()
    out.wait_send()


def swap(kernel, name, shape, number, array):
    return pl.pallas_call(
        kernel,
        name=name,
        out_shape=jax.ShapeDtypeStruct(shape, array.dtype),
        in_specs=[ANY_SPACE],
        out_specs=ANY_SPACE,
        scratch_shapes=[pltpu.SemaphoreType.DMA((1,))] * 3,
        compiler_params=pltpu.CompilerParams(collective_id=number, has_side_effects=True),
    )(array)


def lanes_low(rows):
    return lax.broadcasted_iota(jnp.int32, (rows, 128), 1) < 64


def across_lanes(a, b):
    return lax.dot_general(a, b, (((1,), (1,)), ((), ())), preferred_element_type=jnp.float32)


def down_rows(a, b):
    return lax.dot_general(a, b, (((0,), (0,)), ((), ())), preferred_element_type=jnp.float32)


def attend_kernel(bounds, q_docs, k_docs, q_ref, kv, o_ref, lse_ref, top, total, acc):
    i = pl.program_id(1)
    low = lanes_low(TILE)
    q = q_ref[0]
    none = jnp.zeros_like(q)
    q_heads = (jnp.where(low, q, none), jnp.where(low, none, q))
    docs = q_docs[0]
    top[...] = jnp.full_like(top, BOTTOM)
    total[...] = jnp.zeros_like(total)
    acc[...] = jnp.zeros_like(acc)
    scale = HEAD_DIM ** -0.5 * LOG2E

    def step(j, carry):
        k, v = kv[0, j], jnp.swapaxes(kv[1, j], 0, 1)
        same = docs == k_docs[j]
        for head in range(2):
            rows = slice(head * HEAD_DIM, (head + 1) * HEAD_DIM)
            s = jnp.where(same, across_lanes(k, q_heads[head]) * scale, BOTTOM)
            old = top[head]
            new = jnp.maximum(old, jnp.max(s, axis=0, keepdims=True))
            fade = jnp.exp2(old - new)
            p = jnp.exp2(s - new)
            total[head] = total[head] * fade + jnp.sum(p, axis=0, keepdims=True)
            top[head] = new
            acc[rows] = acc[rows] * fade + jnp.dot(
                v[rows], p.astype(jnp.bfloat16), preferred_element_type=jnp.float32
            )
        return carry

    lax.fori_loop(bounds[i, 0], bounds[i, 1], step, 0)
    for head in range(2):
        rows = slice(head * HEAD_DIM, (head + 1) * HEAD_DIM)
        acc[rows] = acc[rows] / total[head]
        lse_ref[0, 0, pl.ds(head, 1)] = top[head] + jnp.log2(total[head])
    o_ref[0] = jnp.swapaxes(acc[...], 0, 1).astype(jnp.bfloat16)


def attend(bounds, q_docs, k_docs, q_heads, kv):
    return pl.pallas_call(
        attend_kernel,
        name="attend",
        grid_spec=pltpu.PrefetchScalarGridSpec(
            num_scalar_prefetch=1,
            grid=(3, 2),
            in_specs=[
                pl.BlockSpec((1, 1, TILE), lambda p, i, b: (i, 0, 0)),
                pl.BlockSpec((10, TILE, 1), lambda p, i, b: (0, 0, 0)),
                pl.BlockSpec((1, TILE, 128), lambda p, i, b: (i, 0, p)),
                pl.BlockSpec((2, 10, TILE, 128), lambda p, i, b: (0, 0, 0, p)),
            ],
            out_specs=[
                pl.BlockSpec((1, TILE, 128), lambda p, i, b: (i, 0, p)),
                pl.BlockSpec((1, 1, 2, TILE), lambda p, i, b: (p, i, 0, 0)),
            ],
            scratch_shapes=[
                pltpu.VMEM((2, 1, TILE), jnp.float32),
                pltpu.VMEM((2, 1, TILE), jnp.float32),
                pltpu.VMEM((128, TILE), jnp.float32),
            ],
        ),
        out_shape=(
            jax.ShapeDtypeStruct((2, TILE, HALF), jnp.bfloat16),
            jax.ShapeDtypeStruct((3, 2, 2, TILE), jnp.float32),
        ),
        compiler_params=pltpu.CompilerParams(vmem_limit_bytes=40 << 20),
    )(bounds, q_docs, k_docs, q_heads, kv)


def attend_back_kernel(bounds, q_docs, k_docs, q_ref, do_ref, o_ref, lse_ref, kv, dq_ref, dkv_ref, dkv, dq):
    i = pl.program_id(1)
    low = lanes_low(TILE)

    @pl.when(i == 0)
    def _():
        dkv[...] = jnp.zeros_like(dkv)

    q, d_out = q_ref[0], do_ref[0]
    none = jnp.zeros_like(q)
    q_heads = (jnp.where(low, q, none), jnp.where(low, none, q))
    do_heads = (jnp.where(low, d_out, none), jnp.where(low, none, d_out))
    prod = d_out.astype(jnp.float32) * o_ref[0].astype(jnp.float32)
    first = lax.broadcasted_iota(jnp.int32, (8, 128), 0)
    halves = lax.broadcasted_iota(jnp.int32, (8, 128), 1) // HEAD_DIM
    deltas = lax.dot_general(
        (first == halves).astype(jnp.float32), prod, (((1,), (1,)), ((), ())),
        precision=lax.Precision.HIGHEST, preferred_element_type=jnp.float32,
    )
    deltas = (deltas[0:1], deltas[1:2])
    lses = (lse_ref[0, 0, 0:1], lse_ref[0, 0, 1:2])
    docs = q_docs[0]
    dq[...] = jnp.zeros_like(dq)
    scale = HEAD_DIM ** -0.5 * LOG2E

    def step(j, carry):
        k, v = kv[0, j], kv[1, j]
        k_flip = jnp.swapaxes(k, 0, 1)
        same = docs == k_docs[j]
        dk, dv = [], []
        for head in range(2):
            rows = slice(head * HEAD_DIM, (head + 1) * HEAD_DIM)
            s = across_lanes(k, q_heads[head]) * scale
            p = jnp.where(same, jnp.exp2(s - lses[head]), 0.0)
            dp = across_lanes(v, do_heads[head])
            ds = (p * (dp - deltas[head])).astype(jnp.bfloat16)
            p_low = p.astype(jnp.bfloat16)
            dq[rows] += jnp.dot(k_flip[rows], ds, preferred_element_type=jnp.float32)
            dk.append(jnp.dot(ds, q_heads[head], preferred_element_type=jnp.float32))
            dv.append(jnp.dot(p_low, do_heads[head], preferred_element_type=jnp.float32))
        dkv[0, j] += dk[0] + dk[1]
        dkv[1, j] += dv[0] + dv[1]
        return carry

    lax.fori_loop(bounds[i, 0], bounds[i, 1], step, 0)
    dq_ref[0] = jnp.swapaxes(dq[...] * HEAD_DIM ** -0.5, 0, 1).astype(jnp.bfloat16)

    @pl.when(i == 1)
    def _():
        dkv_ref[0] = (dkv[0] * HEAD_DIM ** -0.5).astype(jnp.bfloat16)
        dkv_ref[1] = dkv[1].astype(jnp.bfloat16)


def attend_back(bounds, q_docs, k_docs, q_heads, d_heads, o_heads, lse, kv):
    own = pl.BlockSpec((1, TILE, 128), lambda p, i, b: (i, 0, p))
    window = pl.BlockSpec((2, 10, TILE, 128), lambda p, i, b: (0, 0, 0, p))
    return pl.pallas_call(
        attend_back_kernel,
        name="attend_back",
        grid_spec=pltpu.PrefetchScalarGridSpec(
            num_scalar_prefetch=1,
            grid=(3, 2),
            in_specs=[
                pl.BlockSpec((1, 1, TILE), lambda p, i, b: (i, 0, 0)),
                pl.BlockSpec((10, TILE, 1), lambda p, i, b: (0, 0, 0)),
                own, own, own,
                pl.BlockSpec((1, 1, 2, TILE), lambda p, i, b: (p, i, 0, 0)),
                window,
            ],
            out_specs=[own, window],
            scratch_shapes=[
                pltpu.VMEM((2, 10, TILE, 128), jnp.float32),
                pltpu.VMEM((128, TILE), jnp.float32),
            ],
        ),
        out_shape=(
            jax.ShapeDtypeStruct((2, TILE, HALF), jnp.bfloat16),
            jax.ShapeDtypeStruct((2, 10, TILE, HALF), jnp.bfloat16),
        ),
        compiler_params=pltpu.CompilerParams(vmem_limit_bytes=40 << 20),
    )(bounds, q_docs, k_docs, q_heads, d_heads, o_heads, lse, kv)


def collect_kernel(dq, dkv, out, edges, own, beside, passed, result, send, recv, local):
    s, q, c, partner, twin, after, before = stream_mates()
    greet_at((partner, twin, after, before))
    mine = cols_of(q)
    sent = []

    def go(src, dst, at, target):
        cp = sending(src, dst, send.at[at], recv.at[at], target)
        cp.start()
        sent.append(cp)

    def arrive(dst, at, target):
        sending(dst, dst, send.at[at], recv.at[at], target).wait_recv()

    go(dkv.at[:, pl.ds(2, 2)], beside.at[0], 0, twin)
    go(dkv.at[:, pl.ds(6, 2)], beside.at[1], 1, twin)
    loads = [
        pltpu.make_async_copy(dkv.at[:, pl.ds(0, 2)], edges.at[0], local.at[0]),
        pltpu.make_async_copy(dkv.at[:, pl.ds(8, 2)], edges.at[1], local.at[1]),
        pltpu.make_async_copy(dkv.at[:, pl.ds(4, 2)], own, local.at[2]),
        pltpu.make_async_copy(dq.at[q], out.at[0, :, mine], local.at[3]),
    ]
    for cp in loads:
        cp.start()
    go(dq.at[1 - q], out.at[0, :, mine], 2, partner)
    loads[0].wait()
    loads[1].wait()
    arrive(beside.at[0], 0, twin)
    arrive(beside.at[1], 1, twin)
    outer = 1 - c

    def sums(h, fn):
        for j in range(2):
            def rows(r, _):
                at = (j, h, pl.ds(pl.multiple_of(r * 64, 64), 64), slice(None))
                fn(at)
                return 0
            lax.fori_loop(0, TILE // 64, rows, 0)

    for n, h in enumerate((1 - q, q)):
        def one(at):
            edges[(outer, *at)] = (
                edges[(outer, *at)].astype(jnp.float32) + beside[(outer, *at)].astype(jnp.float32)
            ).astype(jnp.bfloat16)

        sums(h, one)
        go(edges.at[0, :, h], passed.at[1, :, h], 3 + n, before)
        go(edges.at[1, :, h], passed.at[0, :, h], 5 + n, after)
    loads[2].wait()
    kept = None
    for n, h in enumerate((1 - q, q)):
        arrive(passed.at[1, :, h], 3 + n, after)
        arrive(passed.at[0, :, h], 5 + n, before)

        def one(at):
            f = jnp.float32
            total = own[at].astype(f) + beside[(c, *at)].astype(f) + (passed[(0, *at)].astype(f) + passed[(1, *at)].astype(f))
            result[at] = total.astype(jnp.bfloat16)

        sums(h, one)
        if n == 0:
            go(result.at[:, h], out.at[pl.ds(1, 2), :, mine], 7, partner)
        else:
            kept = pltpu.make_async_copy(result.at[:, h], out.at[pl.ds(1, 2), :, mine], local.at[4])
            kept.start()
    loads[3].wait()
    kept.wait()
    theirs = cols_of(1 - q)
    arrive(out.at[0, :, theirs], 2, partner)
    arrive(out.at[pl.ds(1, 2), :, theirs], 7, partner)
    for cp in sent:
        cp.wait_send()


def collect(dq, dkv):
    pair = (2, 2, TILE, HALF)
    return pl.pallas_call(
        collect_kernel,
        name="collect",
        out_shape=jax.ShapeDtypeStruct((3, TILE, 2 * HALF), jnp.bfloat16),
        in_specs=[ANY_SPACE, ANY_SPACE],
        out_specs=ANY_SPACE,
        scratch_shapes=[
            pltpu.VMEM((2, *pair), jnp.bfloat16),
            pltpu.VMEM(pair, jnp.bfloat16),
            pltpu.VMEM((2, *pair), jnp.bfloat16),
            pltpu.VMEM((2, *pair), jnp.bfloat16),
            pltpu.VMEM(pair, jnp.bfloat16),
            pltpu.SemaphoreType.DMA((8,)),
            pltpu.SemaphoreType.DMA((8,)),
            pltpu.SemaphoreType.DMA((5,)),
        ],
        compiler_params=pltpu.CompilerParams(collective_id=6, has_side_effects=True, vmem_limit_bytes=30 << 20),
    )(dq, dkv)


from jax.sharding import PartitionSpec as P

DOC_MAX = 1024
NORM_EPS = 1e-12


def layer_norm(resid, gain_vec, shift_vec):
    row_mean = jnp.mean(resid, axis=-1, keepdims=True)
    centred = resid - row_mean
    variance = jnp.mean(centred * centred, axis=-1, keepdims=True)
    return centred * lax.rsqrt(variance + NORM_EPS) * gain_vec + shift_vec


def doc_index(doc_lengths, positions, stream_len):
    starts = jnp.cumsum(doc_lengths, dtype=jnp.int32) - doc_lengths
    counted = jnp.sum((positions[:, None] >= starts[None, :]).astype(jnp.int32), axis=1, dtype=jnp.int32) - 1
    return jnp.where(positions < stream_len, counted, stream_len)


def dot32(spec, a, b):
    return jnp.einsum(spec, a, b, preferred_element_type=jnp.float32)


def body(
    tokens, w_qkv, bias_q, bias_v, w_out, bias_out, gain_one, shift_one, w_in, bias_in,
    w_down, bias_down, gain_two, shift_two, doc_lengths, cotangent,
):
    seq_count = lax.axis_size("seq")
    shard_count = lax.axis_size("shard")
    shard_place = lax.axis_index("shard")
    tok_rows, model_width = tokens.shape
    half_width = model_width // seq_count
    group_rows = tok_rows * seq_count
    reach_groups = 1 + (DOC_MAX - 2) // group_rows
    window = (2 * reach_groups + 1) * group_rows
    stream_len = group_rows * shard_count
    key_pos = (shard_place - reach_groups) * group_rows + jnp.arange(window, dtype=jnp.int32)
    key_docs = doc_index(doc_lengths, key_pos, stream_len)
    query_docs = key_docs[reach_groups * group_rows : (reach_groups + 1) * group_rows].reshape(2, 1, TILE)
    key_docs = key_docs.reshape(10, TILE, 1)
    first, last = query_docs[:, :, 0], query_docs[:, :, -1]
    bounds = jnp.stack(
        [
            jnp.sum((key_docs[:, -1, 0] < first).astype(jnp.int32), axis=1),
            jnp.sum((key_docs[:, 0, 0] <= last).astype(jnp.int32), axis=1),
        ],
        axis=1,
    )

    vectors = (bias_q, bias_v, bias_out, gain_one, shift_one, bias_down, gain_two, shift_two)
    vec = jnp.concatenate(
        [
            jnp.stack(vectors).astype(jnp.float32),
            jnp.pad(bias_in.astype(jnp.float32).reshape(1, 24), ((0, 7), (0, 0))),
            jnp.zeros((8, 98), jnp.float32),
        ],
        axis=1,
    )
    cat = jnp.concatenate([w_qkv, w_out, w_in], axis=1)
    wide, tall, vecs = gather_weights(cat, w_down.reshape(3, 8, model_width), vec)
    wide = wide.reshape(8, model_width, model_width)
    tall = tall.reshape(2, 4 * model_width, model_width // 2)
    vecs = jnp.transpose(vecs, (4, 1, 2, 3, 0, 5)).reshape(8, 128, 128)
    rows = vecs[:, :, :6].reshape(8, 1, model_width)
    bias_q_all, bias_v_all, bias_out_all, gain_one_all, shift_one_all, bias_down_all, gain_two_all, shift_two_all = rows
    bias_in_all = vecs[0, :, 6:30].reshape(4, 1, model_width)

    qkv = dot32("td,cdn->ctn", tokens, wide[:3])
    shifts = jnp.stack([bias_q_all, jnp.zeros_like(bias_q_all), bias_v_all])
    q_heads, kv = spread((qkv + shifts).astype(jnp.bfloat16))
    o_heads, lse = attend(bounds, query_docs, key_docs, q_heads, kv)
    back_tokens = swap(to_tokens_kernel, "to_tokens", (tok_rows, model_width), 4, o_heads)
    branch = jnp.dot(back_tokens, wide[3], preferred_element_type=jnp.float32) + bias_out_all
    resid_one = tokens.astype(jnp.float32) + branch
    normed, norm_one_pull = jax.vjp(layer_norm, resid_one, gain_one_all, shift_one_all)
    normed_low = normed.astype(jnp.bfloat16)
    hidden = dot32("td,cdn->ctn", normed_low, wide[4:]) + bias_in_all
    active, gelu_pull = jax.vjp(lambda h: jax.nn.gelu(h, approximate=False), hidden)
    active_low = active.astype(jnp.bfloat16)
    tall4 = tall.reshape(2, 4, model_width, model_width // 2)
    branch_two = jnp.concatenate([dot32("ctf,cfn->tn", active_low, tall4[j]) for j in range(2)], axis=1) + bias_down_all
    resid_two = normed + branch_two
    layer_value, norm_two_pull = jax.vjp(layer_norm, resid_two, gain_two_all, shift_two_all)
    layer_out = layer_value.astype(jnp.bfloat16)

    d_resid_two, d_gain_two, d_shift_two = norm_two_pull(cotangent.astype(jnp.float32))
    d_branch_two = d_resid_two.astype(jnp.bfloat16)
    d_bias_down = jnp.sum(d_resid_two, axis=0, keepdims=True)
    grads_down = [
        dot32("ctf,tn->cfn", active_low, d_branch_two[:, j * half_width : (j + 1) * half_width]).astype(jnp.bfloat16)
        for j in range(2)
    ]
    d_active = sum(
        dot32("tn,cfn->ctf", d_branch_two[:, j * half_width : (j + 1) * half_width], tall4[j]) for j in range(2)
    )
    d_hidden = gelu_pull(d_active)[0].astype(jnp.bfloat16)
    d_bias_in = jnp.sum(d_hidden.astype(jnp.float32), axis=1)
    grad_in = dot32("td,ctn->cdn", normed_low, d_hidden).astype(jnp.bfloat16)
    d_normed = d_resid_two + dot32("ctn,cdn->td", d_hidden, wide[4:])
    d_resid_one, d_gain_one, d_shift_one = norm_one_pull(d_normed)
    d_branch = d_resid_one.astype(jnp.bfloat16)
    d_bias_out = jnp.sum(d_resid_one, axis=0, keepdims=True)
    grad_out = dot32("tc,td->cd", back_tokens, d_branch).astype(jnp.bfloat16)
    d_attended = dot32("td,cd->tc", d_branch, wide[3]).astype(jnp.bfloat16)
    d_heads = swap(to_heads_kernel, "to_heads", (seq_count, tok_rows, half_width), 5, d_attended)
    d_qkv = collect(*attend_back(bounds, query_docs, key_docs, q_heads, d_heads, o_heads, lse, kv))
    d_bias_q = jnp.sum(d_qkv[0].astype(jnp.float32), axis=0, keepdims=True)
    d_bias_v = jnp.sum(d_qkv[2].astype(jnp.float32), axis=0, keepdims=True)
    grad_qkv = dot32("td,ctn->cdn", tokens, d_qkv).astype(jnp.bfloat16)
    grad_tokens = d_resid_one + dot32("ctn,cdn->td", d_qkv, wide[:3])

    gw = jnp.concatenate([grad_qkv, grad_out[None], grad_in], axis=0).reshape(2, 2, 2, 4, 4, 2, 3, 8, model_width)
    gt = jnp.stack(grads_down).reshape(2, 4, 4, 2, 2, 2, 3, 8, half_width)
    gv = jnp.concatenate(
        [d_bias_q, d_bias_v, d_bias_out, d_gain_one, d_shift_one, d_bias_down, d_gain_two, d_shift_two, d_bias_in,
         jnp.zeros((4, model_width), jnp.float32)], axis=0)
    sum_w, sum_t, sum_v = reduce_grads(gw, gt, gv)
    mine = lax.dynamic_slice(sum_v, (0, 6 * shard_place), (8, 6))
    in_mine = lax.dynamic_slice(sum_v[8:12].reshape(-1), (24 * shard_place,), (24,))
    return (
        layer_out, grad_tokens, sum_w[:, : 3 * model_width], mine[0], mine[1],
        sum_w[:, 3 * model_width : 4 * model_width], mine[2], mine[3], mine[4],
        sum_w[:, 4 * model_width :], in_mine, sum_t.reshape(24, model_width), mine[5], mine[6], mine[7],
    )


def solution(mesh):
    both, own = P(("shard", "seq"), None), P("shard")
    rows = P("shard", None)
    return jax.shard_map(
        body,
        mesh=mesh,
        in_specs=(both, rows, own, own, rows, own, own, own, rows, own, rows, own, own, own, P(), both),
        out_specs=(both, both, rows, own, own, rows, own, own, own, rows, own, rows, own, own, own),
        check_vma=False,
    )
```

```python
import functools
import jax
import jax.numpy as jnp
from jax import lax
from jax.experimental import pallas as pl
from jax.experimental.pallas import tpu as pltpu
from jax.sharding import PartitionSpec as P

HEAD_DIM = 64
NORM_EPS = 1e-12
MESH = pl.DeviceIdType.MESH
ANY_SPACE = pl.BlockSpec(memory_space=pl.ANY)
IN_VMEM = pl.BlockSpec(memory_space=pltpu.VMEM)
LOG2E = 1.4426950408889634
TILE = 256
HALF = 384
BOTTOM = -1e30
EXTENT = {"x": 4, "y": 4, "z": 8}
ORDERS = (("z", "y", "x"), ("z", "y", "x"), ("z", "x", "y"))
OTHERS = {dim: range(1, size) for dim, size in EXTENT.items()}
HALVES = (((0, 256), (256, 128)), ((0, 128), (128, 256)), ((0, 256), (256, 128)))
STREAMS = (0, 1, 2)
WIDE = (2, 2, 4, 4, 2, 3, 8, HALF)
TALL = (4, 4, 2, 2, 2, 3, 8, HALF)


def place():
    s = lax.axis_index("shard")
    q = lax.axis_index("seq")
    return {
        "c": lax.rem(s, 2),
        "y": lax.rem(s // 2, 4),
        "x": s // 32,
        "z": lax.rem(s // 8, 4) * 2 + q,
    }


def device_at(at):
    return {
        "shard": ((at["x"] * 4 + at["z"] // 2) * 4 + at["y"]) * 2 + at["c"],
        "seq": lax.rem(at["z"], 2),
    }


def moved(at, **steps):
    new = dict(at)
    for dim, step in steps.items():
        size = 2 if dim == "c" else EXTENT[dim]
        new[dim] = lax.rem(at[dim] + step + size, size)
    return new


def stream_mates():
    s = lax.axis_index("shard")
    q = lax.axis_index("seq")
    partner = {"shard": s, "seq": 1 - q}
    after = {"shard": lax.rem(s + 2, 128), "seq": q}
    before = {"shard": lax.rem(s + 126, 128), "seq": q}
    return partner, before, after


def greet(targets):
    barrier = pltpu.get_barrier_semaphore()
    for target in targets:
        pl.semaphore_signal(barrier, inc=1, device_id=target, device_id_type=MESH)
    pl.semaphore_wait(barrier, len(targets))


def sending(src, dst, send, recv, target):
    return pltpu.make_async_remote_copy(
        src_ref=src, dst_ref=dst, send_sem=send, recv_sem=recv, device_id=target, device_id_type=MESH
    )


def neighbours(at):
    return [moved(at, **{d: step}) for d in ("x", "y", "z") for step in (1, -1)]


def octet_mates(me):
    across = dict(me)
    across["y"] = me["y"] + 1 - 2 * lax.rem(me["y"], 2)
    twin = moved(me, c=1)
    diagonal = dict(across)
    diagonal["c"] = twin["c"]
    return twin, across, diagonal


def span(index):
    return slice(None) if index is None else pl.ds(index, 1)


def picks_of(sets, gone=()):
    x, y, z = sets["x"], sets["y"], sets["z"]
    pick = {
        "x": x,
        "m": None if y is None else y // 2,
        "yp": None if y is None else lax.rem(y, 2),
        "zh": None if z is None else z // 2,
        "q": None if z is None else lax.rem(z, 2),
    }
    names = {"x": ("x",), "y": ("m", "yp"), "z": ("zh", "q")}
    for dim in gone:
        for name in names[dim]:
            pick[name] = 0
    return pick


WIDE_DIMS = ("yp", "q", "x", "zh", "m")
TALL_DIMS = ("x", "zh", "m", "yp", "q")
DIM_SIZE = {"yp": 2, "q": 2, "x": 4, "zh": 4, "m": 2}


def dims_of(k):
    return TALL_DIMS if k == 2 else WIDE_DIMS


def view(ref, k, part, sets, half=None, gone=(), lead=()):
    pick = picks_of(sets, gone)
    cut = (0, HALF) if half is None else HALVES[k][half]
    at = tuple(span(pick[d]) for d in dims_of(k))
    rows = () if part is None else (part,)
    return ref.at[(*lead, *at, *rows, slice(None), pl.ds(*cut))]


def gather_kernel(
    cat_ref, down_ref, vec_ref, tok_ref, first, second, third, vecs, window,
    land, stage, own, oct_s, oct_r, local, near_s, near_r, send, recv, core_s, core_r, vec_s, vec_r, tok_s, tok_r,
):
    me = place()
    c, x, y, z = me["c"], me["x"], me["y"], me["z"]
    yp, q, m, zh = lax.rem(y, 2), lax.rem(z, 2), y // 2, z // 2
    outs = (first, second, third)
    twin, across, diagonal = octet_mates(me)
    twin_id = device_at(twin)
    partner, before, after = stream_mates()
    lines = [moved(me, **{d: o}) for d in EXTENT for o in OTHERS[d]]
    greet([device_at(a) for a in lines + [twin, diagonal]] + [before, after])

    def chunk_of(at):
        cols = (lax.rem(at["y"], 2) * 2 + q) * 768 + at["c"] * HALF
        return cat_ref.at[:, :, pl.ds(pl.multiple_of(cols, 128), HALF)]

    index = yp * 2 + c
    mates = (twin, across, diagonal)
    out = [
        sending(chunk_of(mate), land.at[:, index], oct_s.at[k], oct_r.at[k], device_at(mate))
        for k, mate in enumerate(mates)
    ]
    for cp in out:
        cp.start()
    kept = pltpu.make_async_copy(chunk_of(me), land.at[:, index], local.at[0])
    kept.start()
    gives = q == c
    down_out = sending(
        down_ref.at[:, :, pl.ds(pl.multiple_of((1 - c) * HALF, 128), HALF)], own.at[2], oct_s.at[3], oct_r.at[3], twin_id
    )
    down_kept = pltpu.make_async_copy(
        down_ref.at[:, :, pl.ds(pl.multiple_of(c * HALF, 128), HALF)], own.at[2], local.at[1]
    )

    @pl.when(gives)
    def _():
        down_out.start()
        down_kept.start()

    vec_kept = pltpu.make_async_copy(vec_ref, vecs.at[c, x, zh, y], local.at[2])
    vec_kept.start()

    sent = []

    def go(src, dst, send_sem, recv_sem, target):
        cp = sending(src, dst, send_sem, recv_sem, target)
        cp.start()
        sent.append(cp)

    def arrive(dst, send_sem, recv_sem, target):
        sending(dst, dst, send_sem, recv_sem, target).wait_recv()

    def tok_go(src, dst, at, target):
        go(src, dst, tok_s.at[at], tok_r.at[at], target)

    tok_kept = pltpu.make_async_copy(tok_ref, window.at[1, c, q], local.at[3])
    tok_kept.start()
    tok_go(tok_ref, window.at[1, c, q], 0, partner)
    tok_go(tok_ref, window.at[0, c, q], 1, after)
    tok_go(tok_ref, window.at[2, c, q], 2, before)
    tok_go(tok_ref, window.at[1, c, q], 3, twin_id)

    def tok_forward():
        theirs = window.at[1, c, 1 - q]
        arrive(theirs, tok_s.at[0], tok_r.at[0], partner)
        tok_go(theirs, window.at[0, c, 1 - q], 4, after)
        tok_go(theirs, window.at[2, c, 1 - q], 5, before)
        tok_go(theirs, window.at[1, c, 1 - q], 6, twin_id)

    def tok_share(h, first_slot, at):
        arrive(window.at[0, c, h], tok_s.at[first_slot], tok_r.at[first_slot], before)
        arrive(window.at[2, c, h], tok_s.at[first_slot + 1], tok_r.at[first_slot + 1], after)
        tok_go(window.at[0, c, h], window.at[0, c, h], at, twin_id)
        tok_go(window.at[2, c, h], window.at[2, c, h], at + 1, twin_id)

    vec_rounds = (("x", (1, 2, 3)), ("y", (1, 2, 3)), ("z", (2, 4, 6)), ("c", (1,)))

    def vec_copies(number, arriving):
        dim, steps = vec_rounds[number]
        done = [d for d, _ in vec_rounds[:number]]
        copies = []
        for k, step in enumerate(steps):
            source = moved(me, **{dim: (1 if dim == "c" else -step)}) if arriving else me
            pick = [None if d in done else (source["z"] // 2 if d == "z" else source[d]) for d in ("c", "x", "z", "y")]
            ref = vecs.at[tuple(span(p) for p in pick)]
            copies.append(
                sending(ref, ref, vec_s.at[number, k], vec_r.at[number, k], device_at(moved(me, **{dim: step})))
            )
        return copies

    def vec_start(number):
        for cp in vec_copies(number, False):
            cp.start()
            sent.append(cp)

    def vec_wait(number):
        for cp in vec_copies(number, True):
            cp.wait_recv()

    kept.wait()
    for k, mate in enumerate(mates):
        mate_index = lax.rem(mate["y"], 2) * 2 + mate["c"]
        arrive(land.at[:, mate_index], oct_s.at[k], oct_r.at[k], device_at(mate))
    for k in range(2):
        for owner in range(4):
            stage[pl.ds(6 * owner, 6), :] = land[k, owner].astype(jnp.float32)
        for part in range(3):
            own[k, part] = stage[pl.ds(8 * part, 8), :].astype(jnp.bfloat16)

    @pl.when(gives)
    def _():
        down_kept.wait()

    @pl.when(jnp.logical_not(gives))
    def _():
        down_out.wait_recv()

    homes = (first.at[c, yp, q, x, zh, m], second.at[c, yp, q, x, zh, m], third.at[c, x, zh, m, yp, q])
    flush = [pltpu.make_async_copy(own.at[k], homes[k], local.at[4 + k]) for k in STREAMS]
    for cp in flush:
        cp.start()
    twins = []

    def share(k, part, sets, half, slot):
        mine = view(outs[k], k, part, sets, half, (), (c,))
        theirs = view(outs[k], k, part, sets, half, (), (1 - c,))
        go(mine, mine, core_s.at[slot, k], core_r.at[slot, k], twin_id)
        twins.append((theirs, core_s.at[slot, k], core_r.at[slot, k]))

    def sets_at(part, phase, index):
        sets = {"x": x, "y": y, "z": z}
        for earlier in ORDERS[part][:phase]:
            sets[earlier] = None
        dim = ORDERS[part][phase]
        sets[dim] = lax.rem(index + EXTENT[dim], EXTENT[dim])
        return sets

    def near(k, part, phase, arriving):
        dim = ORDERS[part][phase]
        for o in OTHERS[dim]:
            sems = near_s.at[part, phase, o, k], near_r.at[part, phase, o, k]
            target = device_at(moved(me, **{dim: o}))
            if arriving:
                arrive(view(outs[k], k, part, sets_at(part, phase, me[dim] - o), None, (), (c,)), *sems, target)
            elif phase == 0:
                go(own.at[k, part], homes[k].at[part], *sems, target)
            else:
                ref = view(outs[k], k, part, sets_at(part, phase, me[dim]), None, (), (c,))
                go(ref, ref, *sems, target)

    def ring(k, part, step, arriving):
        dim = ORDERS[part][2]
        size = EXTENT[dim]
        for direction, sign in enumerate((1, -1)):
            sets = sets_at(part, 2, me[dim] - sign * (step if arriving else step - 1))
            half = direction if step == size // 2 else None
            ref = view(outs[k], k, part, sets, half, (), (c,))
            slot = part * 2 + step - 1
            sems = send.at[slot, direction, k], recv.at[slot, direction, k]
            target = device_at(moved(me, **{dim: sign}))
            if arriving:
                arrive(ref, *sems, target)
            else:
                go(ref, ref, *sems, target)

    def ring_share(k, part, step):
        dim = ORDERS[part][2]
        for direction, sign in enumerate((1, -1)):
            half = direction if step == EXTENT[dim] // 2 else None
            share(k, part, sets_at(part, 2, me[dim] - sign * step), half, 3 + (part * 2 + step - 1) * 2 + direction)

    for k in STREAMS:
        for part in range(3):
            near(k, part, 0, False)
    vec_kept.wait()
    vec_start(0)
    for cp in flush:
        cp.wait()
    for k in STREAMS:
        for part in range(3):
            near(k, part, 0, True)
            near(k, part, 1, False)
    tok_forward()
    vec_wait(0)
    vec_start(1)
    for k in STREAMS:
        for part in range(3):
            near(k, part, 1, True)
            ring(k, part, 1, False)
    for k in STREAMS:
        for part in range(3):
            share(k, part, sets_at(part, 2, me[ORDERS[part][2]]), None, part)
    vec_wait(1)
    vec_start(2)
    for k in STREAMS:
        for part in range(3):
            ring(k, part, 1, True)
            ring(k, part, 2, False)
            ring_share(k, part, 1)
    vec_wait(2)
    vec_start(3)
    tok_share(q, 1, 7)
    for k in STREAMS:
        for part in range(3):
            ring(k, part, 2, True)
            ring_share(k, part, 2)
    tok_share(1 - q, 4, 9)
    vec_wait(3)
    for ref, send_sem, recv_sem in twins:
        arrive(ref, send_sem, recv_sem, twin_id)
    arrive(window.at[1, 1 - c, q], tok_s.at[3], tok_r.at[3], twin_id)
    arrive(window.at[1, 1 - c, 1 - q], tok_s.at[6], tok_r.at[6], twin_id)
    for h, at in ((q, 7), (1 - q, 9)):
        arrive(window.at[0, 1 - c, h], tok_s.at[at], tok_r.at[at], twin_id)
        arrive(window.at[2, 1 - c, h], tok_s.at[at + 1], tok_r.at[at + 1], twin_id)
    tok_kept.wait()
    for cp in out + sent:
        cp.wait_send()

    @pl.when(gives)
    def _():
        down_out.wait_send()


def gather(cat, down, vec, tokens):
    dma = pltpu.SemaphoreType.DMA
    return pl.pallas_call(
        gather_kernel,
        name="gather",
        out_shape=(
            jax.ShapeDtypeStruct((2, *WIDE), jnp.bfloat16),
            jax.ShapeDtypeStruct((2, *WIDE), jnp.bfloat16),
            jax.ShapeDtypeStruct((2, *TALL), jnp.bfloat16),
            jax.ShapeDtypeStruct((2, 4, 4, 4, 8, 128), jnp.float32),
            jax.ShapeDtypeStruct((3, 2, 2, TILE, 768), jnp.bfloat16),
        ),
        in_specs=[ANY_SPACE] * 4,
        out_specs=(ANY_SPACE,) * 5,
        scratch_shapes=[
            pltpu.VMEM((2, 4, 6, HALF), jnp.bfloat16),
            pltpu.VMEM((24, HALF), jnp.float32),
            pltpu.VMEM((3, 3, 8, HALF), jnp.bfloat16),
            dma((4,)), dma((4,)), dma((7,)), dma((3, 2, 8, 3)), dma((3, 2, 8, 3)), dma((6, 2, 3)), dma((6, 2, 3)),
            dma((15, 3)), dma((15, 3)),
            dma((4, 3)), dma((4, 3)), dma((11,)), dma((11,)),
        ],
        compiler_params=pltpu.CompilerParams(collective_id=1, has_side_effects=True, vmem_limit_bytes=58 << 20),
    )(cat, down, vec, tokens)


def reduce_kernel(*refs):
    (g0, g0_other, g1, g2, gv, dx, base, out0, out1, out2, out_v, out_tok) = refs[:12]
    grads = (None, g1, g2)
    refs = refs[12:]
    acc, other, refs = refs[:3], refs[3:6], refs[6:]
    lands = {}
    for n, (part, phase, k) in enumerate((a, b, k) for a in range(3) for b in range(3) for k in STREAMS):
        lands[part, phase, k] = refs[n]
    refs = refs[27:]
    (
        stage, rows, tall_f, v_c, v_x, v_y, v_z, t_acc, t_in, t_land, t_part, t_mate, t_base, t_out,
        local, core_s, core_r, near_s, near_r, send, recv, fin_s, fin_r, t_s, t_r, vec_s, vec_r, tok_s, tok_r, tok_l,
    ) = refs
    me = place()
    c, x, y, z = me["c"], me["x"], me["y"], me["z"]
    yp, q, m, zh = lax.rem(y, 2), lax.rem(z, 2), y // 2, z // 2
    twin, across, diagonal = octet_mates(me)
    twin_id = device_at(twin)
    partner, before, after = stream_mates()

    def other_q(at):
        new = dict(at)
        new["z"] = at["z"] + 1 - 2 * lax.rem(at["z"], 2)
        return new

    ring_mates = [moved(me, **{d: k}) for d in ("x", "y", "z") for k in range(1, EXTENT[d])]
    mates = [twin, across, diagonal] + [other_q(a) for a in (me, twin, across, diagonal)]
    targets = ring_mates + [twin, diagonal] + [other_q(a) for a in (twin, across, diagonal)]
    greet([device_at(a) for a in targets] + [before, after])
    sent = []

    def go(src, dst, send_sem, recv_sem, target):
        cp = sending(src, dst, send_sem, recv_sem, target)
        cp.start()
        sent.append(cp)

    def arrive(dst, send_sem, recv_sem, target):
        sending(dst, dst, send_sem, recv_sem, target).wait_recv()

    def order_of(part):
        return ORDERS[part][::-1]

    def sets_of(part, phase, index):
        sets = {"x": x, "y": y, "z": z}
        order = order_of(part)
        for later in order[phase + 1:]:
            sets[later] = None
        sets[order[phase]] = lax.rem(index + 2 * EXTENT[order[phase]], EXTENT[order[phase]])
        return sets

    def add_region(k, part, sets, sources, half=None, gone=()):
        pick, from_pick = picks_of(sets), picks_of(sets, gone)
        dims = dims_of(k)
        inner = dims[3:] if k < 2 else dims[2:]
        outer = [d for d in dims if d not in inner and pick[d] is None]
        count = 1
        for d in outer:
            count *= DIM_SIZE[d]
        cut = pl.ds(*((0, HALF) if half is None else HALVES[k][half]))

        def one(i):
            at = {}
            for d in reversed(outer):
                at[d] = lax.rem(i, DIM_SIZE[d]) if count > 1 else 0
                i = i // DIM_SIZE[d]

            def index(picked):
                return tuple(
                    (at[d] if d in at else slice(None)) if picked[d] is None else pl.ds(picked[d], 1) if d in inner else picked[d]
                    for d in dims
                )

            to = (*index(pick), part, slice(None), cut)
            fr = (*index(from_pick), slice(None), cut)
            if len(sources) == 1:
                acc[k][to] = acc[k][to] + sources[0][fr]
            else:
                total = acc[k][to].astype(jnp.float32)
                for src in sources:
                    total = total + src[fr].astype(jnp.float32)
                acc[k][to] = total.astype(jnp.bfloat16)

        if count == 1:
            one(0)
        else:
            lax.fori_loop(0, count, lambda i, carry: (one(i), carry)[1], 0)

    def hop(part, n):
        return sets_of(part, 0, me[order_of(part)[0]] + (2, 1, -1, 0)[n])

    own_copies = {}

    def cross(k, part, n):
        slot = part * 4 + n
        sets = hop(part, n)
        src = view(grads[k], k, part, sets, None, (), (1 - c,))
        go(src, view(other[k], k, part, sets), core_s.at[slot, k], core_r.at[slot, k], twin_id)
        kept = pltpu.make_async_copy(
            view(grads[k], k, part, sets, None, (), (c,)), view(acc[k], k, part, sets), local.at[slot, k]
        )
        kept.start()
        own_copies[k, part, n] = kept

    for part in range(3):
        go(g0_other.at[:, :, :, part], other[0].at[:, :, :, part], core_s.at[part, 0], core_r.at[part, 0], twin_id)
        whole = (slice(None),) * 5 + (part,)
        own_copies[0, part] = pltpu.make_async_copy(g0.at[whole], acc[0].at[whole], local.at[part, 0])
        own_copies[0, part].start()
    for n in range(4):
        for k in (1, 2):
            for part in range(3):
                cross(k, part, n)

    go(dx.at[:, 1 - c], t_in, tok_s.at[0], tok_r.at[0], twin_id)
    tok_kept = pltpu.make_async_copy(dx.at[:, c], t_acc, tok_l.at[0])
    tok_kept.start()
    base_kept = pltpu.make_async_copy(base, t_base, tok_l.at[1])
    base_kept.start()

    vec_lands = (v_c, v_x, v_y, v_z)
    vec_dims = ("c", "x", "y", "z")

    def vec_start(number):
        dim, land = vec_dims[number], vec_lands[number]
        for k in range(1, land.shape[0]):
            mine = land.at[me[dim]]
            go(mine, mine, vec_s.at[number, k], vec_r.at[number, k], device_at(moved(me, **{dim: k})))

    def vec_finish(number):
        dim, land = vec_dims[number], vec_lands[number]
        size = land.shape[0]
        for k in range(1, size):
            theirs = land.at[lax.rem(me[dim] - k + size, size)]
            arrive(theirs, vec_s.at[number, k], vec_r.at[number, k], device_at(moved(me, **{dim: k})))
        total = land[0]
        for k in range(1, size):
            total = total + land[k]
        return total

    def row_blocks(fn):
        lax.fori_loop(0, TILE // 32, lambda r, carry: (fn(pl.ds(pl.multiple_of(r * 32, 32), 32)), carry)[1], 0)

    def tok_cross():
        tok_kept.wait()
        arrive(t_in, tok_s.at[0], tok_r.at[0], twin_id)
        for n, h in enumerate((1 - q, q)):
            for r in (0, 2):
                def one(at):
                    t_acc[r, h, at] = t_acc[r, h, at] + t_in[r, h, at]
                row_blocks(one)
            go(t_acc.at[0, h], t_land.at[1, h], tok_s.at[1 + n], tok_r.at[1 + n], before)
            go(t_acc.at[2, h], t_land.at[0, h], tok_s.at[3 + n], tok_r.at[3 + n], after)

    def tok_total(h, at):
        f = jnp.float32
        return t_acc[1, h, at].astype(f) + t_in[1, h, at].astype(f) + t_land[0, h, at].astype(f) + t_land[1, h, at].astype(f)

    def tok_theirs():
        h = 1 - q
        arrive(t_land.at[1, h], tok_s.at[1], tok_r.at[1], after)
        arrive(t_land.at[0, h], tok_s.at[3], tok_r.at[3], before)

        def one(at):
            t_part[at] = tok_total(h, at).astype(jnp.bfloat16)
        row_blocks(one)
        go(t_part, t_mate, tok_s.at[5], tok_r.at[5], partner)

    def tok_mine():
        arrive(t_land.at[1, q], tok_s.at[2], tok_r.at[2], after)
        arrive(t_land.at[0, q], tok_s.at[4], tok_r.at[4], before)
        arrive(t_mate, tok_s.at[5], tok_r.at[5], partner)
        base_kept.wait()

        def one(at):
            t_out[at] = tok_total(q, at) + t_mate[at].astype(jnp.float32) + t_base[at]
        row_blocks(one)
        done = pltpu.make_async_copy(t_out, out_tok, tok_l.at[2])
        done.start()
        return done

    def meet(k, part, n):
        if k > 0:
            slot = part * 4 + n
            own_copies[k, part, n].wait()
            sets = hop(part, n)
            arrive(view(other[k], k, part, sets), core_s.at[slot, k], core_r.at[slot, k], twin_id)
            add_region(k, part, sets, [other[k].at[(slice(None),) * 5 + (part,)]])
        elif n == 0:
            own_copies[0, part].wait()
            theirs = other[0].at[:, :, :, part]
            arrive(theirs, core_s.at[part, 0], core_r.at[part, 0], twin_id)

            def one(i, carry):
                acc[0][1, 1, i, :, :, part] = acc[0][1, 1, i, :, :, part] + other[0][i, :, :, part]
                return carry

            lax.fori_loop(0, 4, one, 0)

    def ring(k, part, step, arriving):
        dim = order_of(part)[0]
        ahead = 3 - step - (1 if arriving else 0)
        for direction, sign in enumerate((1, -1)):
            half = direction if step == 1 else None
            sets = sets_of(part, 0, me[dim] + sign * ahead)
            land = lands[part, 0, k].at[direction]
            slot = part * 2 + step - 1
            sems = send.at[slot, direction, k], recv.at[slot, direction, k]
            target = device_at(moved(me, **{dim: sign}))
            here = view(land, k, None, sets, half)
            if arriving:
                arrive(here, *sems, target)
                add_region(k, part, sets, [land], half)
            else:
                go(view(acc[k], k, part, sets, half), here, *sems, target)

    def near(k, part, phase, arriving):
        order = order_of(part)
        dim, gone = order[phase], order[: phase + 1]
        mine = sets_of(part, phase, me[dim])
        sources = []
        for o in OTHERS[dim]:
            sems = near_s.at[part, phase - 1, o, k], near_r.at[part, phase - 1, o, k]
            target = device_at(moved(me, **{dim: o}))
            land = lands[part, phase, k].at[o - 1]
            here = view(land, k, None, mine, None, gone)
            if arriving:
                arrive(here, *sems, target)
                sources.append(land)
            else:
                go(view(acc[k], k, part, sets_of(part, phase, me[dim] + o)), here, *sems, target)
        if arriving:
            add_region(k, part, mine, sources, None, gone)

    pairs = [(k, part) for k in (1, 2, 0) for part in range(3)]
    for k, part in pairs:
        meet(k, part, 0)
        ring(k, part, 1, False)
    tok_cross()
    v_c[c] = gv[...]
    vec_start(0)

    def vec_next(n):
        total = vec_finish(n)
        if n < 3:
            vec_lands[n + 1][me[vec_dims[n + 1]]] = total
            vec_start(n + 1)
        else:
            out_v[...] = total

    for k, part in pairs:
        meet(k, part, 1)
        meet(k, part, 2)
        ring(k, part, 1, True)
        ring(k, part, 2, False)
    vec_next(0)
    for k, part in pairs:
        meet(k, part, 3)
    vec_next(1)
    tok_theirs()
    vec_next(2)
    for k, part in pairs:
        ring(k, part, 2, True)
        near(k, part, 1, False)
    vec_next(3)
    tok_done = tok_mine()
    for k, part in pairs:
        near(k, part, 1, True)
        near(k, part, 2, False)
    for k, part in pairs:
        near(k, part, 2, True)

    for k in range(2):
        for part in range(3):
            stage[pl.ds(8 * part, 8), :] = acc[k][yp, q, x, zh, m, part].astype(jnp.float32)
        for owner in range(4):
            rows[k, owner] = stage[pl.ds(6 * owner, 6), :]
    for part in range(3):
        tall_f[part] = acc[2][x, zh, m, yp, q, part].astype(jnp.float32)

    def cols_at(at):
        return pl.ds(pl.multiple_of((lax.rem(at["y"], 2) * 2 + lax.rem(at["z"], 2)) * 768 + at["c"] * HALF, 128), HALF)

    def owner_of(at):
        return lax.rem(at["y"], 2) * 2 + at["c"]

    for k, out in enumerate((out0, out1)):
        for n, mate in enumerate(mates):
            go(rows.at[k, owner_of(mate)], out.at[:, cols_at(me)], fin_s.at[k, n], fin_r.at[k, n], device_at(mate))
    kept = [
        pltpu.make_async_copy(rows.at[k, owner_of(me)], out.at[:, cols_at(me)], fin_s.at[k, 7])
        for k, out in enumerate((out0, out1))
    ]
    for cp in kept:
        cp.start()
    stays = c == q
    half_at = [pl.ds(pl.multiple_of(a * HALF, 128), HALF) for a in (c, 1 - c)]
    t_self = pltpu.make_async_copy(tall_f, out2.at[:, :, half_at[0]], t_s.at[0])
    there_same, there_cross = device_at(other_q(me)), device_at(other_q(twin))
    t_twin = sending(tall_f, out2.at[:, :, half_at[0]], t_s.at[0], t_r.at[0], twin_id)
    t_same = sending(tall_f, out2.at[:, :, half_at[0]], t_s.at[1], t_r.at[1], there_same)
    t_cross = sending(tall_f, out2.at[:, :, half_at[0]], t_s.at[1], t_r.at[2], there_cross)

    @pl.when(stays)
    def _():
        t_self.start()
        t_same.start()

    @pl.when(jnp.logical_not(stays))
    def _():
        t_twin.start()
        t_cross.start()

    for k, out in enumerate((out0, out1)):
        for n, mate in enumerate(mates):
            arrive(out.at[:, cols_at(mate)], fin_s.at[k, n], fin_r.at[k, n], device_at(mate))

    @pl.when(stays)
    def _():
        arrive(out2.at[:, :, half_at[1]], t_s.at[0], t_r.at[0], twin_id)
        t_self.wait()
        t_same.wait_send()

    @pl.when(jnp.logical_not(stays))
    def _():
        arrive(out2.at[:, :, half_at[0]], t_s.at[1], t_r.at[1], there_same)
        arrive(out2.at[:, :, half_at[1]], t_s.at[1], t_r.at[2], there_cross)
        t_twin.wait_send()
        t_cross.wait_send()

    for cp in kept:
        cp.wait()
    tok_done.wait()
    for cp in sent:
        cp.wait_send()


def reduce_all(g0, g0_other, g1, g2, gv, dx, base):
    bf, f32, dma = jnp.bfloat16, jnp.float32, pltpu.SemaphoreType.DMA
    lands = []
    for part in range(3):
        order = ORDERS[part][::-1]
        for phase in range(3):
            size = dict(DIM_SIZE)
            for dim, names in (("x", ("x",)), ("y", ("m", "yp")), ("z", ("zh", "q"))):
                if phase > 0 and dim in order[: phase + 1]:
                    for name in names:
                        size[name] = 1
            count = 2 if phase == 0 else EXTENT[order[phase]] - 1
            lands += [pltpu.VMEM((count, *(size[d] for d in dims_of(k)), 8, HALF), bf) for k in STREAMS]
    whole = [pltpu.VMEM(WIDE, bf), pltpu.VMEM(TALL, bf)]
    return pl.pallas_call(
        reduce_kernel,
        name="reduce_all",
        out_shape=(
            jax.ShapeDtypeStruct((6, 3072), f32),
            jax.ShapeDtypeStruct((6, 3072), f32),
            jax.ShapeDtypeStruct((3, 8, 768), f32),
            jax.ShapeDtypeStruct((16, 768), f32),
            jax.ShapeDtypeStruct((TILE, 768), f32),
        ),
        in_specs=[ANY_SPACE, ANY_SPACE, ANY_SPACE, ANY_SPACE, IN_VMEM, ANY_SPACE, ANY_SPACE],
        out_specs=(ANY_SPACE, ANY_SPACE, ANY_SPACE, IN_VMEM, ANY_SPACE),
        scratch_shapes=[
            pltpu.VMEM(WIDE, bf), *whole, pltpu.VMEM((4, 4, 2, 3, 8, HALF), bf), *whole, *lands,
            pltpu.VMEM((24, HALF), f32),
            pltpu.VMEM((2, 4, 6, HALF), f32),
            pltpu.VMEM((3, 8, HALF), f32),
            pltpu.VMEM((2, 16, 768), f32),
            pltpu.VMEM((4, 16, 768), f32),
            pltpu.VMEM((4, 16, 768), f32),
            pltpu.VMEM((8, 16, 768), f32),
            pltpu.VMEM((3, 2, TILE, 768), bf),
            pltpu.VMEM((3, 2, TILE, 768), bf),
            pltpu.VMEM((2, 2, TILE, 768), bf),
            pltpu.VMEM((TILE, 768), bf),
            pltpu.VMEM((TILE, 768), bf),
            pltpu.VMEM((TILE, 768), f32),
            pltpu.VMEM((TILE, 768), f32),
            dma((12, 3)), dma((12, 3)), dma((12, 3)), dma((3, 2, 8, 3)), dma((3, 2, 8, 3)), dma((6, 2, 3)), dma((6, 2, 3)),
            dma((2, 8)), dma((2, 7)),
            dma((2,)), dma((3,)), dma((4, 8)), dma((4, 8)), dma((6,)), dma((6,)), dma((3,)),
        ],
        compiler_params=pltpu.CompilerParams(collective_id=2, has_side_effects=True, vmem_limit_bytes=60 << 20),
    )(g0, g0_other, g1, g2, gv, dx, base)


def to_tokens_kernel(heads, rows, send, recv, local):
    me = place()
    c = me["c"]
    twin = device_at(moved(me, c=1))
    mine, other = (pl.ds(pl.multiple_of(a * HALF, 128), HALF) for a in (c, 1 - c))
    greet((twin,))
    out = sending(heads.at[1 - c], rows.at[:, mine], send.at[0], recv.at[0], twin)
    out.start()
    kept = pltpu.make_async_copy(heads.at[c], rows.at[:, mine], local.at[0])
    kept.start()
    kept.wait()
    sending(heads.at[c], rows.at[:, other], send.at[0], recv.at[0], twin).wait_recv()
    out.wait_send()


def to_heads_kernel(rows, heads, send, recv, local):
    me = place()
    c = me["c"]
    twin = device_at(moved(me, c=1))
    mine, other = (pl.ds(pl.multiple_of(a * HALF, 128), HALF) for a in (c, 1 - c))
    greet((twin,))
    out = sending(rows.at[:, other], heads.at[c], send.at[0], recv.at[0], twin)
    out.start()
    kept = pltpu.make_async_copy(rows.at[:, mine], heads.at[c], local.at[0])
    kept.start()
    kept.wait()
    sending(rows.at[:, mine], heads.at[1 - c], send.at[0], recv.at[0], twin).wait_recv()
    out.wait_send()


def swap(kernel, name, shape, number, array):
    return pl.pallas_call(
        kernel,
        name=name,
        out_shape=jax.ShapeDtypeStruct(shape, array.dtype),
        in_specs=[ANY_SPACE],
        out_specs=IN_VMEM,
        scratch_shapes=[pltpu.SemaphoreType.DMA((1,))] * 3,
        compiler_params=pltpu.CompilerParams(collective_id=number, has_side_effects=True, vmem_limit_bytes=58 << 20),
    )(array)


def dot32(a, b):
    return jnp.dot(a, b, preferred_element_type=jnp.float32)


def lanes_low(rows):
    return lax.broadcasted_iota(jnp.int32, (rows, 128), 1) < HEAD_DIM


def across_lanes(a, b):
    return lax.dot_general(a, b, (((1,), (1,)), ((), ())), preferred_element_type=jnp.float32)


def flipped(a):
    return jnp.swapaxes(a, 0, 1)


def project_kernel(plan, x_ref, w_ref, bq_ref, bv_ref, q_ref, kv_ref):
    t = pl.program_id(0)
    x = x_ref[0]
    for i in range(2):
        @pl.when(t == plan[1 + i])
        def _():
            q_ref[i] = (dot32(x, w_ref[0, 0]) + bq_ref[0]).astype(jnp.bfloat16)

    @pl.when(jnp.logical_and(t >= plan[7], t < plan[8]))
    def _():
        kv_ref[0, 0] = dot32(x, w_ref[0, 1]).astype(jnp.bfloat16)
        kv_ref[1, 0] = (dot32(x, w_ref[0, 2]) + bv_ref[0]).astype(jnp.bfloat16)


def project(plan, window, first, bias_q, bias_v):
    half = pl.BlockSpec((1, 1, HALF), lambda t, p: (p[0], 0, 0))
    return pl.pallas_call(
        project_kernel,
        name="project",
        grid_spec=pltpu.PrefetchScalarGridSpec(
            num_scalar_prefetch=1,
            grid=(12,),
            in_specs=[
                pl.BlockSpec((1, TILE, 768), lambda t, p: (t, 0, 0)),
                pl.BlockSpec((1, 4, 768, HALF), lambda t, p: (p[0], 0, 0, 0)),
                half, half,
            ],
            out_specs=[
                pl.BlockSpec((2, TILE, HALF), lambda t, p: (0, 0, 0)),
                pl.BlockSpec((2, 1, TILE, HALF), lambda t, p: (0, t, 0, 0)),
            ],
        ),
        out_shape=(
            jax.ShapeDtypeStruct((2, TILE, HALF), jnp.bfloat16),
            jax.ShapeDtypeStruct((2, 12, TILE, HALF), jnp.bfloat16),
        ),
        compiler_params=pltpu.CompilerParams(vmem_limit_bytes=58 << 20),
    )(plan, window, first, bias_q, bias_v)


def attend_kernel(plan, q_docs, k_docs, q_ref, kv, o_ref, lse_ref, top, total, acc):
    i = pl.program_id(1)
    low = lanes_low(TILE)
    q = q_ref[0]
    none = jnp.zeros_like(q)
    q_heads = (jnp.where(low, q, none), jnp.where(low, none, q))
    docs = q_docs[0]
    top[...] = jnp.full_like(top, BOTTOM)
    total[...] = jnp.zeros_like(total)
    acc[...] = jnp.zeros_like(acc)
    scale = HEAD_DIM ** -0.5 * LOG2E

    def step(j, carry):
        k, v = kv[0, j], flipped(kv[1, j])
        same = docs == k_docs[j]
        for head in range(2):
            rows = slice(head * HEAD_DIM, (head + 1) * HEAD_DIM)
            s = jnp.where(same, across_lanes(k, q_heads[head]) * scale, BOTTOM)
            old = top[head]
            new = jnp.maximum(old, jnp.max(s, axis=0, keepdims=True))
            fade = jnp.exp2(old - new)
            p = jnp.exp2(s - new)
            total[head] = total[head] * fade + jnp.sum(p, axis=0, keepdims=True)
            top[head] = new
            acc[rows] = acc[rows] * fade + dot32(v[rows], p.astype(jnp.bfloat16))
        return carry

    lax.fori_loop(plan[3 + 2 * i], plan[4 + 2 * i], step, 0)
    for head in range(2):
        rows = slice(head * HEAD_DIM, (head + 1) * HEAD_DIM)
        acc[rows] = acc[rows] / total[head]
        lse_ref[0, 0, pl.ds(head, 1)] = top[head] + jnp.log2(total[head])
    o_ref[0] = flipped(acc[...]).astype(jnp.bfloat16)


OWN_PAIR = pl.BlockSpec((1, TILE, 128), lambda p, i, b: (i, 0, p))
WINDOW_PAIR = pl.BlockSpec((2, 12, TILE, 128), lambda p, i, b: (0, 0, 0, p))
STATS = pl.BlockSpec((1, 1, 2, TILE), lambda p, i, b: (p, i, 0, 0))
DOC_SPECS = [
    pl.BlockSpec((1, 1, TILE), lambda p, i, b: (i, 0, 0)),
    pl.BlockSpec((12, TILE, 1), lambda p, i, b: (0, 0, 0)),
]


def attend(plan, q_docs, k_docs, q_heads, kv):
    return pl.pallas_call(
        attend_kernel,
        name="attend",
        grid_spec=pltpu.PrefetchScalarGridSpec(
            num_scalar_prefetch=1,
            grid=(3, 2),
            in_specs=[*DOC_SPECS, OWN_PAIR, WINDOW_PAIR],
            out_specs=[OWN_PAIR, STATS],
            scratch_shapes=[
                pltpu.VMEM((2, 1, TILE), jnp.float32),
                pltpu.VMEM((2, 1, TILE), jnp.float32),
                pltpu.VMEM((128, TILE), jnp.float32),
            ],
        ),
        out_shape=(
            jax.ShapeDtypeStruct((2, TILE, HALF), jnp.bfloat16),
            jax.ShapeDtypeStruct((3, 2, 2, TILE), jnp.float32),
        ),
        compiler_params=pltpu.CompilerParams(vmem_limit_bytes=58 << 20),
    )(plan, q_docs, k_docs, q_heads, kv)


def attend_back_kernel(plan, q_docs, k_docs, q_ref, do_ref, o_ref, lse_ref, kv, dq_ref, dkv_ref, dkv, dq):
    i = pl.program_id(1)
    low = lanes_low(TILE)

    @pl.when(i == 0)
    def _():
        dkv[...] = jnp.zeros_like(dkv)

    q, d_out = q_ref[0], do_ref[0]
    none = jnp.zeros_like(q)
    q_heads = (jnp.where(low, q, none), jnp.where(low, none, q))
    do_heads = (jnp.where(low, d_out, none), jnp.where(low, none, d_out))
    prod = d_out.astype(jnp.float32) * o_ref[0].astype(jnp.float32)
    first = lax.broadcasted_iota(jnp.int32, (8, 128), 0)
    halves = lax.broadcasted_iota(jnp.int32, (8, 128), 1) // HEAD_DIM
    deltas = lax.dot_general(
        (first == halves).astype(jnp.float32), prod, (((1,), (1,)), ((), ())),
        precision=lax.Precision.HIGHEST, preferred_element_type=jnp.float32,
    )
    deltas = (deltas[0:1], deltas[1:2])
    lses = (lse_ref[0, 0, 0:1], lse_ref[0, 0, 1:2])
    docs = q_docs[0]
    dq[...] = jnp.zeros_like(dq)
    scale = HEAD_DIM ** -0.5 * LOG2E

    def step(j, carry):
        k, v = kv[0, j], kv[1, j]
        k_flip = flipped(k)
        same = docs == k_docs[j]
        dk, dv = [], []
        for head in range(2):
            rows = slice(head * HEAD_DIM, (head + 1) * HEAD_DIM)
            s = across_lanes(k, q_heads[head]) * scale
            p = jnp.where(same, jnp.exp2(s - lses[head]), 0.0)
            dp = across_lanes(v, do_heads[head])
            ds = (p * (dp - deltas[head])).astype(jnp.bfloat16)
            dq[rows] += dot32(k_flip[rows], ds)
            dk.append(dot32(ds, q_heads[head]))
            dv.append(dot32(p.astype(jnp.bfloat16), do_heads[head]))
        dkv[0, j] += dk[0] + dk[1]
        dkv[1, j] += dv[0] + dv[1]
        return carry

    lax.fori_loop(plan[3 + 2 * i], plan[4 + 2 * i], step, 0)
    dq_ref[0] = flipped(dq[...] * HEAD_DIM ** -0.5).astype(jnp.bfloat16)

    @pl.when(i == 1)
    def _():
        dkv_ref[0] = (dkv[0] * HEAD_DIM ** -0.5).astype(jnp.bfloat16)
        dkv_ref[1] = dkv[1].astype(jnp.bfloat16)


def attend_back(plan, q_docs, k_docs, q_heads, d_heads, o_heads, lse, kv):
    return pl.pallas_call(
        attend_back_kernel,
        name="attend_back",
        grid_spec=pltpu.PrefetchScalarGridSpec(
            num_scalar_prefetch=1,
            grid=(3, 2),
            in_specs=[*DOC_SPECS, OWN_PAIR, OWN_PAIR, OWN_PAIR, STATS, WINDOW_PAIR],
            out_specs=[OWN_PAIR, WINDOW_PAIR],
            scratch_shapes=[
                pltpu.VMEM((2, 12, TILE, 128), jnp.float32),
                pltpu.VMEM((128, TILE), jnp.float32),
            ],
        ),
        out_shape=(
            jax.ShapeDtypeStruct((2, TILE, HALF), jnp.bfloat16),
            jax.ShapeDtypeStruct((2, 12, TILE, HALF), jnp.bfloat16),
        ),
        compiler_params=pltpu.CompilerParams(vmem_limit_bytes=58 << 20),
    )(plan, q_docs, k_docs, q_heads, d_heads, o_heads, lse, kv)


def project_back_kernel(plan, x_ref, w_ref, dq_ref, dkv_ref, dw_ref, dx_ref, sums_ref, dw, sums):
    t = pl.program_id(0)

    @pl.when(t == 0)
    def _():
        dw[...] = jnp.zeros_like(dw)
        sums[...] = jnp.zeros_like(sums)

    used = jnp.logical_and(t >= plan[7], t < plan[8])

    @pl.when(used)
    def _():
        x_flip = flipped(x_ref[0])
        dk, dv = dkv_ref[0, 0], dkv_ref[1, 0]
        dw[1] += dot32(x_flip, dk)
        dw[2] += dot32(x_flip, dv)
        sums[1:2] += jnp.sum(dv.astype(jnp.float32), axis=0, keepdims=True)
        dx = across_lanes(dk, w_ref[0, 1]) + across_lanes(dv, w_ref[0, 2])
        dx_ref[0] = dx.astype(jnp.bfloat16)
        for i in range(2):
            @pl.when(t == plan[1 + i])
            def _():
                dq = dq_ref[i]
                dw[0] += dot32(x_flip, dq)
                sums[0:1] += jnp.sum(dq.astype(jnp.float32), axis=0, keepdims=True)
                dx_ref[0] = (dx + across_lanes(dq, w_ref[0, 0])).astype(jnp.bfloat16)

    @pl.when(jnp.logical_not(used))
    def _():
        dx_ref[...] = jnp.zeros_like(dx_ref)

    @pl.when(t == 11)
    def _():
        dw_ref[...] = dw[...].astype(jnp.bfloat16)
        sums_ref[...] = sums[...]


def project_back(plan, window, first, dq, dkv):
    return pl.pallas_call(
        project_back_kernel,
        name="project_back",
        grid_spec=pltpu.PrefetchScalarGridSpec(
            num_scalar_prefetch=1,
            grid=(12,),
            in_specs=[
                pl.BlockSpec((1, TILE, 768), lambda t, p: (t, 0, 0)),
                pl.BlockSpec((1, 4, 768, HALF), lambda t, p: (p[0], 0, 0, 0)),
                pl.BlockSpec((2, TILE, HALF), lambda t, p: (0, 0, 0)),
                pl.BlockSpec((2, 1, TILE, HALF), lambda t, p: (0, t, 0, 0)),
            ],
            out_specs=[
                pl.BlockSpec((3, 768, HALF), lambda t, p: (0, 0, 0)),
                pl.BlockSpec((1, TILE, 768), lambda t, p: (t, 0, 0)),
                pl.BlockSpec((8, HALF), lambda t, p: (0, 0)),
            ],
            scratch_shapes=[pltpu.VMEM((3, 768, HALF), jnp.float32), pltpu.VMEM((8, HALF), jnp.float32)],
        ),
        out_shape=(
            jax.ShapeDtypeStruct((3, 768, HALF), jnp.bfloat16),
            jax.ShapeDtypeStruct((12, TILE, 768), jnp.bfloat16),
            jax.ShapeDtypeStruct((8, HALF), jnp.float32),
        ),
        compiler_params=pltpu.CompilerParams(vmem_limit_bytes=58 << 20),
    )(plan, window, first, dq, dkv)


def norm_parts(resid):
    centred = resid - jnp.mean(resid, axis=1, keepdims=True)
    inverse = lax.rsqrt(jnp.mean(centred * centred, axis=1, keepdims=True) + NORM_EPS)
    return centred * inverse, inverse


def norm_back(upstream, gain, n, inverse):
    e = upstream * gain
    return inverse * (e - jnp.mean(e, axis=1, keepdims=True) - n * jnp.mean(e * n, axis=1, keepdims=True))


def row_sum(a):
    return jnp.sum(a, axis=0, keepdims=True)


def mlp_kernel(
    att_ref, tok_ref, cot_ref, rows, bias_in, first, second, third,
    out_ref, d_one_ref, d_att_ref, dwo_ref, dw_in_ref, dw_down_ref, sums_ref, sums_in_ref,
    w_out, w_in, w_down, n_one, low, low_flip, slope, active, wide, sem,
):
    f32, bf = jnp.float32, jnp.bfloat16
    loads = [pltpu.make_async_copy(first.at[:, 3], w_out, sem.at[0])]
    loads += [pltpu.make_async_copy(second, w_in, sem.at[1]), pltpu.make_async_copy(third, w_down, sem.at[2])]
    for cp in loads:
        cp.start()

    def row(n):
        return rows[n : n + 1]

    halves = (slice(0, HALF), slice(HALF, 768))
    loads[0].wait()
    att = att_ref[...]
    for h in range(2):
        wide[:, halves[h]] = dot32(att, w_out[h])
    one, inverse_one = norm_parts(tok_ref[...].astype(f32) + (wide[...] + row(2)))
    n_one[...] = one
    normed = one * row(3) + row(4)
    low[...] = normed.astype(bf)
    low_flip[...] = flipped(low[...])
    wide[...] = normed + row(5)
    loads[1].wait()
    loads[2].wait()

    def up(m, carry):
        h = dot32(low[...], w_in[lax.rem(m, 2), m // 2]) + bias_in[m]
        cdf = 0.5 * (1.0 + lax.erf(h * 0.7071067811865476))
        slope[m] = cdf + h * jnp.exp(h * h * -0.5) * 0.3989422804014327
        a = (h * cdf).astype(bf)
        active[m] = flipped(a)
        for k in range(2):
            wide[:, halves[k]] += dot32(a, w_down[k, m])
        return carry

    lax.fori_loop(0, 8, up, 0)
    two, inverse_two = norm_parts(wide[...])
    out_ref[...] = (two * row(6) + row(7)).astype(bf)
    upstream = cot_ref[...].astype(f32)
    sums_ref[0:2] = jnp.zeros((2, 768), f32)
    sums_ref[6:7] = row_sum(upstream * two)
    sums_ref[7:8] = row_sum(upstream)
    d_two = norm_back(upstream, row(6), two, inverse_two)
    sums_ref[5:6] = row_sum(d_two)
    d_low = d_two.astype(bf)
    wide[...] = d_two

    def down(m, carry):
        d_active = None
        for k in range(2):
            d_half = d_low[:, halves[k]]
            dw_down_ref[k, m] = dot32(active[m], d_half).astype(bf)
            part = across_lanes(d_half, w_down[k, m])
            d_active = part if d_active is None else d_active + part
        d_hidden = (d_active * slope[m]).astype(bf)
        sums_in_ref[m] = row_sum(d_hidden.astype(f32))
        dw_in_ref[lax.rem(m, 2), m // 2] = dot32(low_flip[...], d_hidden).astype(bf)
        wide[...] += across_lanes(d_hidden, w_in[lax.rem(m, 2), m // 2])
        return carry

    lax.fori_loop(0, 8, down, 0)
    d_normed = wide[...]
    one = n_one[...]
    sums_ref[3:4] = row_sum(d_normed * one)
    sums_ref[4:5] = row_sum(d_normed)
    d_one = norm_back(d_normed, row(3), one, inverse_one)
    d_one_ref[...] = d_one
    sums_ref[2:3] = row_sum(d_one)
    d_low = d_one.astype(bf)
    att_flip = flipped(att_ref[...])
    d_att = None
    for h in range(2):
        d_half = d_low[:, halves[h]]
        dwo_ref[h] = dot32(att_flip, d_half).astype(bf)
        part = across_lanes(d_half, w_out[h])
        d_att = part if d_att is None else d_att + part
    d_att_ref[...] = d_att.astype(bf)


def mlp(att, tokens, cotangent, rows, bias_in, first, second, third):
    f32, bf = jnp.float32, jnp.bfloat16
    return pl.pallas_call(
        mlp_kernel,
        name="mlp",
        in_specs=[IN_VMEM] * 5 + [ANY_SPACE] * 3,
        out_specs=(IN_VMEM,) * 8,
        out_shape=(
            jax.ShapeDtypeStruct((TILE, 768), bf),
            jax.ShapeDtypeStruct((TILE, 768), f32),
            jax.ShapeDtypeStruct((TILE, 768), bf),
            jax.ShapeDtypeStruct((2, 768, HALF), bf),
            jax.ShapeDtypeStruct((2, 4, 768, HALF), bf),
            jax.ShapeDtypeStruct((2, 8, HALF, HALF), bf),
            jax.ShapeDtypeStruct((8, 768), f32),
            jax.ShapeDtypeStruct((8, 1, HALF), f32),
        ),
        scratch_shapes=[
            pltpu.VMEM((2, 768, HALF), bf),
            pltpu.VMEM((2, 4, 768, HALF), bf),
            pltpu.VMEM((2, 8, HALF, HALF), bf),
            pltpu.VMEM((TILE, 768), f32),
            pltpu.VMEM((TILE, 768), bf),
            pltpu.VMEM((768, TILE), bf),
            pltpu.VMEM((8, TILE, HALF), f32),
            pltpu.VMEM((8, HALF, TILE), bf),
            pltpu.VMEM((TILE, 768), f32),
            pltpu.SemaphoreType.DMA((3,)),
        ],
        compiler_params=pltpu.CompilerParams(vmem_limit_bytes=58 << 20),
    )(att, tokens, cotangent, rows, bias_in, first, second, third)


def body(
    tokens, w_qkv, bias_q, bias_v, w_out, bias_out, gain_one, shift_one, w_in, bias_in,
    w_down, bias_down, gain_two, shift_two, doc_lengths, cotangent,
):
    shard, seq = lax.axis_index("shard"), lax.axis_index("seq")
    core = lax.rem(shard, 2)
    f32, bf = jnp.float32, jnp.bfloat16
    width = tokens.shape[1]
    stream_len = tokens.shape[0] * lax.axis_size("seq") * lax.axis_size("shard")

    positions = (shard // 2 - 1) * (4 * TILE) + jnp.arange(12 * TILE, dtype=jnp.int32)
    starts = jnp.cumsum(doc_lengths, dtype=jnp.int32) - doc_lengths
    counted = jnp.sum((positions[:, None] >= starts[None, :]).astype(jnp.int32), axis=1, dtype=jnp.int32) - 1
    docs = jnp.where(positions < stream_len, counted, stream_len).reshape(12, TILE)
    query_docs = lax.dynamic_slice(docs, (4 + seq, 0), (3, TILE))[::2]
    lower = jnp.sum((docs[None, :, -1] < query_docs[:, :1]).astype(jnp.int32), axis=1)
    upper = jnp.sum((docs[None, :, 0] <= query_docs[:, -1:]).astype(jnp.int32), axis=1)
    plan = jnp.stack([core, 4 + seq, 6 + seq, lower[0], upper[0], lower[1], upper[1], lower[0], upper[1]])
    query_docs, key_docs = query_docs.reshape(2, 1, TILE), docs.reshape(12, TILE, 1)

    vectors = (bias_q, bias_v, bias_out, gain_one, shift_one, bias_down, gain_two, shift_two)
    vec = jnp.concatenate(
        [
            jnp.stack(vectors).astype(f32),
            jnp.pad(bias_in.astype(f32).reshape(1, 24), ((0, 7), (0, 0))),
            jnp.zeros((8, 98), f32),
        ],
        axis=1,
    )
    cat = jnp.stack([jnp.concatenate([w_qkv, w_out], axis=1), w_in])
    first, second, third, vecs, window = gather(cat, w_down.reshape(3, 8, width), vec, tokens)
    first = first.reshape(2, 4, width, HALF)
    second = second.reshape(2, 4, width, HALF)
    third = third.reshape(2, 8, HALF, HALF)
    window = window.reshape(12, TILE, width)
    vecs = jnp.transpose(vecs, (4, 1, 2, 3, 0, 5)).reshape(8, 128, 128)
    rows = vecs[:, :, :6].reshape(8, width)
    hidden_bias = vecs[0, :, 6:30].reshape(8, 1, HALF)

    q_heads, kv = project(plan, window, first, rows[0].reshape(2, 1, HALF), rows[1].reshape(2, 1, HALF))
    o_heads, lse = attend(plan, query_docs, key_docs, q_heads, kv)
    attended = swap(to_tokens_kernel, "to_tokens", (TILE, width), 4, o_heads)
    layer_out, d_one, d_att, dw_out, dw_in, dw_down, sums, sums_in = mlp(
        attended, tokens, cotangent, rows, hidden_bias, first, second, third
    )
    d_heads = swap(to_heads_kernel, "to_heads", (2, TILE, HALF), 5, d_att)
    dq, dkv = attend_back(plan, query_docs, key_docs, q_heads, d_heads, o_heads, lse, kv)
    dw_qkv, dx, head_sums = project_back(plan, window, first, dq, dkv)

    mine = jnp.arange(2) == core
    dw_out_mine = lax.dynamic_index_in_dim(dw_out, core, 0)
    dw_out_other = lax.dynamic_index_in_dim(dw_out, 1 - core, 0, keepdims=False)
    grad_first = jnp.concatenate([dw_qkv, dw_out_mine], axis=0)
    both = jnp.where(mine[None, :, None], head_sums[:2, None], 0.0).reshape(2, width)
    vec_sums = jnp.concatenate([both, sums[2:], sums_in.reshape(4, width), jnp.zeros((4, width), f32)], axis=0)
    sum_first, sum_in, sum_down, sum_vec, grad_tokens = reduce_all(
        grad_first.reshape(WIDE), dw_out_other.reshape(4, 4, 2, 3, 8, HALF), dw_in.reshape(2, *WIDE), dw_down.reshape(2, *TALL), vec_sums,
        dx.reshape(3, 2, 2, TILE, width), d_one,
    )
    own = lax.dynamic_slice(sum_vec, (0, 6 * shard), (8, 6))
    own_in = lax.dynamic_slice(sum_vec[8:12].reshape(-1), (24 * shard,), (24,))
    return (
        layer_out, grad_tokens, sum_first[:, : 3 * width], own[0], own[1], sum_first[:, 3 * width :],
        own[2], own[3], own[4], sum_in, own_in, sum_down.reshape(24, width), own[5], own[6], own[7],
    )


def solution(mesh):
    both, own = P(("shard", "seq"), None), P("shard")
    rows = P("shard", None)
    return jax.shard_map(
        body,
        mesh=mesh,
        in_specs=(both, rows, own, own, rows, own, own, own, rows, own, rows, own, own, own, P(), both),
        out_specs=(both, both, rows, own, own, rows, own, own, own, rows, own, rows, own, own, own),
        check_vma=False,
    )
```

```python
import functools
import jax
import jax.numpy as jnp
from jax import lax
from jax.experimental import pallas as pl
from jax.experimental.pallas import tpu as pltpu
from jax.sharding import PartitionSpec as P

HEAD_DIM = 64
NORM_EPS = 1e-12
MESH = pl.DeviceIdType.MESH
ANY_SPACE = pl.BlockSpec(memory_space=pl.ANY)
IN_VMEM = pl.BlockSpec(memory_space=pltpu.VMEM)
LOG2E = 1.4426950408889634
TILE = 256
HALF = 384
BOTTOM = -1e30
EXTENT = {"x": 4, "y": 4, "z": 8}
ORDERS = (("z", "y", "x"), ("z", "y", "x"), ("z", "x", "y"))
OTHERS = {dim: range(1, size) for dim, size in EXTENT.items()}
HALVES = (((0, 256), (256, 128)), ((0, 128), (128, 256)), ((0, 256), (256, 128)))
STREAMS = (0, 1, 2)
WIDE = (2, 2, 4, 4, 2, 3, 8, HALF)
TALL = (4, 4, 2, 2, 2, 3, 8, HALF)


def place():
    s = lax.axis_index("shard")
    q = lax.axis_index("seq")
    return {
        "c": lax.rem(s, 2),
        "y": lax.rem(s // 2, 4),
        "x": s // 32,
        "z": lax.rem(s // 8, 4) * 2 + q,
    }


def device_at(at):
    return {
        "shard": ((at["x"] * 4 + at["z"] // 2) * 4 + at["y"]) * 2 + at["c"],
        "seq": lax.rem(at["z"], 2),
    }


def moved(at, **steps):
    new = dict(at)
    for dim, step in steps.items():
        size = 2 if dim == "c" else EXTENT[dim]
        new[dim] = lax.rem(at[dim] + step + size, size)
    return new


def stream_mates():
    s = lax.axis_index("shard")
    q = lax.axis_index("seq")
    partner = {"shard": s, "seq": 1 - q}
    after = {"shard": lax.rem(s + 2, 128), "seq": q}
    before = {"shard": lax.rem(s + 126, 128), "seq": q}
    return partner, before, after


def greet(targets):
    barrier = pltpu.get_barrier_semaphore()
    for target in targets:
        pl.semaphore_signal(barrier, inc=1, device_id=target, device_id_type=MESH)
    pl.semaphore_wait(barrier, len(targets))


def sending(src, dst, send, recv, target):
    return pltpu.make_async_remote_copy(
        src_ref=src, dst_ref=dst, send_sem=send, recv_sem=recv, device_id=target, device_id_type=MESH
    )


def neighbours(at):
    return [moved(at, **{d: step}) for d in ("x", "y", "z") for step in (1, -1)]


def octet_mates(me):
    across = dict(me)
    across["y"] = me["y"] + 1 - 2 * lax.rem(me["y"], 2)
    twin = moved(me, c=1)
    diagonal = dict(across)
    diagonal["c"] = twin["c"]
    return twin, across, diagonal


def span(index):
    return slice(None) if index is None else pl.ds(index, 1)


def picks_of(sets, gone=()):
    x, y, z = sets["x"], sets["y"], sets["z"]
    pick = {
        "x": x,
        "m": None if y is None else y // 2,
        "yp": None if y is None else lax.rem(y, 2),
        "zh": None if z is None else z // 2,
        "q": None if z is None else lax.rem(z, 2),
    }
    names = {"x": ("x",), "y": ("m", "yp"), "z": ("zh", "q")}
    for dim in gone:
        for name in names[dim]:
            pick[name] = 0
    return pick


WIDE_DIMS = ("yp", "q", "x", "zh", "m")
TALL_DIMS = ("x", "zh", "m", "yp", "q")
DIM_SIZE = {"yp": 2, "q": 2, "x": 4, "zh": 4, "m": 2}


def dims_of(k):
    return TALL_DIMS if k == 2 else WIDE_DIMS


def view(ref, k, part, sets, half=None, gone=(), lead=()):
    pick = picks_of(sets, gone)
    cut = (0, HALF) if half is None else HALVES[k][half]
    at = tuple(span(pick[d]) for d in dims_of(k))
    rows = () if part is None else (part,)
    return ref.at[(*lead, *at, *rows, slice(None), pl.ds(*cut))]


def gather_kernel(
    cat_ref, down_ref, vec_ref, tok_ref, first, second, third, vecs, window,
    land, stage, own, oct_s, oct_r, local, near_s, near_r, send, recv, core_s, core_r, vec_s, vec_r, tok_s, tok_r,
):
    me = place()
    c, x, y, z = me["c"], me["x"], me["y"], me["z"]
    yp, q, m, zh = lax.rem(y, 2), lax.rem(z, 2), y // 2, z // 2
    outs = (first, second, third)
    twin, across, diagonal = octet_mates(me)
    twin_id = device_at(twin)
    partner, before, after = stream_mates()
    lines = [moved(me, **{d: o}) for d in EXTENT for o in OTHERS[d]]
    greet([device_at(a) for a in lines + [twin, diagonal]] + [before, after])

    def chunk_of(at):
        cols = (lax.rem(at["y"], 2) * 2 + q) * 768 + at["c"] * HALF
        return cat_ref.at[:, :, pl.ds(pl.multiple_of(cols, 128), HALF)]

    index = yp * 2 + c
    mates = (twin, across, diagonal)
    out = [
        sending(chunk_of(mate), land.at[:, index], oct_s.at[k], oct_r.at[k], device_at(mate))
        for k, mate in enumerate(mates)
    ]
    for cp in out:
        cp.start()
    kept = pltpu.make_async_copy(chunk_of(me), land.at[:, index], local.at[0])
    kept.start()
    gives = q == c
    down_out = sending(
        down_ref.at[:, :, pl.ds(pl.multiple_of((1 - c) * HALF, 128), HALF)], own.at[2], oct_s.at[3], oct_r.at[3], twin_id
    )
    down_kept = pltpu.make_async_copy(
        down_ref.at[:, :, pl.ds(pl.multiple_of(c * HALF, 128), HALF)], own.at[2], local.at[1]
    )

    @pl.when(gives)
    def _():
        down_out.start()
        down_kept.start()

    vec_kept = pltpu.make_async_copy(vec_ref, vecs.at[c, x, zh, y], local.at[2])
    vec_kept.start()

    sent = []

    def go(src, dst, send_sem, recv_sem, target):
        cp = sending(src, dst, send_sem, recv_sem, target)
        cp.start()
        sent.append(cp)

    def arrive(dst, send_sem, recv_sem, target):
        sending(dst, dst, send_sem, recv_sem, target).wait_recv()

    def tok_go(src, dst, at, target):
        go(src, dst, tok_s.at[at], tok_r.at[at], target)

    tok_kept = pltpu.make_async_copy(tok_ref, window.at[1, c, q], local.at[3])

    def tok_start():
        tok_kept.start()
        tok_go(tok_ref, window.at[1, c, q], 0, partner)
        tok_go(tok_ref, window.at[0, c, q], 1, after)
        tok_go(tok_ref, window.at[2, c, q], 2, before)
        tok_go(tok_ref, window.at[1, c, q], 3, twin_id)

    def tok_forward():
        theirs = window.at[1, c, 1 - q]
        arrive(theirs, tok_s.at[0], tok_r.at[0], partner)
        tok_go(theirs, window.at[0, c, 1 - q], 4, after)
        tok_go(theirs, window.at[2, c, 1 - q], 5, before)
        tok_go(theirs, window.at[1, c, 1 - q], 6, twin_id)

    def tok_share(h, first_slot, at):
        arrive(window.at[0, c, h], tok_s.at[first_slot], tok_r.at[first_slot], before)
        arrive(window.at[2, c, h], tok_s.at[first_slot + 1], tok_r.at[first_slot + 1], after)
        tok_go(window.at[0, c, h], window.at[0, c, h], at, twin_id)
        tok_go(window.at[2, c, h], window.at[2, c, h], at + 1, twin_id)

    vec_rounds = (("x", (1, 2, 3)), ("y", (1, 2, 3)), ("z", (2, 4, 6)), ("c", (1,)))

    def vec_copies(number, arriving):
        dim, steps = vec_rounds[number]
        done = [d for d, _ in vec_rounds[:number]]
        copies = []
        for k, step in enumerate(steps):
            source = moved(me, **{dim: (1 if dim == "c" else -step)}) if arriving else me
            pick = [None if d in done else (source["z"] // 2 if d == "z" else source[d]) for d in ("c", "x", "z", "y")]
            ref = vecs.at[tuple(span(p) for p in pick)]
            copies.append(
                sending(ref, ref, vec_s.at[number, k], vec_r.at[number, k], device_at(moved(me, **{dim: step})))
            )
        return copies

    def vec_start(number):
        for cp in vec_copies(number, False):
            cp.start()
            sent.append(cp)

    def vec_wait(number):
        for cp in vec_copies(number, True):
            cp.wait_recv()

    kept.wait()
    for k, mate in enumerate(mates):
        mate_index = lax.rem(mate["y"], 2) * 2 + mate["c"]
        arrive(land.at[:, mate_index], oct_s.at[k], oct_r.at[k], device_at(mate))
    for k in range(2):
        for owner in range(4):
            stage[pl.ds(6 * owner, 6), :] = land[k, owner].astype(jnp.float32)
        for part in range(3):
            own[k, part] = stage[pl.ds(8 * part, 8), :].astype(jnp.bfloat16)

    @pl.when(gives)
    def _():
        down_kept.wait()

    @pl.when(jnp.logical_not(gives))
    def _():
        down_out.wait_recv()

    homes = (first.at[c, yp, q, x, zh, m], second.at[c, yp, q, x, zh, m], third.at[c, x, zh, m, yp, q])
    flush = [pltpu.make_async_copy(own.at[k], homes[k], local.at[4 + k]) for k in STREAMS]
    for cp in flush:
        cp.start()
    twins = []

    def share(k, part, sets, half, slot):
        mine = view(outs[k], k, part, sets, half, (), (c,))
        theirs = view(outs[k], k, part, sets, half, (), (1 - c,))
        go(mine, mine, core_s.at[slot, k], core_r.at[slot, k], twin_id)
        twins.append((theirs, core_s.at[slot, k], core_r.at[slot, k]))

    def sets_at(part, phase, index):
        sets = {"x": x, "y": y, "z": z}
        for earlier in ORDERS[part][:phase]:
            sets[earlier] = None
        dim = ORDERS[part][phase]
        sets[dim] = lax.rem(index + EXTENT[dim], EXTENT[dim])
        return sets

    def near(k, part, phase, arriving):
        dim = ORDERS[part][phase]
        for o in OTHERS[dim]:
            sems = near_s.at[part, phase, o, k], near_r.at[part, phase, o, k]
            target = device_at(moved(me, **{dim: o}))
            if arriving:
                arrive(view(outs[k], k, part, sets_at(part, phase, me[dim] - o), None, (), (c,)), *sems, target)
            elif phase == 0:
                go(own.at[k, part], homes[k].at[part], *sems, target)
            else:
                ref = view(outs[k], k, part, sets_at(part, phase, me[dim]), None, (), (c,))
                go(ref, ref, *sems, target)

    def ring(k, part, step, arriving):
        dim = ORDERS[part][2]
        size = EXTENT[dim]
        for direction, sign in enumerate((1, -1)):
            sets = sets_at(part, 2, me[dim] - sign * (step if arriving else step - 1))
            half = direction if step == size // 2 else None
            ref = view(outs[k], k, part, sets, half, (), (c,))
            slot = part * 2 + step - 1
            sems = send.at[slot, direction, k], recv.at[slot, direction, k]
            target = device_at(moved(me, **{dim: sign}))
            if arriving:
                arrive(ref, *sems, target)
            else:
                go(ref, ref, *sems, target)

    def ring_share(k, part, step):
        dim = ORDERS[part][2]
        for direction, sign in enumerate((1, -1)):
            half = direction if step == EXTENT[dim] // 2 else None
            share(k, part, sets_at(part, 2, me[dim] - sign * step), half, 3 + (part * 2 + step - 1) * 2 + direction)

    for k in STREAMS:
        for part in range(3):
            near(k, part, 0, False)
    vec_kept.wait()
    vec_start(0)
    for cp in flush:
        cp.wait()
    for k in STREAMS:
        for part in range(3):
            near(k, part, 0, True)
            near(k, part, 1, False)
    tok_start()
    vec_wait(0)
    vec_start(1)
    for k in STREAMS:
        for part in range(3):
            near(k, part, 1, True)
            ring(k, part, 1, False)
    tok_forward()
    for k in STREAMS:
        for part in range(3):
            share(k, part, sets_at(part, 2, me[ORDERS[part][2]]), None, part)
    vec_wait(1)
    vec_start(2)
    for k in STREAMS:
        for part in range(3):
            ring(k, part, 1, True)
            ring(k, part, 2, False)
            ring_share(k, part, 1)
    vec_wait(2)
    vec_start(3)
    tok_share(q, 1, 7)
    for k in STREAMS:
        for part in range(3):
            ring(k, part, 2, True)
            ring_share(k, part, 2)
    tok_share(1 - q, 4, 9)
    vec_wait(3)
    for ref, send_sem, recv_sem in twins:
        arrive(ref, send_sem, recv_sem, twin_id)
    arrive(window.at[1, 1 - c, q], tok_s.at[3], tok_r.at[3], twin_id)
    arrive(window.at[1, 1 - c, 1 - q], tok_s.at[6], tok_r.at[6], twin_id)
    for h, at in ((q, 7), (1 - q, 9)):
        arrive(window.at[0, 1 - c, h], tok_s.at[at], tok_r.at[at], twin_id)
        arrive(window.at[2, 1 - c, h], tok_s.at[at + 1], tok_r.at[at + 1], twin_id)
    tok_kept.wait()
    for cp in out + sent:
        cp.wait_send()

    @pl.when(gives)
    def _():
        down_out.wait_send()


def gather(cat, down, vec, tokens):
    dma = pltpu.SemaphoreType.DMA
    return pl.pallas_call(
        gather_kernel,
        name="gather",
        out_shape=(
            jax.ShapeDtypeStruct((2, *WIDE), jnp.bfloat16),
            jax.ShapeDtypeStruct((2, *WIDE), jnp.bfloat16),
            jax.ShapeDtypeStruct((2, *TALL), jnp.bfloat16),
            jax.ShapeDtypeStruct((2, 4, 4, 4, 8, 128), jnp.float32),
            jax.ShapeDtypeStruct((3, 2, 2, TILE, 768), jnp.bfloat16),
        ),
        in_specs=[ANY_SPACE] * 4,
        out_specs=(ANY_SPACE,) * 5,
        scratch_shapes=[
            pltpu.VMEM((2, 4, 6, HALF), jnp.bfloat16),
            pltpu.VMEM((24, HALF), jnp.float32),
            pltpu.VMEM((3, 3, 8, HALF), jnp.bfloat16),
            dma((4,)), dma((4,)), dma((7,)), dma((3, 2, 8, 3)), dma((3, 2, 8, 3)), dma((6, 2, 3)), dma((6, 2, 3)),
            dma((15, 3)), dma((15, 3)),
            dma((4, 3)), dma((4, 3)), dma((11,)), dma((11,)),
        ],
        compiler_params=pltpu.CompilerParams(collective_id=1, has_side_effects=True),
    )(cat, down, vec, tokens)


def back_kernel(*refs):
    (q_docs, k_docs, q_ref, do_ref, o_ref, lse_ref, gv, kv_hbm, window_hbm, first, dwo, g1, g2, base) = refs[:14]
    (out0, out1, out2, out_v, out_tok) = refs[14:19]
    grads = (None, g1, g2)
    refs = refs[19:]
    acc, other, refs = refs[:3], refs[3:6], refs[6:]
    lands = {}
    for n, (part, phase, k) in enumerate((a, b, k) for a in range(3) for b in range(3) for k in STREAMS):
        lands[part, phase, k] = refs[n]
    refs = refs[27:]
    (
        stage, rows, tall_f, v_c, v_x, v_y, v_z, t_all, t_in, t_land, t_part, t_mate, t_base,
        kv, window, w_heads, dkv_all, dkv, dq_all, dq_acc, dw, q_rows, v_rows,
        local, core_s, core_r, near_s, near_r, send, recv, fin_s, fin_r, t_s, t_r, vec_s, vec_r, tok_s, tok_r, tok_l, load,
    ) = refs
    me = place()
    c, x, y, z = me["c"], me["x"], me["y"], me["z"]
    yp, q, m, zh = lax.rem(y, 2), lax.rem(z, 2), y // 2, z // 2
    twin, across, diagonal = octet_mates(me)
    twin_id = device_at(twin)
    partner, before, after = stream_mates()

    def other_q(at):
        new = dict(at)
        new["z"] = at["z"] + 1 - 2 * lax.rem(at["z"], 2)
        return new

    ring_mates = [moved(me, **{d: k}) for d in ("x", "y", "z") for k in range(1, EXTENT[d])]
    mates = [twin, across, diagonal] + [other_q(a) for a in (me, twin, across, diagonal)]
    targets = ring_mates + [twin, diagonal] + [other_q(a) for a in (twin, across, diagonal)]
    greet([device_at(a) for a in targets] + [before, after])
    sent = []

    def go(src, dst, send_sem, recv_sem, target):
        cp = sending(src, dst, send_sem, recv_sem, target)
        cp.start()
        sent.append(cp)

    def arrive(dst, send_sem, recv_sem, target):
        sending(dst, dst, send_sem, recv_sem, target).wait_recv()

    def order_of(part):
        return ORDERS[part][::-1]

    def sets_of(part, phase, index):
        sets = {"x": x, "y": y, "z": z}
        order = order_of(part)
        for later in order[phase + 1:]:
            sets[later] = None
        sets[order[phase]] = lax.rem(index + 2 * EXTENT[order[phase]], EXTENT[order[phase]])
        return sets

    def add_region(k, part, sets, sources, half=None, gone=()):
        pick, from_pick = picks_of(sets), picks_of(sets, gone)
        dims = dims_of(k)
        inner = dims[3:] if k < 2 else dims[2:]
        outer = [d for d in dims if d not in inner and pick[d] is None]
        count = 1
        for d in outer:
            count *= DIM_SIZE[d]
        cut = pl.ds(*((0, HALF) if half is None else HALVES[k][half]))

        def one(i):
            at = {}
            for d in reversed(outer):
                at[d] = lax.rem(i, DIM_SIZE[d]) if count > 1 else 0
                i = i // DIM_SIZE[d]

            def index(picked):
                return tuple(
                    (at[d] if d in at else slice(None)) if picked[d] is None else pl.ds(picked[d], 1) if d in inner else picked[d]
                    for d in dims
                )

            to = (*index(pick), part, slice(None), cut)
            fr = (*index(from_pick), slice(None), cut)
            if len(sources) == 1:
                acc[k][to] = acc[k][to] + sources[0][fr]
            else:
                total = acc[k][to].astype(jnp.float32)
                for src in sources:
                    total = total + src[fr].astype(jnp.float32)
                acc[k][to] = total.astype(jnp.bfloat16)

        if count == 1:
            one(0)
        else:
            lax.fori_loop(0, count, lambda i, carry: (one(i), carry)[1], 0)

    def hop(part, n):
        return sets_of(part, 0, me[order_of(part)[0]] + (2, 1, -1, 0)[n])

    own_copies = {}

    def cross(k, part, n):
        slot = part * 4 + n
        sets = hop(part, n)
        src = view(grads[k], k, part, sets, None, (), (1 - c,))
        go(src, view(other[k], k, part, sets), core_s.at[slot, k], core_r.at[slot, k], twin_id)
        kept = pltpu.make_async_copy(
            view(grads[k], k, part, sets, None, (), (c,)), view(acc[k], k, part, sets), local.at[slot, k]
        )
        kept.start()
        own_copies[k, part, n] = kept

    loads = [
        pltpu.make_async_copy(kv_hbm, kv, load.at[0]),
        pltpu.make_async_copy(first.at[c, pl.ds(0, 3)], w_heads, load.at[1]),
        pltpu.make_async_copy(window_hbm, window, load.at[2]),
        pltpu.make_async_copy(dwo.at[c], acc[0].at[1, 1], load.at[3]),
        pltpu.make_async_copy(base, t_base, load.at[4]),
    ]
    loads[0].start()
    for n in range(4):
        for k in (1, 2):
            for part in range(3):
                cross(k, part, n)

    for cp in loads[1:]:
        cp.start()
    go(dwo.at[1 - c], other[0], core_s.at[0, 0], core_r.at[0, 0], twin_id)

    vec_lands = (v_c, v_x, v_y, v_z)
    vec_dims = ("c", "x", "y", "z")

    def vec_start(number):
        dim, land = vec_dims[number], vec_lands[number]
        for k in range(1, land.shape[0]):
            mine = land.at[me[dim]]
            go(mine, mine, vec_s.at[number, k], vec_r.at[number, k], device_at(moved(me, **{dim: k})))

    def vec_finish(number):
        dim, land = vec_dims[number], vec_lands[number]
        size = land.shape[0]
        for k in range(1, size):
            theirs = land.at[lax.rem(me[dim] - k + size, size)]
            arrive(theirs, vec_s.at[number, k], vec_r.at[number, k], device_at(moved(me, **{dim: k})))
        total = land[0]
        for k in range(1, size):
            total = total + land[k]
        return total

    def row_blocks(fn):
        lax.fori_loop(0, TILE // 32, lambda r, carry: (fn(pl.ds(pl.multiple_of(r * 32, 32), 32)), carry)[1], 0)

    def tok_twin(group, at):
        go(t_all.at[1 - c, group], t_in.at[group], tok_s.at[at], tok_r.at[at], twin_id)

    def tok_edges():
        for n, (group, at) in enumerate(((0, 0), (2, 6))):
            arrive(t_in.at[group], tok_s.at[at], tok_r.at[at], twin_id)
        for n, h in enumerate((1 - q, q)):
            for group in (0, 2):
                def one(at):
                    t_all[c, group, h, at] = t_all[c, group, h, at] + t_in[group, h, at]
                row_blocks(one)
            go(t_all.at[c, 0, h], t_land.at[1, h], tok_s.at[1 + n], tok_r.at[1 + n], before)
            go(t_all.at[c, 2, h], t_land.at[0, h], tok_s.at[3 + n], tok_r.at[3 + n], after)

    def tok_total(h, at):
        f = jnp.float32
        return t_all[c, 1, h, at].astype(f) + t_in[1, h, at].astype(f) + t_land[0, h, at].astype(f) + t_land[1, h, at].astype(f)

    def tok_theirs():
        h = 1 - q
        arrive(t_in.at[1], tok_s.at[7], tok_r.at[7], twin_id)
        arrive(t_land.at[1, h], tok_s.at[1], tok_r.at[1], after)
        arrive(t_land.at[0, h], tok_s.at[3], tok_r.at[3], before)

        def one(at):
            t_part[at] = tok_total(h, at).astype(jnp.bfloat16)
        row_blocks(one)
        go(t_part, t_mate, tok_s.at[5], tok_r.at[5], partner)

    def tok_mine():
        arrive(t_land.at[1, q], tok_s.at[2], tok_r.at[2], after)
        arrive(t_land.at[0, q], tok_s.at[4], tok_r.at[4], before)
        arrive(t_mate, tok_s.at[5], tok_r.at[5], partner)
        loads[4].wait()

        def one(at):
            t_base[at] = tok_total(q, at) + t_mate[at].astype(jnp.float32) + t_base[at]
        row_blocks(one)
        done = pltpu.make_async_copy(t_base, out_tok, tok_l.at[0])
        done.start()
        return done

    def meet(k, part, n):
        slot = part * 4 + n
        own_copies[k, part, n].wait()
        sets = hop(part, n)
        arrive(view(other[k], k, part, sets), core_s.at[slot, k], core_r.at[slot, k], twin_id)
        add_region(k, part, sets, [other[k].at[(slice(None),) * 5 + (part,)]])

    def meet_out():
        loads[3].wait()
        arrive(other[0], core_s.at[0, 0], core_r.at[0, 0], twin_id)

        def one(i, carry):
            acc[0][1, 1, i] = acc[0][1, 1, i] + other[0][i]
            return carry

        lax.fori_loop(0, 4, one, 0)

    def ring(k, part, step, arriving):
        dim = order_of(part)[0]
        ahead = 3 - step - (1 if arriving else 0)
        for direction, sign in enumerate((1, -1)):
            half = direction if step == 1 else None
            sets = sets_of(part, 0, me[dim] + sign * ahead)
            land = lands[part, 0, k].at[direction, step - 1]
            slot = part * 2 + step - 1
            sems = send.at[slot, direction, k], recv.at[slot, direction, k]
            target = device_at(moved(me, **{dim: sign}))
            here = view(land, k, None, sets, half, (dim,))
            if arriving:
                arrive(here, *sems, target)
                add_region(k, part, sets, [land], half, (dim,))
            else:
                go(view(acc[k], k, part, sets, half), here, *sems, target)

    def near(k, part, phase, arriving):
        order = order_of(part)
        dim, gone = order[phase], order[: phase + 1]
        mine = sets_of(part, phase, me[dim])
        sources = []
        for o in OTHERS[dim]:
            sems = near_s.at[part, phase - 1, o, k], near_r.at[part, phase - 1, o, k]
            target = device_at(moved(me, **{dim: o}))
            land = lands[part, phase, k].at[o - 1]
            here = view(land, k, None, mine, None, gone)
            if arriving:
                arrive(here, *sems, target)
                sources.append(land)
            else:
                go(view(acc[k], k, part, sets_of(part, phase, me[dim] + o)), here, *sems, target)
        if arriving:
            add_region(k, part, mine, sources, None, gone)

    def vec_next(n):
        total = vec_finish(n)
        if n < 3:
            vec_lands[n + 1][me[vec_dims[n + 1]]] = total
            vec_start(n + 1)
        else:
            out_v[...] = total

    low = lanes_low(TILE)
    scale = HEAD_DIM ** -0.5 * LOG2E
    picker = (
        lax.broadcasted_iota(jnp.int32, (8, 128), 0) == lax.broadcasted_iota(jnp.int32, (8, 128), 1) // HEAD_DIM
    ).astype(jnp.float32)

    def heads_back(pair, i):
        cols = slice(pair * 128, (pair + 1) * 128)
        qs, d_out = q_ref[i, :, cols], do_ref[i, :, cols]
        none = jnp.zeros_like(qs)
        q_heads = (jnp.where(low, qs, none), jnp.where(low, none, qs))
        do_heads = (jnp.where(low, d_out, none), jnp.where(low, none, d_out))
        prod = d_out.astype(jnp.float32) * o_ref[i, :, cols].astype(jnp.float32)
        deltas = lax.dot_general(
            picker, prod, (((1,), (1,)), ((), ())), precision=lax.Precision.HIGHEST, preferred_element_type=jnp.float32
        )
        if i == 0:
            dkv[...] = jnp.zeros_like(dkv)
        dq_acc[...] = jnp.zeros_like(dq_acc)

        def step(n, carry):
            t = q + 2 * i + n
            k, v = kv[0, t, :, cols], kv[1, t, :, cols]
            k_flip = flipped(k)
            same = q_docs[i] == k_docs[t]
            dk, dv = [], []
            for head in range(2):
                lanes = slice(head * HEAD_DIM, (head + 1) * HEAD_DIM)
                scores = across_lanes(k, q_heads[head]) * scale
                p = jnp.where(same, jnp.exp2(scores - lse_ref[pair, i, head : head + 1]), 0.0)
                dp = across_lanes(v, do_heads[head])
                ds = (p * (dp - deltas[head : head + 1])).astype(jnp.bfloat16)
                dq_acc[lanes] += dot32(k_flip[lanes], ds)
                dk.append(dot32(ds, q_heads[head]))
                dv.append(dot32(p.astype(jnp.bfloat16), do_heads[head]))
            dkv[0, t] += dk[0] + dk[1]
            dkv[1, t] += dv[0] + dv[1]
            return carry

        lax.fori_loop(0, 9, step, 0)
        dq_all[i, :, cols] = flipped(dq_acc[...] * HEAD_DIM ** -0.5).astype(jnp.bfloat16)
        if i == 1:
            def keep(t, carry):
                dkv_all[0, t, :, cols] = (dkv[0, t] * HEAD_DIM ** -0.5).astype(jnp.bfloat16)
                dkv_all[1, t, :, cols] = dkv[1, t].astype(jnp.bfloat16)
                return carry

            lax.fori_loop(0, 12, keep, 0)

    def tile_back(group, n):
        core, h = n // 2, lax.rem(n, 2)
        t = group * 4 + n
        x_flip = flipped(window[t])
        dk, dv = dkv_all[0, t], dkv_all[1, t]
        dw[1] += dot32(x_flip, dk)
        dw[2] += dot32(x_flip, dv)
        v_rows[...] = v_rows[...] + jnp.sum(dv.astype(jnp.float32), axis=0, keepdims=True)
        dx = across_lanes(dk, w_heads[1]) + across_lanes(dv, w_heads[2])
        t_all[core, group, h] = dx.astype(jnp.bfloat16)
        if group == 1:
            @pl.when(h == q)
            def _():
                dq = dq_all[core]
                dw[0] += dot32(x_flip, dq)
                q_rows[...] = q_rows[...] + jnp.sum(dq.astype(jnp.float32), axis=0, keepdims=True)
                t_all[core, group, h] = (dx + across_lanes(dq, w_heads[0])).astype(jnp.bfloat16)

    def tiles_back(group):
        lax.fori_loop(0, 4, lambda n, carry: (tile_back(group, n), carry)[1], 0)

    parts = range(3)
    late = [(k, part) for k in (1, 2) for part in parts]
    for k, part in late:
        meet(k, part, 0)
        ring(k, part, 1, False)
    loads[0].wait()
    heads_back(0, 0)
    for k, part in late:
        meet(k, part, 1)
        meet(k, part, 2)
    for part in parts:
        ring(1, part, 1, True)
        ring(1, part, 2, False)
    heads_back(0, 1)
    for part in parts:
        ring(2, part, 1, True)
        ring(2, part, 2, False)
    heads_back(1, 0)
    for k, part in late:
        meet(k, part, 3)
    meet_out()
    heads_back(1, 1)
    for part in parts:
        ring(1, part, 2, True)
        near(1, part, 1, False)
    heads_back(2, 0)
    for part in parts:
        ring(2, part, 2, True)
        near(2, part, 1, False)
    for part in parts:
        near(1, part, 1, True)
        near(1, part, 2, False)
    heads_back(2, 1)
    for part in parts:
        near(2, part, 1, True)
        near(2, part, 2, False)
    loads[1].wait()
    loads[2].wait()
    dw[...] = jnp.zeros_like(dw)
    q_rows[...] = jnp.zeros_like(q_rows)
    v_rows[...] = jnp.zeros_like(v_rows)
    tiles_back(0)
    tok_twin(0, 0)
    tiles_back(2)
    tok_twin(2, 6)
    for k, part in late:
        near(k, part, 2, True)
    tiles_back(1)
    tok_twin(1, 7)

    def grads_low(i, carry):
        rows_at = pl.ds(pl.multiple_of(i * 192, 192), 192)
        for number, (a, b) in enumerate(((0, 0), (0, 1), (1, 0))):
            acc[0][a, b, i] = dw[number, rows_at].reshape(4, 2, 3, 8, HALF).astype(jnp.bfloat16)
        return carry

    lax.fori_loop(0, 4, grads_low, 0)
    for part in parts:
        ring(0, part, 1, False)
    v_c[c] = gv[...]
    half_cols = pl.ds(pl.multiple_of(c * HALF, 128), HALF)
    v_c[c, 0:1, half_cols] = q_rows[...]
    v_c[c, 1:2, half_cols] = v_rows[...]
    vec_start(0)
    tok_edges()
    vec_next(0)
    for part in parts:
        ring(0, part, 1, True)
        ring(0, part, 2, False)
    vec_next(1)
    for part in parts:
        ring(0, part, 2, True)
        near(0, part, 1, False)
    vec_next(2)
    for part in parts:
        near(0, part, 1, True)
        near(0, part, 2, False)
    tok_theirs()
    vec_next(3)
    for part in parts:
        near(0, part, 2, True)

    for k in range(2):
        for part in range(3):
            stage[pl.ds(8 * part, 8), :] = acc[k][yp, q, x, zh, m, part].astype(jnp.float32)
        for owner in range(4):
            rows[k, owner] = stage[pl.ds(6 * owner, 6), :]
    for part in range(3):
        tall_f[part] = acc[2][x, zh, m, yp, q, part].astype(jnp.float32)

    def cols_at(at):
        return pl.ds(pl.multiple_of((lax.rem(at["y"], 2) * 2 + lax.rem(at["z"], 2)) * 768 + at["c"] * HALF, 128), HALF)

    def owner_of(at):
        return lax.rem(at["y"], 2) * 2 + at["c"]

    for k, out in enumerate((out0, out1)):
        for n, mate in enumerate(mates):
            go(rows.at[k, owner_of(mate)], out.at[:, cols_at(me)], fin_s.at[k, n], fin_r.at[k, n], device_at(mate))
    kept = [
        pltpu.make_async_copy(rows.at[k, owner_of(me)], out.at[:, cols_at(me)], fin_s.at[k, 7])
        for k, out in enumerate((out0, out1))
    ]
    for cp in kept:
        cp.start()
    stays = c == q
    half_at = [pl.ds(pl.multiple_of(a * HALF, 128), HALF) for a in (c, 1 - c)]
    t_self = pltpu.make_async_copy(tall_f, out2.at[:, :, half_at[0]], t_s.at[0])
    there_same, there_cross = device_at(other_q(me)), device_at(other_q(twin))
    t_twin = sending(tall_f, out2.at[:, :, half_at[0]], t_s.at[0], t_r.at[0], twin_id)
    t_same = sending(tall_f, out2.at[:, :, half_at[0]], t_s.at[1], t_r.at[1], there_same)
    t_cross = sending(tall_f, out2.at[:, :, half_at[0]], t_s.at[1], t_r.at[2], there_cross)

    @pl.when(stays)
    def _():
        t_self.start()
        t_same.start()

    @pl.when(jnp.logical_not(stays))
    def _():
        t_twin.start()
        t_cross.start()

    for k, out in enumerate((out0, out1)):
        for n, mate in enumerate(mates):
            arrive(out.at[:, cols_at(mate)], fin_s.at[k, n], fin_r.at[k, n], device_at(mate))

    @pl.when(stays)
    def _():
        arrive(out2.at[:, :, half_at[1]], t_s.at[0], t_r.at[0], twin_id)
        t_self.wait()
        t_same.wait_send()

    @pl.when(jnp.logical_not(stays))
    def _():
        arrive(out2.at[:, :, half_at[0]], t_s.at[1], t_r.at[1], there_same)
        arrive(out2.at[:, :, half_at[1]], t_s.at[1], t_r.at[2], there_cross)
        t_twin.wait_send()
        t_cross.wait_send()

    tok_mine().wait()
    for cp in kept:
        cp.wait()
    for cp in sent:
        cp.wait_send()


def back(q_docs, k_docs, q_heads, d_heads, o_heads, lse, gv, kv, window, first, dwo, g1, g2, base):
    bf, f32, dma = jnp.bfloat16, jnp.float32, pltpu.SemaphoreType.DMA
    lands = []
    for part in range(3):
        order = ORDERS[part][::-1]
        for phase in range(3):
            size = dict(DIM_SIZE)
            for dim, names in (("x", ("x",)), ("y", ("m", "yp")), ("z", ("zh", "q"))):
                if dim in order[: phase + 1]:
                    for name in names:
                        size[name] = 1
            count = (2, 2) if phase == 0 else (EXTENT[order[phase]] - 1,)
            lands += [pltpu.VMEM((*count, *(size[d] for d in dims_of(k)), 8, HALF), bf) for k in STREAMS]
    whole = [pltpu.VMEM(WIDE, bf), pltpu.VMEM(TALL, bf)]
    return pl.pallas_call(
        back_kernel,
        name="back",
        out_shape=(
            jax.ShapeDtypeStruct((6, 3072), f32),
            jax.ShapeDtypeStruct((6, 3072), f32),
            jax.ShapeDtypeStruct((3, 8, 768), f32),
            jax.ShapeDtypeStruct((16, 768), f32),
            jax.ShapeDtypeStruct((TILE, 768), f32),
        ),
        in_specs=[IN_VMEM] * 7 + [ANY_SPACE] * 7,
        out_specs=(ANY_SPACE, ANY_SPACE, ANY_SPACE, IN_VMEM, ANY_SPACE),
        scratch_shapes=[
            pltpu.VMEM(WIDE, bf), *whole, pltpu.VMEM((4, 4, 2, 3, 8, HALF), bf), *whole, *lands,
            pltpu.VMEM((24, HALF), f32),
            pltpu.VMEM((2, 4, 6, HALF), f32),
            pltpu.VMEM((3, 8, HALF), f32),
            pltpu.VMEM((2, 16, 768), f32),
            pltpu.VMEM((4, 16, 768), f32),
            pltpu.VMEM((4, 16, 768), f32),
            pltpu.VMEM((8, 16, 768), f32),
            pltpu.VMEM((2, 3, 2, TILE, 768), bf),
            pltpu.VMEM((3, 2, TILE, 768), bf),
            pltpu.VMEM((2, 2, TILE, 768), bf),
            pltpu.VMEM((TILE, 768), bf),
            pltpu.VMEM((TILE, 768), bf),
            pltpu.VMEM((TILE, 768), f32),
            pltpu.VMEM((2, 12, TILE, HALF), bf),
            pltpu.VMEM((12, TILE, 768), bf),
            pltpu.VMEM((3, 768, HALF), bf),
            pltpu.VMEM((2, 12, TILE, HALF), bf),
            pltpu.VMEM((2, 12, TILE, 128), f32),
            pltpu.VMEM((2, TILE, HALF), bf),
            pltpu.VMEM((128, TILE), f32),
            pltpu.VMEM((3, 768, HALF), f32),
            pltpu.VMEM((1, HALF), f32),
            pltpu.VMEM((1, HALF), f32),
            dma((12, 3)), dma((12, 3)), dma((12, 3)), dma((3, 2, 8, 3)), dma((3, 2, 8, 3)), dma((6, 2, 3)), dma((6, 2, 3)),
            dma((2, 8)), dma((2, 7)),
            dma((2,)), dma((3,)), dma((4, 8)), dma((4, 8)), dma((8,)), dma((8,)), dma((1,)), dma((5,)),
        ],
        compiler_params=pltpu.CompilerParams(collective_id=2, has_side_effects=True, vmem_limit_bytes=63 << 20),
    )(q_docs, k_docs, q_heads, d_heads, o_heads, lse, gv, kv, window, first, dwo, g1, g2, base)


def to_tokens_kernel(heads, rows, send, recv, local):
    me = place()
    c = me["c"]
    twin = device_at(moved(me, c=1))
    mine, other = (pl.ds(pl.multiple_of(a * HALF, 128), HALF) for a in (c, 1 - c))
    greet((twin,))
    out = sending(heads.at[1 - c], rows.at[:, mine], send.at[0], recv.at[0], twin)
    out.start()
    kept = pltpu.make_async_copy(heads.at[c], rows.at[:, mine], local.at[0])
    kept.start()
    kept.wait()
    sending(heads.at[c], rows.at[:, other], send.at[0], recv.at[0], twin).wait_recv()
    out.wait_send()


def to_heads_kernel(rows, heads, send, recv, local):
    me = place()
    c = me["c"]
    twin = device_at(moved(me, c=1))
    mine, other = (pl.ds(pl.multiple_of(a * HALF, 128), HALF) for a in (c, 1 - c))
    greet((twin,))
    out = sending(rows.at[:, other], heads.at[c], send.at[0], recv.at[0], twin)
    out.start()
    kept = pltpu.make_async_copy(rows.at[:, mine], heads.at[c], local.at[0])
    kept.start()
    kept.wait()
    sending(rows.at[:, mine], heads.at[1 - c], send.at[0], recv.at[0], twin).wait_recv()
    out.wait_send()


def swap(kernel, name, shape, number, array):
    return pl.pallas_call(
        kernel,
        name=name,
        out_shape=jax.ShapeDtypeStruct(shape, array.dtype),
        in_specs=[ANY_SPACE],
        out_specs=IN_VMEM,
        scratch_shapes=[pltpu.SemaphoreType.DMA((1,))] * 3,
        compiler_params=pltpu.CompilerParams(collective_id=number, has_side_effects=True, vmem_limit_bytes=58 << 20),
    )(array)


def dot32(a, b):
    return jnp.dot(a, b, preferred_element_type=jnp.float32)


def lanes_low(rows):
    return lax.broadcasted_iota(jnp.int32, (rows, 128), 1) < HEAD_DIM


def across_lanes(a, b):
    return lax.dot_general(a, b, (((1,), (1,)), ((), ())), preferred_element_type=jnp.float32)


def flipped(a):
    return jnp.swapaxes(a, 0, 1)


def project_kernel(plan, x_ref, w_ref, bq_ref, bv_ref, q_ref, kv_ref):
    t = pl.program_id(0)
    x = x_ref[0]
    for i in range(2):
        @pl.when(t == plan[1 + i])
        def _():
            q_ref[i] = (dot32(x, w_ref[0, 0]) + bq_ref[0]).astype(jnp.bfloat16)

    kv_ref[0, 0] = dot32(x, w_ref[0, 1]).astype(jnp.bfloat16)
    kv_ref[1, 0] = (dot32(x, w_ref[0, 2]) + bv_ref[0]).astype(jnp.bfloat16)


def project(plan, window, first, bias_q, bias_v):
    half = pl.BlockSpec((1, 1, HALF), lambda t, p: (p[0], 0, 0))
    return pl.pallas_call(
        project_kernel,
        name="project",
        grid_spec=pltpu.PrefetchScalarGridSpec(
            num_scalar_prefetch=1,
            grid=(12,),
            in_specs=[
                pl.BlockSpec((1, TILE, 768), lambda t, p: (t, 0, 0)),
                pl.BlockSpec((1, 4, 768, HALF), lambda t, p: (p[0], 0, 0, 0)),
                half, half,
            ],
            out_specs=[
                pl.BlockSpec((2, TILE, HALF), lambda t, p: (0, 0, 0)),
                pl.BlockSpec((2, 1, TILE, HALF), lambda t, p: (0, t, 0, 0)),
            ],
        ),
        out_shape=(
            jax.ShapeDtypeStruct((2, TILE, HALF), jnp.bfloat16),
            jax.ShapeDtypeStruct((2, 12, TILE, HALF), jnp.bfloat16),
        ),
        compiler_params=pltpu.CompilerParams(vmem_limit_bytes=58 << 20),
    )(plan, window, first, bias_q, bias_v)


def attend_kernel(plan, q_docs, k_docs, q_ref, kv, o_ref, lse_ref, top, total, acc):
    i = pl.program_id(1)
    low = lanes_low(TILE)
    q = q_ref[0]
    none = jnp.zeros_like(q)
    q_heads = (jnp.where(low, q, none), jnp.where(low, none, q))
    docs = q_docs[0]
    top[...] = jnp.full_like(top, BOTTOM)
    total[...] = jnp.zeros_like(total)
    acc[...] = jnp.zeros_like(acc)
    scale = HEAD_DIM ** -0.5 * LOG2E

    def step(j, carry):
        k, v = kv[0, j], flipped(kv[1, j])
        same = docs == k_docs[j]
        for head in range(2):
            rows = slice(head * HEAD_DIM, (head + 1) * HEAD_DIM)
            s = jnp.where(same, across_lanes(k, q_heads[head]) * scale, BOTTOM)
            old = top[head]
            new = jnp.maximum(old, jnp.max(s, axis=0, keepdims=True))
            fade = jnp.exp2(old - new)
            p = jnp.exp2(s - new)
            total[head] = total[head] * fade + jnp.sum(p, axis=0, keepdims=True)
            top[head] = new
            acc[rows] = acc[rows] * fade + dot32(v[rows], p.astype(jnp.bfloat16))
        return carry

    lax.fori_loop(plan[3 + 2 * i], plan[4 + 2 * i], step, 0)
    for head in range(2):
        rows = slice(head * HEAD_DIM, (head + 1) * HEAD_DIM)
        acc[rows] = acc[rows] / total[head]
        lse_ref[0, 0, pl.ds(head, 1)] = top[head] + jnp.log2(total[head])
    o_ref[0] = flipped(acc[...]).astype(jnp.bfloat16)


OWN_PAIR = pl.BlockSpec((1, TILE, 128), lambda p, i, b: (i, 0, p))
WINDOW_PAIR = pl.BlockSpec((2, 12, TILE, 128), lambda p, i, b: (0, 0, 0, p))
STATS = pl.BlockSpec((1, 1, 2, TILE), lambda p, i, b: (p, i, 0, 0))
DOC_SPECS = [
    pl.BlockSpec((1, 1, TILE), lambda p, i, b: (i, 0, 0)),
    pl.BlockSpec((12, TILE, 1), lambda p, i, b: (0, 0, 0)),
]


def attend(plan, q_docs, k_docs, q_heads, kv):
    return pl.pallas_call(
        attend_kernel,
        name="attend",
        grid_spec=pltpu.PrefetchScalarGridSpec(
            num_scalar_prefetch=1,
            grid=(3, 2),
            in_specs=[*DOC_SPECS, OWN_PAIR, WINDOW_PAIR],
            out_specs=[OWN_PAIR, STATS],
            scratch_shapes=[
                pltpu.VMEM((2, 1, TILE), jnp.float32),
                pltpu.VMEM((2, 1, TILE), jnp.float32),
                pltpu.VMEM((128, TILE), jnp.float32),
            ],
        ),
        out_shape=(
            jax.ShapeDtypeStruct((2, TILE, HALF), jnp.bfloat16),
            jax.ShapeDtypeStruct((3, 2, 2, TILE), jnp.float32),
        ),
        compiler_params=pltpu.CompilerParams(vmem_limit_bytes=58 << 20),
    )(plan, q_docs, k_docs, q_heads, kv)


def norm_parts(resid):
    centred = resid - jnp.mean(resid, axis=1, keepdims=True)
    inverse = lax.rsqrt(jnp.mean(centred * centred, axis=1, keepdims=True) + NORM_EPS)
    return centred * inverse, inverse


def norm_back(upstream, gain, n, inverse):
    e = upstream * gain
    return inverse * (e - jnp.mean(e, axis=1, keepdims=True) - n * jnp.mean(e * n, axis=1, keepdims=True))


def row_sum(a):
    return jnp.sum(a, axis=0, keepdims=True)


def mlp_kernel(
    att_ref, tok_ref, cot_ref, rows, bias_in, first, second, third,
    out_ref, d_one_ref, d_att_ref, dwo_ref, dw_in_ref, dw_down_ref, sums_ref, sums_in_ref,
    w_out, w_in, w_down, n_one, low, low_flip, slope, active, wide, sem,
):
    f32, bf = jnp.float32, jnp.bfloat16
    loads = [pltpu.make_async_copy(first.at[:, 3], w_out, sem.at[0])]
    loads += [pltpu.make_async_copy(second, w_in, sem.at[1]), pltpu.make_async_copy(third, w_down, sem.at[2])]
    for cp in loads:
        cp.start()

    def row(n):
        return rows[n : n + 1]

    halves = (slice(0, HALF), slice(HALF, 768))
    loads[0].wait()
    att = att_ref[...]
    for h in range(2):
        wide[:, halves[h]] = dot32(att, w_out[h])
    one, inverse_one = norm_parts(tok_ref[...].astype(f32) + (wide[...] + row(2)))
    n_one[...] = one
    normed = one * row(3) + row(4)
    low[...] = normed.astype(bf)
    low_flip[...] = flipped(low[...])
    wide[...] = normed + row(5)
    loads[1].wait()
    loads[2].wait()

    def up(m, carry):
        h = dot32(low[...], w_in[lax.rem(m, 2), m // 2]) + bias_in[m]
        cdf = 0.5 * (1.0 + lax.erf(h * 0.7071067811865476))
        slope[m] = cdf + h * jnp.exp(h * h * -0.5) * 0.3989422804014327
        a = (h * cdf).astype(bf)
        active[m] = flipped(a)
        for k in range(2):
            wide[:, halves[k]] += dot32(a, w_down[k, m])
        return carry

    lax.fori_loop(0, 8, up, 0)
    two, inverse_two = norm_parts(wide[...])
    out_ref[...] = (two * row(6) + row(7)).astype(bf)
    upstream = cot_ref[...].astype(f32)
    sums_ref[0:2] = jnp.zeros((2, 768), f32)
    sums_ref[6:7] = row_sum(upstream * two)
    sums_ref[7:8] = row_sum(upstream)
    d_two = norm_back(upstream, row(6), two, inverse_two)
    sums_ref[5:6] = row_sum(d_two)
    d_low = d_two.astype(bf)
    wide[...] = d_two

    def down(m, carry):
        d_active = None
        for k in range(2):
            d_half = d_low[:, halves[k]]
            dw_down_ref[k, m] = dot32(active[m], d_half).astype(bf)
            part = across_lanes(d_half, w_down[k, m])
            d_active = part if d_active is None else d_active + part
        d_hidden = (d_active * slope[m]).astype(bf)
        sums_in_ref[m] = row_sum(d_hidden.astype(f32))
        dw_in_ref[lax.rem(m, 2), m // 2] = dot32(low_flip[...], d_hidden).astype(bf)
        wide[...] += across_lanes(d_hidden, w_in[lax.rem(m, 2), m // 2])
        return carry

    lax.fori_loop(0, 8, down, 0)
    d_normed = wide[...]
    one = n_one[...]
    sums_ref[3:4] = row_sum(d_normed * one)
    sums_ref[4:5] = row_sum(d_normed)
    d_one = norm_back(d_normed, row(3), one, inverse_one)
    d_one_ref[...] = d_one
    sums_ref[2:3] = row_sum(d_one)
    d_low = d_one.astype(bf)
    att_flip = flipped(att_ref[...])
    d_att = None
    for h in range(2):
        d_half = d_low[:, halves[h]]
        dwo_ref[h] = dot32(att_flip, d_half).astype(bf)
        part = across_lanes(d_half, w_out[h])
        d_att = part if d_att is None else d_att + part
    d_att_ref[...] = d_att.astype(bf)


def mlp(att, tokens, cotangent, rows, bias_in, first, second, third):
    f32, bf = jnp.float32, jnp.bfloat16
    return pl.pallas_call(
        mlp_kernel,
        name="mlp",
        in_specs=[IN_VMEM] * 5 + [ANY_SPACE] * 3,
        out_specs=(IN_VMEM,) * 8,
        out_shape=(
            jax.ShapeDtypeStruct((TILE, 768), bf),
            jax.ShapeDtypeStruct((TILE, 768), f32),
            jax.ShapeDtypeStruct((TILE, 768), bf),
            jax.ShapeDtypeStruct((2, 768, HALF), bf),
            jax.ShapeDtypeStruct((2, 4, 768, HALF), bf),
            jax.ShapeDtypeStruct((2, 8, HALF, HALF), bf),
            jax.ShapeDtypeStruct((8, 768), f32),
            jax.ShapeDtypeStruct((8, 1, HALF), f32),
        ),
        scratch_shapes=[
            pltpu.VMEM((2, 768, HALF), bf),
            pltpu.VMEM((2, 4, 768, HALF), bf),
            pltpu.VMEM((2, 8, HALF, HALF), bf),
            pltpu.VMEM((TILE, 768), f32),
            pltpu.VMEM((TILE, 768), bf),
            pltpu.VMEM((768, TILE), bf),
            pltpu.VMEM((8, TILE, HALF), f32),
            pltpu.VMEM((8, HALF, TILE), bf),
            pltpu.VMEM((TILE, 768), f32),
            pltpu.SemaphoreType.DMA((3,)),
        ],
        compiler_params=pltpu.CompilerParams(vmem_limit_bytes=58 << 20),
    )(att, tokens, cotangent, rows, bias_in, first, second, third)


def body(
    tokens, w_qkv, bias_q, bias_v, w_out, bias_out, gain_one, shift_one, w_in, bias_in,
    w_down, bias_down, gain_two, shift_two, doc_lengths, cotangent,
):
    shard, seq = lax.axis_index("shard"), lax.axis_index("seq")
    core = lax.rem(shard, 2)
    f32, bf = jnp.float32, jnp.bfloat16
    width = tokens.shape[1]
    stream_len = tokens.shape[0] * lax.axis_size("seq") * lax.axis_size("shard")

    positions = (shard // 2 - 1) * (4 * TILE) + jnp.arange(12 * TILE, dtype=jnp.int32)
    starts = jnp.cumsum(doc_lengths, dtype=jnp.int32) - doc_lengths
    counted = jnp.sum((positions[:, None] >= starts[None, :]).astype(jnp.int32), axis=1, dtype=jnp.int32) - 1
    docs = jnp.where(positions < stream_len, counted, stream_len).reshape(12, TILE)
    query_docs = lax.dynamic_slice(docs, (4 + seq, 0), (3, TILE))[::2]
    lower = jnp.sum((docs[None, :, -1] < query_docs[:, :1]).astype(jnp.int32), axis=1)
    upper = jnp.sum((docs[None, :, 0] <= query_docs[:, -1:]).astype(jnp.int32), axis=1)
    plan = jnp.stack([core, 4 + seq, 6 + seq, lower[0], upper[0], lower[1], upper[1], lower[0], upper[1]])
    query_docs, key_docs = query_docs.reshape(2, 1, TILE), docs.reshape(12, TILE, 1)

    vectors = (bias_q, bias_v, bias_out, gain_one, shift_one, bias_down, gain_two, shift_two)
    vec = jnp.concatenate(
        [
            jnp.stack(vectors).astype(f32),
            jnp.pad(bias_in.astype(f32).reshape(1, 24), ((0, 7), (0, 0))),
            jnp.zeros((8, 98), f32),
        ],
        axis=1,
    )
    cat = jnp.stack([jnp.concatenate([w_qkv, w_out], axis=1), w_in])
    first, second, third, vecs, window = gather(cat, w_down.reshape(3, 8, width), vec, tokens)
    first = first.reshape(2, 4, width, HALF)
    second = second.reshape(2, 4, width, HALF)
    third = third.reshape(2, 8, HALF, HALF)
    window = window.reshape(12, TILE, width)
    vecs = jnp.transpose(vecs, (4, 1, 2, 3, 0, 5)).reshape(8, 128, 128)
    rows = vecs[:, :, :6].reshape(8, width)
    hidden_bias = vecs[0, :, 6:30].reshape(8, 1, HALF)

    q_heads, kv = project(plan, window, first, rows[0].reshape(2, 1, HALF), rows[1].reshape(2, 1, HALF))
    o_heads, lse = attend(plan, query_docs, key_docs, q_heads, kv)
    attended = swap(to_tokens_kernel, "to_tokens", (TILE, width), 4, o_heads)
    layer_out, d_one, d_att, dw_out, dw_in, dw_down, sums, sums_in = mlp(
        attended, tokens, cotangent, rows, hidden_bias, first, second, third
    )
    d_heads = swap(to_heads_kernel, "to_heads", (2, TILE, HALF), 5, d_att)
    vec_sums = jnp.concatenate([sums, sums_in.reshape(4, width), jnp.zeros((4, width), f32)], axis=0)
    sum_first, sum_in, sum_down, sum_vec, grad_tokens = back(
        query_docs, key_docs, q_heads, d_heads, o_heads, lse, vec_sums, kv, window, first,
        dw_out.reshape(2, 4, 4, 2, 3, 8, HALF), dw_in.reshape(2, *WIDE), dw_down.reshape(2, *TALL), d_one,
    )
    own = lax.dynamic_slice(sum_vec, (0, 6 * shard), (8, 6))
    own_in = lax.dynamic_slice(sum_vec[8:12].reshape(-1), (24 * shard,), (24,))
    return (
        layer_out, grad_tokens, sum_first[:, : 3 * width], own[0], own[1], sum_first[:, 3 * width :],
        own[2], own[3], own[4], sum_in, own_in, sum_down.reshape(24, width), own[5], own[6], own[7],
    )


def solution(mesh):
    both, own = P(("shard", "seq"), None), P("shard")
    rows = P("shard", None)
    return jax.shard_map(
        body,
        mesh=mesh,
        in_specs=(both, rows, own, own, rows, own, own, own, rows, own, rows, own, own, own, P(), both),
        out_specs=(both, both, rows, own, own, rows, own, own, own, rows, own, rows, own, own, own),
        check_vma=False,
    )
```

```python
import functools
import jax
import jax.numpy as jnp
from jax import lax
from jax.experimental import pallas as pl
from jax.experimental.pallas import tpu as pltpu
from jax.sharding import PartitionSpec as P

HEAD_DIM = 64
NORM_EPS = 1e-12
MESH = pl.DeviceIdType.MESH
ANY_SPACE = pl.BlockSpec(memory_space=pl.ANY)
IN_VMEM = pl.BlockSpec(memory_space=pltpu.VMEM)
LOG2E = 1.4426950408889634
TILE = 256
HALF = 384
BOTTOM = -1e30
EXTENT = {"x": 4, "y": 4, "z": 8}
ORDERS = (("z", "y", "x"), ("z", "y", "x"), ("z", "x", "y"))
X_FIRST, Y_FIRST = ("x", "y", "z"), ("y", "x", "z")
SUM_ORDERS = ((X_FIRST, X_FIRST, Y_FIRST), (X_FIRST, Y_FIRST, X_FIRST), (X_FIRST, X_FIRST, Y_FIRST))
OTHERS = {dim: range(1, size) for dim, size in EXTENT.items()}
HALVES = (((0, 256), (256, 128)), ((0, 128), (128, 256)), ((0, 256), (256, 128)))
STREAMS = (0, 1, 2)
WIDE = (2, 2, 4, 4, 2, 3, 8, HALF)
TALL = (4, 4, 2, 2, 2, 3, 8, HALF)


def place():
    s = lax.axis_index("shard")
    q = lax.axis_index("seq")
    return {
        "c": lax.rem(s, 2),
        "y": lax.rem(s // 2, 4),
        "x": s // 32,
        "z": lax.rem(s // 8, 4) * 2 + q,
    }


def device_at(at):
    return {
        "shard": ((at["x"] * 4 + at["z"] // 2) * 4 + at["y"]) * 2 + at["c"],
        "seq": lax.rem(at["z"], 2),
    }


def moved(at, **steps):
    new = dict(at)
    for dim, step in steps.items():
        size = 2 if dim == "c" else EXTENT[dim]
        new[dim] = lax.rem(at[dim] + step + size, size)
    return new


def stream_mates():
    s = lax.axis_index("shard")
    q = lax.axis_index("seq")
    partner = {"shard": s, "seq": 1 - q}
    after = {"shard": lax.rem(s + 2, 128), "seq": q}
    before = {"shard": lax.rem(s + 126, 128), "seq": q}
    return partner, before, after


def greet(targets):
    barrier = pltpu.get_barrier_semaphore()
    for target in targets:
        pl.semaphore_signal(barrier, inc=1, device_id=target, device_id_type=MESH)
    pl.semaphore_wait(barrier, len(targets))


def sending(src, dst, send, recv, target):
    return pltpu.make_async_remote_copy(
        src_ref=src, dst_ref=dst, send_sem=send, recv_sem=recv, device_id=target, device_id_type=MESH
    )


def neighbours(at):
    return [moved(at, **{d: step}) for d in ("x", "y", "z") for step in (1, -1)]


def octet_mates(me):
    across = dict(me)
    across["y"] = me["y"] + 1 - 2 * lax.rem(me["y"], 2)
    twin = moved(me, c=1)
    diagonal = dict(across)
    diagonal["c"] = twin["c"]
    return twin, across, diagonal


def span(index):
    return slice(None) if index is None else pl.ds(index, 1)


def picks_of(sets, gone=()):
    x, y, z = sets["x"], sets["y"], sets["z"]
    pick = {
        "x": x,
        "m": None if y is None else y // 2,
        "yp": None if y is None else lax.rem(y, 2),
        "zh": None if z is None else z // 2,
        "q": None if z is None else lax.rem(z, 2),
    }
    names = {"x": ("x",), "y": ("m", "yp"), "z": ("zh", "q")}
    for dim in gone:
        for name in names[dim]:
            pick[name] = 0
    return pick


WIDE_DIMS = ("yp", "q", "x", "zh", "m")
TALL_DIMS = ("x", "zh", "m", "yp", "q")
DIM_SIZE = {"yp": 2, "q": 2, "x": 4, "zh": 4, "m": 2}


def dims_of(k):
    return TALL_DIMS if k == 2 else WIDE_DIMS


def view(ref, k, part, sets, half=None, gone=(), lead=()):
    pick = picks_of(sets, gone)
    cut = (0, HALF) if half is None else HALVES[k][half]
    at = tuple(span(pick[d]) for d in dims_of(k))
    rows = () if part is None else (part,)
    return ref.at[(*lead, *at, *rows, slice(None), pl.ds(*cut))]


def find_docs(lengths, q_docs, k_docs):
    shard, seq = lax.axis_index("shard"), lax.axis_index("seq")
    stream_len = 128 * 2 * TILE
    row = lax.broadcasted_iota(jnp.int32, (128, 128), 0)
    column = lax.broadcasted_iota(jnp.int32, (128, 128), 1)
    wide = jnp.broadcast_to(lengths[...], (128, 128))
    starts_down = jnp.sum(jnp.where(column < row, wide, 0), axis=1, keepdims=True)
    lengths_down = jnp.sum(jnp.where(column == row, wide, 0), axis=1, keepdims=True)
    starts_across = jnp.sum(jnp.where(row < column, jnp.broadcast_to(lengths_down, (128, 128)), 0), axis=0, keepdims=True)
    origin = (shard // 2 - 1) * (4 * TILE)

    def tile(t, carry):
        at = origin + t * TILE + lax.broadcasted_iota(jnp.int32, (TILE, 1), 0)
        counted = jnp.sum((at >= starts_across).astype(jnp.int32), axis=1, keepdims=True) - 1
        k_docs[t] = jnp.where(at < stream_len, counted, stream_len)
        return carry

    lax.fori_loop(0, 12, tile, 0)
    for i in range(2):
        at = origin + (4 + seq + 2 * i) * TILE + lax.broadcasted_iota(jnp.int32, (1, TILE), 1)
        q_docs[i] = jnp.sum((starts_down <= at).astype(jnp.int32), axis=0, keepdims=True) - 1


def front_kernel(
    lengths, cat_ref, down_ref, vec_ref, tok_ref,
    first, second, third, rows_out, bias_in_out, window_out, kv_out, q_heads, o_heads, lse, attended,
    q_docs, k_docs,    land, stage, own, vecs, window, kv, w_heads, w_flat, top, total, acc,
    oct_s, oct_r, local, near_s, near_r, send, recv, core_s, core_r, vec_s, vec_r, tok_s, tok_r, keep, att_s, att_r,
):
    me = place()
    c, x, y, z = me["c"], me["x"], me["y"], me["z"]
    yp, q, m, zh = lax.rem(y, 2), lax.rem(z, 2), y // 2, z // 2
    outs = (first, second, third)
    twin, across, diagonal = octet_mates(me)
    twin_id = device_at(twin)
    partner, before, after = stream_mates()
    lines = [moved(me, **{d: o}) for d in EXTENT for o in OTHERS[d]]
    greet([device_at(a) for a in lines + [twin, diagonal]] + [before, after])

    def chunk_of(at):
        cols = (lax.rem(at["y"], 2) * 2 + q) * 768 + at["c"] * HALF
        return cat_ref.at[:, :, pl.ds(pl.multiple_of(cols, 128), HALF)]

    index = yp * 2 + c
    mates = (twin, across, diagonal)
    out = [
        sending(chunk_of(mate), land.at[:, index], oct_s.at[k], oct_r.at[k], device_at(mate))
        for k, mate in enumerate(mates)
    ]
    for cp in out:
        cp.start()
    kept = pltpu.make_async_copy(chunk_of(me), land.at[:, index], local.at[0])
    kept.start()
    gives = q == c
    down_out = sending(
        down_ref.at[:, :, pl.ds(pl.multiple_of((1 - c) * HALF, 128), HALF)], own.at[2], oct_s.at[3], oct_r.at[3], twin_id
    )
    down_kept = pltpu.make_async_copy(
        down_ref.at[:, :, pl.ds(pl.multiple_of(c * HALF, 128), HALF)], own.at[2], local.at[1]
    )

    @pl.when(gives)
    def _():
        down_out.start()
        down_kept.start()

    vec_kept = pltpu.make_async_copy(vec_ref, vecs.at[c, x, zh, y], local.at[2])
    vec_kept.start()

    sent = []

    def go(src, dst, send_sem, recv_sem, target):
        cp = sending(src, dst, send_sem, recv_sem, target)
        cp.start()
        sent.append(cp)

    def arrive(dst, send_sem, recv_sem, target):
        sending(dst, dst, send_sem, recv_sem, target).wait_recv()

    def tok_go(src, dst, at, target):
        go(src, dst, tok_s.at[at], tok_r.at[at], target)

    tok_kept = pltpu.make_async_copy(tok_ref, window.at[1, c, q], local.at[3])

    def tok_start():
        tok_kept.start()
        tok_go(tok_ref, window.at[1, c, q], 0, partner)
        tok_go(tok_ref, window.at[0, c, q], 1, after)
        tok_go(tok_ref, window.at[2, c, q], 2, before)
        tok_go(tok_ref, window.at[1, c, q], 3, twin_id)

    def tok_forward():
        theirs = window.at[1, c, 1 - q]
        arrive(theirs, tok_s.at[0], tok_r.at[0], partner)
        tok_go(theirs, window.at[0, c, 1 - q], 4, after)
        tok_go(theirs, window.at[2, c, 1 - q], 5, before)
        tok_go(theirs, window.at[1, c, 1 - q], 6, twin_id)

    def tok_share(h, first_slot, at):
        arrive(window.at[0, c, h], tok_s.at[first_slot], tok_r.at[first_slot], before)
        arrive(window.at[2, c, h], tok_s.at[first_slot + 1], tok_r.at[first_slot + 1], after)
        tok_go(window.at[0, c, h], window.at[0, c, h], at, twin_id)
        tok_go(window.at[2, c, h], window.at[2, c, h], at + 1, twin_id)

    vec_rounds = (("x", (1, 2, 3)), ("y", (1, 2, 3)), ("z", (2, 4, 6)), ("c", (1,)))

    def vec_copies(number, arriving):
        dim, steps = vec_rounds[number]
        done = [d for d, _ in vec_rounds[:number]]
        copies = []
        for k, step in enumerate(steps):
            source = moved(me, **{dim: (1 if dim == "c" else -step)}) if arriving else me
            pick = [None if d in done else (source["z"] // 2 if d == "z" else source[d]) for d in ("c", "x", "z", "y")]
            ref = vecs.at[tuple(span(p) for p in pick)]
            copies.append(
                sending(ref, ref, vec_s.at[number, k], vec_r.at[number, k], device_at(moved(me, **{dim: step})))
            )
        return copies

    def vec_start(number):
        for cp in vec_copies(number, False):
            cp.start()
            sent.append(cp)

    def vec_wait(number):
        for cp in vec_copies(number, True):
            cp.wait_recv()

    kept.wait()
    for k, mate in enumerate(mates):
        mate_index = lax.rem(mate["y"], 2) * 2 + mate["c"]
        arrive(land.at[:, mate_index], oct_s.at[k], oct_r.at[k], device_at(mate))
    for k in range(2):
        for owner in range(4):
            stage[pl.ds(6 * owner, 6), :] = land[k, owner].astype(jnp.float32)
        for part in range(3):
            own[k, part] = stage[pl.ds(8 * part, 8), :].astype(jnp.bfloat16)

    @pl.when(gives)
    def _():
        down_kept.wait()

    @pl.when(jnp.logical_not(gives))
    def _():
        down_out.wait_recv()

    homes = (first.at[c, yp, q, x, zh, m], second.at[c, yp, q, x, zh, m], third.at[c, x, zh, m, yp, q])
    flush = [pltpu.make_async_copy(own.at[k], homes[k], local.at[4 + k]) for k in STREAMS]
    for cp in flush:
        cp.start()
    twins = []

    def share(k, part, sets, half, slot):
        mine = view(outs[k], k, part, sets, half, (), (c,))
        theirs = view(outs[k], k, part, sets, half, (), (1 - c,))
        go(mine, mine, core_s.at[slot, k], core_r.at[slot, k], twin_id)
        twins.append((theirs, core_s.at[slot, k], core_r.at[slot, k]))

    def sets_at(part, phase, index):
        sets = {"x": x, "y": y, "z": z}
        for earlier in ORDERS[part][:phase]:
            sets[earlier] = None
        dim = ORDERS[part][phase]
        sets[dim] = lax.rem(index + EXTENT[dim], EXTENT[dim])
        return sets

    def near(k, part, phase, arriving):
        dim = ORDERS[part][phase]
        for o in OTHERS[dim]:
            sems = near_s.at[part, phase, o, k], near_r.at[part, phase, o, k]
            target = device_at(moved(me, **{dim: o}))
            if arriving:
                arrive(view(outs[k], k, part, sets_at(part, phase, me[dim] - o), None, (), (c,)), *sems, target)
            elif phase == 0:
                go(own.at[k, part], homes[k].at[part], *sems, target)
            else:
                ref = view(outs[k], k, part, sets_at(part, phase, me[dim]), None, (), (c,))
                go(ref, ref, *sems, target)

    def ring(k, part, step, arriving):
        dim = ORDERS[part][2]
        size = EXTENT[dim]
        for direction, sign in enumerate((1, -1)):
            sets = sets_at(part, 2, me[dim] - sign * (step if arriving else step - 1))
            half = direction if step == size // 2 else None
            ref = view(outs[k], k, part, sets, half, (), (c,))
            slot = part * 2 + step - 1
            sems = send.at[slot, direction, k], recv.at[slot, direction, k]
            target = device_at(moved(me, **{dim: sign}))
            if arriving:
                arrive(ref, *sems, target)
            else:
                go(ref, ref, *sems, target)

    def ring_share(k, part, step):
        dim = ORDERS[part][2]
        for direction, sign in enumerate((1, -1)):
            half = direction if step == EXTENT[dim] // 2 else None
            share(k, part, sets_at(part, 2, me[dim] - sign * step), half, 3 + (part * 2 + step - 1) * 2 + direction)

    parts = range(3)
    late = [(k, part) for k in (1, 2) for part in parts]
    for part in parts:
        near(0, part, 0, False)
    vec_kept.wait()
    vec_start(0)
    for k, part in late:
        near(k, part, 0, False)
    find_docs(lengths, q_docs, k_docs)
    for cp in flush:
        cp.wait()
    for part in parts:
        near(0, part, 0, True)
        near(0, part, 1, False)
    tok_start()
    vec_wait(0)
    vec_start(1)
    for part in parts:
        near(0, part, 1, True)
        ring(0, part, 1, False)
    for k, part in late:
        near(k, part, 0, True)
        near(k, part, 1, False)
    vec_wait(1)
    vec_start(2)
    tok_forward()
    for part in parts:
        ring(0, part, 1, True)
        ring(0, part, 2, False)
    vec_wait(2)
    vec_start(3)
    for k, part in late:
        near(k, part, 1, True)
        ring(k, part, 1, False)
    for k, part in late:
        share(k, part, sets_at(part, 2, me[ORDERS[part][2]]), None, part)
    vec_wait(3)
    for v in range(8):
        rows_out[v : v + 1] = jnp.zeros((1, 768), jnp.float32)
    lane = lax.broadcasted_iota(jnp.int32, (128, HALF), 0)
    line = lax.broadcasted_iota(jnp.int32, (512, HALF), 0)
    values = [vecs[owner_core].reshape(512, 128).astype(jnp.bfloat16) for owner_core in range(2)]
    for h in range(2):
        column = h * HALF + lax.broadcasted_iota(jnp.int32, (1, HALF), 1)
        cols = slice(h * HALF, (h + 1) * HALF)
        for owner_core in range(2):
            place_in = lax.rem(column, 12) - 6 * owner_core
            picked = dot32(values[owner_core], jnp.logical_and(lane == place_in, lane < 6).astype(jnp.bfloat16))
            for v in range(8):
                rows_out[v : v + 1, cols] += row_sum(jnp.where(line == column // 12 * 8 + v, picked, 0.0))

    def hidden_row(m, carry):
        column = m * HALF + lax.broadcasted_iota(jnp.int32, (1, HALF), 1)
        total = jnp.zeros((1, HALF), jnp.float32)
        for owner_core in range(2):
            place_in = lax.rem(column, 48) - 24 * owner_core
            inside = jnp.logical_and(place_in >= 0, place_in < 24)
            picked = dot32(values[owner_core], jnp.logical_and(lane == place_in + 6, inside).astype(jnp.bfloat16))
            total = total + row_sum(jnp.where(line == column // 48 * 8, picked, 0.0))
        bias_in_out[m] = total
        return carry

    lax.fori_loop(0, 8, hidden_row, 0)
    for part in parts:
        ring(0, part, 2, True)
    load = pltpu.make_async_copy(first.at[c, pl.ds(0, 2), pl.ds(0, 2)], w_heads, keep.at[1])
    load.start()
    go(first.at[c, 1, 1], first.at[c, 1, 1], core_s.at[0, 0], core_r.at[0, 0], twin_id)
    twins.append((first.at[1 - c, 1, 1], core_s.at[0, 0], core_r.at[0, 0]))

    own_half = pl.ds(pl.multiple_of(c * HALF, 128), HALF)
    bias = [rows_out[v : v + 1, own_half] for v in range(2)]
    arrive(window.at[1, 1 - c, q], tok_s.at[3], tok_r.at[3], twin_id)
    arrive(window.at[1, 1 - c, 1 - q], tok_s.at[6], tok_r.at[6], twin_id)
    tok_kept.wait()
    load.wait()

    def project_group(group):
        def one(n, carry):
            core, h = n // 2, lax.rem(n, 2)
            x_tile, t = window[group, core, h], group * 4 + n
            kv[0, t] = dot32(x_tile, weights(1)).astype(jnp.bfloat16)
            kv[1, t] = (dot32(x_tile, weights(2)) + bias[1]).astype(jnp.bfloat16)
            return carry

        lax.fori_loop(0, 4, one, 0)

    def flatten(i, carry):
        rows = pl.ds(pl.multiple_of(i * 192, 192), 192)
        for number in range(3):
            piece = w_heads[number // 2, number % 2, i].astype(jnp.float32)
            w_flat[number, rows] = piece.reshape(192, HALF).astype(jnp.bfloat16)
        return carry

    lax.fori_loop(0, 4, flatten, 0)

    def weights(number):
        return w_flat[number]

    low = lanes_low(TILE)
    scale = HEAD_DIM ** -0.5 * LOG2E

    def heads_front(pair, i, near_by):
        cols = slice(pair * 128, (pair + 1) * 128)
        at = pair * 2 + i
        qs = q_heads[i, :, cols]
        none = jnp.zeros_like(qs)
        queries = (jnp.where(low, qs, none), jnp.where(low, none, qs))
        if near_by:
            top[at] = jnp.full((2, 1, TILE), BOTTOM, jnp.float32)
            total[at] = jnp.zeros((2, 1, TILE), jnp.float32)
            acc[at] = jnp.zeros((128, TILE), jnp.float32)

        def step(n, carry):
            u = q + 2 * i + n
            t = 4 + n if near_by else u + 4 * (u // 4)
            k, v = kv[0, t, :, cols], flipped(kv[1, t, :, cols])
            same = q_docs[i] == k_docs[t]
            scores = [jnp.where(same, across_lanes(k, queries[head]) * scale, BOTTOM) for head in range(2)]
            old = [top[at, head] for head in range(2)]
            new = [jnp.maximum(old[head], jnp.max(scores[head], axis=0, keepdims=True)) for head in range(2)]
            fade = [jnp.exp2(old[head] - new[head]) for head in range(2)]
            p = [jnp.exp2(scores[head] - new[head]) for head in range(2)]
            sums = [total[at, head] * fade[head] + jnp.sum(p[head], axis=0, keepdims=True) for head in range(2)]
            adds = [dot32(v[head * HEAD_DIM : (head + 1) * HEAD_DIM], p[head].astype(jnp.bfloat16)) for head in range(2)]
            for head in range(2):
                rows = slice(head * HEAD_DIM, (head + 1) * HEAD_DIM)
                acc[at, rows] = acc[at, rows] * fade[head] + adds[head]
                total[at, head] = sums[head]
                top[at, head] = new[head]
            return carry

        lax.fori_loop(0, 4 if near_by else 5, step, 0)
        if not near_by:
            for head in range(2):
                rows = slice(head * HEAD_DIM, (head + 1) * HEAD_DIM)
                acc[at, rows] = acc[at, rows] / total[at, head]
                lse[pair, i, head : head + 1] = top[at, head] + jnp.log2(total[at, head])
            o_heads[i, :, cols] = flipped(acc[at]).astype(jnp.bfloat16)

    for i in range(2):
        q_heads[i] = (dot32(window[1, i, q], weights(0)) + bias[0]).astype(jnp.bfloat16)
    project_group(1)
    for pair in range(3):
        heads_front(pair, 0, True)
    tok_share(q, 1, 7)
    for pair in range(3):
        heads_front(pair, 1, True)
    tok_share(1 - q, 4, 9)
    for part in parts:
        ring(1, part, 1, True)
        ring(1, part, 2, False)
    for h, at in ((q, 7), (1 - q, 9)):
        arrive(window.at[0, 1 - c, h], tok_s.at[at], tok_r.at[at], twin_id)
        arrive(window.at[2, 1 - c, h], tok_s.at[at + 1], tok_r.at[at + 1], twin_id)
    kept_window = pltpu.make_async_copy(window, window_out, keep.at[2])
    kept_window.start()
    project_group(0)
    for part in parts:
        ring(2, part, 1, True)
        ring(2, part, 2, False)
    project_group(2)
    kept_kv = pltpu.make_async_copy(kv, kv_out, keep.at[3])
    kept_kv.start()
    for part in parts:
        ring_share(1, part, 1)
    heads_front(0, 0, False)
    heads_front(1, 0, False)
    for part in parts:
        ring_share(2, part, 1)
    heads_front(2, 0, False)
    for part in parts:
        ring(1, part, 2, True)
        ring_share(1, part, 2)
    heads_front(0, 1, False)
    heads_front(1, 1, False)
    heads_front(2, 1, False)
    mine_cols, other_cols = (pl.ds(pl.multiple_of(a * HALF, 128), HALF) for a in (c, 1 - c))
    go(o_heads.at[1 - c], attended.at[:, mine_cols], att_s.at[0], att_r.at[0], twin_id)
    kept_att = pltpu.make_async_copy(o_heads.at[c], attended.at[:, mine_cols], keep.at[4])
    kept_att.start()
    for part in parts:
        ring(2, part, 2, True)
        ring_share(2, part, 2)
    for ref, send_sem, recv_sem in twins:
        arrive(ref, send_sem, recv_sem, twin_id)
    arrive(attended.at[:, other_cols], att_s.at[0], att_r.at[0], twin_id)
    for cp in (kept_window, kept_kv, kept_att):
        cp.wait()
    for cp in out + sent:
        cp.wait_send()

    @pl.when(gives)
    def _():
        down_out.wait_send()


def front(lengths, cat, down, vec, tokens):
    bf, f32, dma = jnp.bfloat16, jnp.float32, pltpu.SemaphoreType.DMA
    return pl.pallas_call(
        front_kernel,
        name="front",
        out_shape=(
            jax.ShapeDtypeStruct((2, *WIDE), bf),
            jax.ShapeDtypeStruct((2, *WIDE), bf),
            jax.ShapeDtypeStruct((2, *TALL), bf),
            jax.ShapeDtypeStruct((8, 768), f32),
            jax.ShapeDtypeStruct((8, 1, HALF), f32),
            jax.ShapeDtypeStruct((3, 2, 2, TILE, 768), bf),
            jax.ShapeDtypeStruct((2, 12, TILE, HALF), bf),
            jax.ShapeDtypeStruct((2, TILE, HALF), bf),
            jax.ShapeDtypeStruct((2, TILE, HALF), bf),
            jax.ShapeDtypeStruct((3, 2, 2, TILE), f32),
            jax.ShapeDtypeStruct((TILE, 768), bf),
        ),
        in_specs=[IN_VMEM] + [ANY_SPACE] * 4,
        out_specs=(ANY_SPACE,) * 3 + (IN_VMEM,) * 2 + (ANY_SPACE,) * 2 + (IN_VMEM,) * 4,
        scratch_shapes=[
            pltpu.VMEM((2, 1, TILE), jnp.int32),
            pltpu.VMEM((12, TILE, 1), jnp.int32),
            pltpu.VMEM((2, 4, 6, HALF), bf),
            pltpu.VMEM((24, HALF), f32),
            pltpu.VMEM((3, 3, 8, HALF), bf),
            pltpu.VMEM((2, 4, 4, 4, 8, 128), f32),
            pltpu.VMEM((3, 2, 2, TILE, 768), bf),
            pltpu.VMEM((2, 12, TILE, HALF), bf),
            pltpu.VMEM((2, 2, 4, 4, 2, 3, 8, HALF), bf),
            pltpu.VMEM((3, 768, HALF), bf),
            pltpu.VMEM((6, 2, 1, TILE), f32),
            pltpu.VMEM((6, 2, 1, TILE), f32),
            pltpu.VMEM((6, 128, TILE), f32),
            dma((4,)), dma((4,)), dma((7,)), dma((3, 2, 8, 3)), dma((3, 2, 8, 3)), dma((6, 2, 3)), dma((6, 2, 3)),
            dma((15, 3)), dma((15, 3)), dma((4, 3)), dma((4, 3)), dma((11,)), dma((11,)), dma((5,)), dma((1,)), dma((1,)),
        ],
        compiler_params=pltpu.CompilerParams(collective_id=1, has_side_effects=True, vmem_limit_bytes=62 << 20),
    )(lengths, cat, down, vec, tokens)


def back_kernel(*refs):
    (lengths, q_ref, o_ref, lse_ref, gv, d_att, kv_hbm, window_hbm, first, dwo, g1, g2, base) = refs[:13]
    (out0, out1, out2, out_v, out_tok) = refs[13:18]
    grads = (None, g1, g2)
    refs = refs[18:]
    acc, other, refs = refs[:3], refs[3:6], refs[6:]
    lands = {}
    for n, (part, phase, k) in enumerate((a, b, k) for a in range(3) for b in range(3) for k in STREAMS):
        lands[part, phase, k] = refs[n]
    refs = refs[27:]
    (
        stage, rows, tall_f, v_c, v_x, v_y, v_z, t_all, t_in, t_land, t_part, t_mate, t_base,
        kv, window, w_heads, dkv_all, dkv, dq_all, dq_acc, dw, q_rows, v_rows, q_docs, k_docs, do_ref,
        local, core_s, core_r, near_s, near_r, send, recv, fin_s, fin_r, t_s, t_r, vec_s, vec_r, tok_s, tok_r, tok_l, load, att_s, att_r,
    ) = refs
    me = place()
    c, x, y, z = me["c"], me["x"], me["y"], me["z"]
    yp, q, m, zh = lax.rem(y, 2), lax.rem(z, 2), y // 2, z // 2
    twin, across, diagonal = octet_mates(me)
    twin_id = device_at(twin)
    partner, before, after = stream_mates()

    def other_q(at):
        new = dict(at)
        new["z"] = at["z"] + 1 - 2 * lax.rem(at["z"], 2)
        return new

    ring_mates = [moved(me, **{d: k}) for d in ("x", "y", "z") for k in range(1, EXTENT[d])]
    mates = [twin, across, diagonal] + [other_q(a) for a in (me, twin, across, diagonal)]
    targets = ring_mates + [twin, diagonal] + [other_q(a) for a in (twin, across, diagonal)]
    greet([device_at(a) for a in targets] + [before, after])
    sent = []

    def go(src, dst, send_sem, recv_sem, target):
        cp = sending(src, dst, send_sem, recv_sem, target)
        cp.start()
        sent.append(cp)

    def arrive(dst, send_sem, recv_sem, target):
        sending(dst, dst, send_sem, recv_sem, target).wait_recv()

    def sets_of(k, part, phase, index):
        sets = {"x": x, "y": y, "z": z}
        order = SUM_ORDERS[k][part]
        for later in order[phase + 1:]:
            sets[later] = None
        sets[order[phase]] = lax.rem(index + 2 * EXTENT[order[phase]], EXTENT[order[phase]])
        return sets

    def add_region(k, part, sets, sources, half=None, gone=()):
        pick, from_pick = picks_of(sets), picks_of(sets, gone)
        dims = dims_of(k)
        inner = dims[3:] if k < 2 else dims[2:]
        outer = [d for d in dims if d not in inner and pick[d] is None]
        count = 1
        for d in outer:
            count *= DIM_SIZE[d]
        cut = pl.ds(*((0, HALF) if half is None else HALVES[k][half]))

        def one(i):
            at = {}
            for d in reversed(outer):
                at[d] = lax.rem(i, DIM_SIZE[d]) if count > 1 else 0
                i = i // DIM_SIZE[d]

            def index(picked):
                return tuple(
                    (at[d] if d in at else slice(None)) if picked[d] is None else pl.ds(picked[d], 1) if d in inner else picked[d]
                    for d in dims
                )

            to = (*index(pick), part, slice(None), cut)
            fr = (*index(from_pick), slice(None), cut)
            if len(sources) == 1:
                acc[k][to] = acc[k][to] + sources[0][fr]
            else:
                total = acc[k][to].astype(jnp.float32)
                for src in sources:
                    total = total + src[fr].astype(jnp.float32)
                acc[k][to] = total.astype(jnp.bfloat16)

        if count == 1:
            one(0)
        else:
            lax.fori_loop(0, count, lambda i, carry: (one(i), carry)[1], 0)

    def hop(k, part, n):
        return sets_of(k, part, 0, me[SUM_ORDERS[k][part][0]] + (2, 1, -1, 0)[n])

    own_copies = {}

    def cross(k, part, n):
        slot = part * 4 + n
        sets = hop(k, part, n)
        src = view(grads[k], k, part, sets, None, (), (1 - c,))
        go(src, view(other[k], k, part, sets), core_s.at[slot, k], core_r.at[slot, k], twin_id)
        kept = pltpu.make_async_copy(
            view(grads[k], k, part, sets, None, (), (c,)), view(acc[k], k, part, sets), local.at[slot, k]
        )
        kept.start()
        own_copies[k, part, n] = kept

    loads = [
        pltpu.make_async_copy(kv_hbm, kv, load.at[0]),
        pltpu.make_async_copy(first.at[c, pl.ds(0, 3)], w_heads, load.at[1]),
        pltpu.make_async_copy(window_hbm, window, load.at[2]),
        pltpu.make_async_copy(dwo.at[c], acc[0].at[1, 1], load.at[3]),
        pltpu.make_async_copy(base, t_base, load.at[4]),
    ]
    loads[0].start()
    own_half, other_half = (pl.ds(pl.multiple_of(a * HALF, 128), HALF) for a in (c, 1 - c))
    go(d_att.at[:, other_half], do_ref.at[c], att_s.at[0], att_r.at[0], twin_id)
    d_kept = pltpu.make_async_copy(d_att.at[:, own_half], do_ref.at[c], load.at[5])
    d_kept.start()
    for n in range(4):
        for k in (1, 2):
            for part in range(3):
                cross(k, part, n)

    for cp in loads[1:]:
        cp.start()
    go(dwo.at[1 - c], other[0], core_s.at[0, 0], core_r.at[0, 0], twin_id)

    vec_lands = (v_c, v_x, v_y, v_z)
    vec_dims = ("c", "x", "y", "z")

    def vec_start(number):
        dim, land = vec_dims[number], vec_lands[number]
        for k in range(1, land.shape[0]):
            mine = land.at[me[dim]]
            go(mine, mine, vec_s.at[number, k], vec_r.at[number, k], device_at(moved(me, **{dim: k})))

    def vec_finish(number):
        dim, land = vec_dims[number], vec_lands[number]
        size = land.shape[0]
        for k in range(1, size):
            theirs = land.at[lax.rem(me[dim] - k + size, size)]
            arrive(theirs, vec_s.at[number, k], vec_r.at[number, k], device_at(moved(me, **{dim: k})))
        total = land[0]
        for k in range(1, size):
            total = total + land[k]
        return total

    def row_blocks(fn):
        lax.fori_loop(0, TILE // 32, lambda r, carry: (fn(pl.ds(pl.multiple_of(r * 32, 32), 32)), carry)[1], 0)

    def tok_twin(group, at):
        go(t_all.at[1 - c, group], t_in.at[group], tok_s.at[at], tok_r.at[at], twin_id)

    def tok_edges():
        for n, (group, at) in enumerate(((0, 0), (2, 6))):
            arrive(t_in.at[group], tok_s.at[at], tok_r.at[at], twin_id)
        for n, h in enumerate((1 - q, q)):
            for group in (0, 2):
                def one(at):
                    t_all[c, group, h, at] = t_all[c, group, h, at] + t_in[group, h, at]
                row_blocks(one)
            go(t_all.at[c, 0, h], t_land.at[1, h], tok_s.at[1 + n], tok_r.at[1 + n], before)
            go(t_all.at[c, 2, h], t_land.at[0, h], tok_s.at[3 + n], tok_r.at[3 + n], after)

    def tok_total(h, at):
        f = jnp.float32
        return t_all[c, 1, h, at].astype(f) + t_in[1, h, at].astype(f) + t_land[0, h, at].astype(f) + t_land[1, h, at].astype(f)

    def tok_theirs():
        h = 1 - q
        arrive(t_in.at[1], tok_s.at[7], tok_r.at[7], twin_id)
        arrive(t_land.at[1, h], tok_s.at[1], tok_r.at[1], after)
        arrive(t_land.at[0, h], tok_s.at[3], tok_r.at[3], before)

        def one(at):
            t_part[at] = tok_total(h, at).astype(jnp.bfloat16)
        row_blocks(one)
        go(t_part, t_mate, tok_s.at[5], tok_r.at[5], partner)

    def tok_mine():
        arrive(t_land.at[1, q], tok_s.at[2], tok_r.at[2], after)
        arrive(t_land.at[0, q], tok_s.at[4], tok_r.at[4], before)
        arrive(t_mate, tok_s.at[5], tok_r.at[5], partner)
        loads[4].wait()

        def one(at):
            t_base[at] = tok_total(q, at) + t_mate[at].astype(jnp.float32) + t_base[at]
        row_blocks(one)
        done = pltpu.make_async_copy(t_base, out_tok, tok_l.at[0])
        done.start()
        return done

    def meet(k, part, n):
        slot = part * 4 + n
        own_copies[k, part, n].wait()
        sets = hop(k, part, n)
        arrive(view(other[k], k, part, sets), core_s.at[slot, k], core_r.at[slot, k], twin_id)
        add_region(k, part, sets, [other[k].at[(slice(None),) * 5 + (part,)]])

    def meet_out():
        loads[3].wait()
        arrive(other[0], core_s.at[0, 0], core_r.at[0, 0], twin_id)

        def one(i, carry):
            acc[0][1, 1, i] = acc[0][1, 1, i] + other[0][i]
            return carry

        lax.fori_loop(0, 4, one, 0)

    def ring(k, part, step, arriving):
        dim = SUM_ORDERS[k][part][0]
        ahead = 3 - step - (1 if arriving else 0)
        for direction, sign in enumerate((1, -1)):
            half = direction if step == 1 else None
            sets = sets_of(k, part, 0, me[dim] + sign * ahead)
            land = lands[part, 0, k].at[direction, step - 1]
            slot = part * 2 + step - 1
            sems = send.at[slot, direction, k], recv.at[slot, direction, k]
            target = device_at(moved(me, **{dim: sign}))
            here = view(land, k, None, sets, half, (dim,))
            if arriving:
                arrive(here, *sems, target)
                add_region(k, part, sets, [land], half, (dim,))
            else:
                go(view(acc[k], k, part, sets, half), here, *sems, target)

    def near(k, part, phase, arriving):
        order = SUM_ORDERS[k][part]
        dim, gone = order[phase], order[: phase + 1]
        mine = sets_of(k, part, phase, me[dim])
        sources = []
        for o in OTHERS[dim]:
            sems = near_s.at[part, phase - 1, o, k], near_r.at[part, phase - 1, o, k]
            target = device_at(moved(me, **{dim: o}))
            land = lands[part, phase, k].at[o - 1]
            here = view(land, k, None, mine, None, gone)
            if arriving:
                arrive(here, *sems, target)
                sources.append(land)
            else:
                go(view(acc[k], k, part, sets_of(k, part, phase, me[dim] + o)), here, *sems, target)
        if arriving:
            add_region(k, part, mine, sources, None, gone)

    def vec_next(n):
        total = vec_finish(n)
        if n < 3:
            vec_lands[n + 1][me[vec_dims[n + 1]]] = total
            vec_start(n + 1)
        else:
            out_v[...] = total

    low = lanes_low(TILE)
    scale = HEAD_DIM ** -0.5 * LOG2E
    picker = (
        lax.broadcasted_iota(jnp.int32, (8, 128), 0) == lax.broadcasted_iota(jnp.int32, (8, 128), 1) // HEAD_DIM
    ).astype(jnp.float32)

    def heads_back(pair, i, near_by):
        cols = slice(pair * 128, (pair + 1) * 128)
        place_at = pair * 2 + i
        qs, d_out = q_ref[i, :, cols], do_ref[i, :, cols]
        none = jnp.zeros_like(qs)
        q_heads = (jnp.where(low, qs, none), jnp.where(low, none, qs))
        do_heads = (jnp.where(low, d_out, none), jnp.where(low, none, d_out))
        prod = d_out.astype(jnp.float32) * o_ref[i, :, cols].astype(jnp.float32)
        deltas = lax.dot_general(
            picker, prod, (((1,), (1,)), ((), ())), precision=lax.Precision.HIGHEST, preferred_element_type=jnp.float32
        )
        if i == 0:
            dkv[...] = jnp.zeros_like(dkv)
        if not near_by:
            dq_acc[place_at] = jnp.zeros((128, TILE), jnp.float32)

        def step(n, carry):
            u = q + 2 * i + n
            t = 4 + n if near_by else u + 4 * (u // 4)
            slot = n if near_by else u
            k, v = kv[0, t, :, cols], kv[1, t, :, cols]
            k_flip = flipped(k)
            same = q_docs[i] == k_docs[t]
            heads = range(2)
            scores = [across_lanes(k, q_heads[h]) * scale for h in heads]
            dp = [across_lanes(v, do_heads[h]) for h in heads]
            p = [jnp.where(same, jnp.exp2(scores[h] - lse_ref[pair, i, h : h + 1]), 0.0) for h in heads]
            ds = [(p[h] * (dp[h] - deltas[h : h + 1])).astype(jnp.bfloat16) for h in heads]
            p_low = [p[h].astype(jnp.bfloat16) for h in heads]
            dq = [dot32(k_flip[h * HEAD_DIM : (h + 1) * HEAD_DIM], ds[h]) for h in heads]
            dk = [dot32(ds[h], q_heads[h]) for h in heads]
            dv = [dot32(p_low[h], do_heads[h]) for h in heads]
            for h in heads:
                lanes = slice(h * HEAD_DIM, (h + 1) * HEAD_DIM)
                dq_acc[place_at, lanes] = dq_acc[place_at, lanes] + dq[h]
            dkv[0, slot] = dkv[0, slot] + (dk[0] + dk[1])
            dkv[1, slot] = dkv[1, slot] + (dv[0] + dv[1])
            return carry

        lax.fori_loop(0, 4 if near_by else 5, step, 0)
        if near_by:
            dq_all[i, :, cols] = flipped(dq_acc[place_at] * HEAD_DIM ** -0.5).astype(jnp.bfloat16)
        if i == 1:
            def keep(u, carry):
                t = 4 + u if near_by else u + 4 * (u // 4)
                dkv_all[0, t, :, cols] = (dkv[0, u] * HEAD_DIM ** -0.5).astype(jnp.bfloat16)
                dkv_all[1, t, :, cols] = dkv[1, u].astype(jnp.bfloat16)
                return carry

            lax.fori_loop(0, 4 if near_by else 8, keep, 0)

    def tile_back(group, n):
        core, h = n // 2, lax.rem(n, 2)
        t = group * 4 + n
        x_flip = flipped(window[t])
        dk, dv = dkv_all[0, t], dkv_all[1, t]
        dw[1] += dot32(x_flip, dk)
        dw[2] += dot32(x_flip, dv)
        v_rows[...] = v_rows[...] + jnp.sum(dv.astype(jnp.float32), axis=0, keepdims=True)
        dx = across_lanes(dk, w_heads[1]) + across_lanes(dv, w_heads[2])
        t_all[core, group, h] = dx.astype(jnp.bfloat16)
        if group == 1:
            @pl.when(h == q)
            def _():
                dq = dq_all[core]
                dw[0] += dot32(x_flip, dq)
                q_rows[...] = q_rows[...] + jnp.sum(dq.astype(jnp.float32), axis=0, keepdims=True)
                t_all[core, group, h] = (dx + across_lanes(dq, w_heads[0])).astype(jnp.bfloat16)

    def tiles_back(group):
        lax.fori_loop(0, 4, lambda n, carry: (tile_back(group, n), carry)[1], 0)

    parts = range(3)
    late = [(k, part) for k in (1, 2) for part in parts]
    find_docs(lengths, q_docs, k_docs)
    for k, part in late:
        meet(k, part, 0)
        ring(k, part, 1, False)
    loads[0].wait()
    d_kept.wait()
    arrive(do_ref.at[1 - c], att_s.at[0], att_r.at[0], twin_id)
    heads_back(0, 0, False)
    for k, part in late:
        meet(k, part, 1)
        meet(k, part, 2)
    for part in parts:
        ring(1, part, 1, True)
        ring(1, part, 2, False)
    heads_back(0, 1, False)
    for part in parts:
        ring(2, part, 1, True)
        ring(2, part, 2, False)
    heads_back(1, 0, False)
    for k, part in late:
        meet(k, part, 3)
    meet_out()
    heads_back(1, 1, False)
    heads_back(2, 0, False)
    for part in parts:
        ring(1, part, 2, True)
        near(1, part, 1, False)
    heads_back(2, 1, False)
    loads[1].wait()
    loads[2].wait()
    dw[...] = jnp.zeros_like(dw)
    q_rows[...] = jnp.zeros_like(q_rows)
    v_rows[...] = jnp.zeros_like(v_rows)
    tiles_back(0)
    tok_twin(0, 0)
    tiles_back(2)
    tok_twin(2, 6)
    for part in parts:
        ring(2, part, 2, True)
        near(2, part, 1, False)
    heads_back(0, 0, True)
    heads_back(0, 1, True)
    for part in parts:
        near(1, part, 1, True)
        near(1, part, 2, False)
    heads_back(1, 0, True)
    heads_back(1, 1, True)
    for part in parts:
        near(2, part, 1, True)
        near(2, part, 2, False)
    heads_back(2, 0, True)
    heads_back(2, 1, True)
    for k, part in late:
        near(k, part, 2, True)
    tok_edges()
    tiles_back(1)
    tok_twin(1, 7)

    def grads_low(i, carry):
        rows_at = pl.ds(pl.multiple_of(i * 192, 192), 192)
        for number, (a, b) in enumerate(((0, 0), (0, 1), (1, 0))):
            acc[0][a, b, i] = dw[number, rows_at].reshape(4, 2, 3, 8, HALF).astype(jnp.bfloat16)
        return carry

    lax.fori_loop(0, 4, grads_low, 0)
    for part in parts:
        ring(0, part, 1, False)
    v_c[c] = gv[...]
    half_cols = pl.ds(pl.multiple_of(c * HALF, 128), HALF)
    v_c[c, 0:1, half_cols] = q_rows[...]
    v_c[c, 1:2, half_cols] = v_rows[...]
    vec_start(0)
    vec_next(0)
    tok_theirs()
    for part in parts:
        ring(0, part, 1, True)
        ring(0, part, 2, False)
    vec_next(1)
    for part in parts:
        ring(0, part, 2, True)
        near(0, part, 1, False)
    vec_next(2)
    for part in parts:
        near(0, part, 1, True)
        near(0, part, 2, False)
    vec_next(3)
    for part in parts:
        near(0, part, 2, True)

    for k in range(2):
        for part in range(3):
            stage[pl.ds(8 * part, 8), :] = acc[k][yp, q, x, zh, m, part].astype(jnp.float32)
        for owner in range(4):
            rows[k, owner] = stage[pl.ds(6 * owner, 6), :]
    for part in range(3):
        tall_f[part] = acc[2][x, zh, m, yp, q, part].astype(jnp.float32)

    def cols_at(at):
        return pl.ds(pl.multiple_of((lax.rem(at["y"], 2) * 2 + lax.rem(at["z"], 2)) * 768 + at["c"] * HALF, 128), HALF)

    def owner_of(at):
        return lax.rem(at["y"], 2) * 2 + at["c"]

    for k, out in enumerate((out0, out1)):
        for n, mate in enumerate(mates):
            go(rows.at[k, owner_of(mate)], out.at[:, cols_at(me)], fin_s.at[k, n], fin_r.at[k, n], device_at(mate))
    kept = [
        pltpu.make_async_copy(rows.at[k, owner_of(me)], out.at[:, cols_at(me)], fin_s.at[k, 7])
        for k, out in enumerate((out0, out1))
    ]
    for cp in kept:
        cp.start()
    stays = c == q
    half_at = [pl.ds(pl.multiple_of(a * HALF, 128), HALF) for a in (c, 1 - c)]
    t_self = pltpu.make_async_copy(tall_f, out2.at[:, :, half_at[0]], t_s.at[0])
    there_same, there_cross = device_at(other_q(me)), device_at(other_q(twin))
    t_twin = sending(tall_f, out2.at[:, :, half_at[0]], t_s.at[0], t_r.at[0], twin_id)
    t_same = sending(tall_f, out2.at[:, :, half_at[0]], t_s.at[1], t_r.at[1], there_same)
    t_cross = sending(tall_f, out2.at[:, :, half_at[0]], t_s.at[1], t_r.at[2], there_cross)

    @pl.when(stays)
    def _():
        t_self.start()
        t_same.start()

    @pl.when(jnp.logical_not(stays))
    def _():
        t_twin.start()
        t_cross.start()

    for k, out in enumerate((out0, out1)):
        for n, mate in enumerate(mates):
            arrive(out.at[:, cols_at(mate)], fin_s.at[k, n], fin_r.at[k, n], device_at(mate))

    @pl.when(stays)
    def _():
        arrive(out2.at[:, :, half_at[1]], t_s.at[0], t_r.at[0], twin_id)
        t_self.wait()
        t_same.wait_send()

    @pl.when(jnp.logical_not(stays))
    def _():
        arrive(out2.at[:, :, half_at[0]], t_s.at[1], t_r.at[1], there_same)
        arrive(out2.at[:, :, half_at[1]], t_s.at[1], t_r.at[2], there_cross)
        t_twin.wait_send()
        t_cross.wait_send()

    tok_mine().wait()
    for cp in kept:
        cp.wait()
    for cp in sent:
        cp.wait_send()


def back(lengths, q_heads, o_heads, lse, gv, d_att, kv, window, first, dwo, g1, g2, base):
    bf, f32, dma = jnp.bfloat16, jnp.float32, pltpu.SemaphoreType.DMA
    lands = []
    for part in range(3):
        for phase in range(3):
            for k in STREAMS:
                order = SUM_ORDERS[k][part]
                size = dict(DIM_SIZE)
                for dim, names in (("x", ("x",)), ("y", ("m", "yp")), ("z", ("zh", "q"))):
                    if dim in order[: phase + 1]:
                        for name in names:
                            size[name] = 1
                count = (2, 2) if phase == 0 else (EXTENT[order[phase]] - 1,)
                lands.append(pltpu.VMEM((*count, *(size[d] for d in dims_of(k)), 8, HALF), bf))
    whole = [pltpu.VMEM(WIDE, bf), pltpu.VMEM(TALL, bf)]
    return pl.pallas_call(
        back_kernel,
        name="back",
        out_shape=(
            jax.ShapeDtypeStruct((6, 3072), f32),
            jax.ShapeDtypeStruct((6, 3072), f32),
            jax.ShapeDtypeStruct((3, 8, 768), f32),
            jax.ShapeDtypeStruct((16, 768), f32),
            jax.ShapeDtypeStruct((TILE, 768), f32),
        ),
        in_specs=[IN_VMEM] * 5 + [ANY_SPACE] * 8,
        out_specs=(ANY_SPACE, ANY_SPACE, ANY_SPACE, IN_VMEM, ANY_SPACE),
        scratch_shapes=[
            pltpu.VMEM(WIDE, bf), *whole, pltpu.VMEM((4, 4, 2, 3, 8, HALF), bf), *whole, *lands,
            pltpu.VMEM((24, HALF), f32),
            pltpu.VMEM((2, 4, 6, HALF), f32),
            pltpu.VMEM((3, 8, HALF), f32),
            pltpu.VMEM((2, 16, 768), f32),
            pltpu.VMEM((4, 16, 768), f32),
            pltpu.VMEM((4, 16, 768), f32),
            pltpu.VMEM((8, 16, 768), f32),
            pltpu.VMEM((2, 3, 2, TILE, 768), bf),
            pltpu.VMEM((3, 2, TILE, 768), bf),
            pltpu.VMEM((2, 2, TILE, 768), bf),
            pltpu.VMEM((TILE, 768), bf),
            pltpu.VMEM((TILE, 768), bf),
            pltpu.VMEM((TILE, 768), f32),
            pltpu.VMEM((2, 12, TILE, HALF), bf),
            pltpu.VMEM((12, TILE, 768), bf),
            pltpu.VMEM((3, 768, HALF), bf),
            pltpu.VMEM((2, 12, TILE, HALF), bf),
            pltpu.VMEM((2, 8, TILE, 128), f32),
            pltpu.VMEM((2, TILE, HALF), bf),
            pltpu.VMEM((6, 128, TILE), f32),
            pltpu.VMEM((3, 768, HALF), f32),
            pltpu.VMEM((1, HALF), f32),
            pltpu.VMEM((1, HALF), f32),
            pltpu.VMEM((2, 1, TILE), jnp.int32),
            pltpu.VMEM((12, TILE, 1), jnp.int32),
            pltpu.VMEM((2, TILE, HALF), bf),
            dma((12, 3)), dma((12, 3)), dma((12, 3)), dma((3, 2, 8, 3)), dma((3, 2, 8, 3)), dma((6, 2, 3)), dma((6, 2, 3)),
            dma((2, 8)), dma((2, 7)),
            dma((2,)), dma((3,)), dma((4, 8)), dma((4, 8)), dma((8,)), dma((8,)), dma((1,)), dma((6,)), dma((1,)), dma((1,)),
        ],
        compiler_params=pltpu.CompilerParams(collective_id=2, has_side_effects=True, vmem_limit_bytes=63 << 20),
    )(lengths, q_heads, o_heads, lse, gv, d_att, kv, window, first, dwo, g1, g2, base)


def dot32(a, b):
    return jnp.dot(a, b, preferred_element_type=jnp.float32)


def lanes_low(rows):
    return lax.broadcasted_iota(jnp.int32, (rows, 128), 1) < HEAD_DIM


def across_lanes(a, b):
    return lax.dot_general(a, b, (((1,), (1,)), ((), ())), preferred_element_type=jnp.float32)


def flipped(a):
    return jnp.swapaxes(a, 0, 1)


def norm_parts(resid):
    centred = resid - jnp.mean(resid, axis=1, keepdims=True)
    inverse = lax.rsqrt(jnp.mean(centred * centred, axis=1, keepdims=True) + NORM_EPS)
    return centred * inverse, inverse


def norm_back(upstream, gain, n, inverse):
    e = upstream * gain
    return inverse * (e - jnp.mean(e, axis=1, keepdims=True) - n * jnp.mean(e * n, axis=1, keepdims=True))


def row_sum(a):
    return jnp.sum(a, axis=0, keepdims=True)


def mlp_kernel(
    att_ref, tok_ref, cot_ref, rows, bias_in, first, second, third,
    out_ref, d_one_ref, d_att_ref, dwo_ref, dw_in_ref, dw_down_ref, sums_ref,
    w_out, w_in, w_down, n_one, low, low_flip, slope, active, wide, sem,
):
    f32, bf = jnp.float32, jnp.bfloat16
    loads = [pltpu.make_async_copy(first.at[:, 3], w_out, sem.at[0])]
    loads += [pltpu.make_async_copy(second, w_in, sem.at[1]), pltpu.make_async_copy(third, w_down, sem.at[2])]
    for cp in loads:
        cp.start()

    def row(n):
        return rows[n : n + 1]

    halves = (slice(0, HALF), slice(HALF, 768))
    loads[0].wait()
    att = att_ref[...]
    for h in range(2):
        wide[:, halves[h]] = dot32(att, w_out[h])
    one, inverse_one = norm_parts(tok_ref[...].astype(f32) + (wide[...] + row(2)))
    n_one[...] = one
    normed = one * row(3) + row(4)
    low[...] = normed.astype(bf)
    low_flip[...] = flipped(low[...])
    wide[...] = normed + row(5)
    loads[1].wait()
    loads[2].wait()

    def up(m, carry):
        h = dot32(low[...], w_in[lax.rem(m, 2), m // 2]) + bias_in[m]
        cdf = 0.5 * (1.0 + lax.erf(h * 0.7071067811865476))
        slope[m] = cdf + h * jnp.exp(h * h * -0.5) * 0.3989422804014327
        a = (h * cdf).astype(bf)
        active[m] = flipped(a)
        for k in range(2):
            wide[:, halves[k]] += dot32(a, w_down[k, m])
        return carry

    lax.fori_loop(0, 8, up, 0)
    two, inverse_two = norm_parts(wide[...])
    out_ref[...] = (two * row(6) + row(7)).astype(bf)
    upstream = cot_ref[...].astype(f32)
    sums_ref[0:2] = jnp.zeros((2, 768), f32)
    sums_ref[12:16] = jnp.zeros((4, 768), f32)
    sums_ref[6:7] = row_sum(upstream * two)
    sums_ref[7:8] = row_sum(upstream)
    d_two = norm_back(upstream, row(6), two, inverse_two)
    sums_ref[5:6] = row_sum(d_two)
    d_low = d_two.astype(bf)
    wide[...] = d_two

    def down(m, carry):
        d_active = None
        for k in range(2):
            d_half = d_low[:, halves[k]]
            dw_down_ref[k, m] = dot32(active[m], d_half).astype(bf)
            part = across_lanes(d_half, w_down[k, m])
            d_active = part if d_active is None else d_active + part
        d_hidden = (d_active * slope[m]).astype(bf)
        sums_ref[pl.ds(8 + m // 2, 1), pl.ds(pl.multiple_of(lax.rem(m, 2) * HALF, 128), HALF)] = row_sum(d_hidden.astype(f32))
        dw_in_ref[lax.rem(m, 2), m // 2] = dot32(low_flip[...], d_hidden).astype(bf)
        wide[...] += across_lanes(d_hidden, w_in[lax.rem(m, 2), m // 2])
        return carry

    lax.fori_loop(0, 8, down, 0)
    d_normed = wide[...]
    one = n_one[...]
    sums_ref[3:4] = row_sum(d_normed * one)
    sums_ref[4:5] = row_sum(d_normed)
    d_one = norm_back(d_normed, row(3), one, inverse_one)
    d_one_ref[...] = d_one
    sums_ref[2:3] = row_sum(d_one)
    d_low = d_one.astype(bf)
    att_flip = flipped(att_ref[...])
    d_att = None
    for h in range(2):
        d_half = d_low[:, halves[h]]
        dwo_ref[h] = dot32(att_flip, d_half).astype(bf)
        part = across_lanes(d_half, w_out[h])
        d_att = part if d_att is None else d_att + part
    d_att_ref[...] = d_att.astype(bf)


def mlp(att, tokens, cotangent, rows, bias_in, first, second, third):
    f32, bf = jnp.float32, jnp.bfloat16
    return pl.pallas_call(
        mlp_kernel,
        name="mlp",
        in_specs=[IN_VMEM] * 5 + [ANY_SPACE] * 3,
        out_specs=(IN_VMEM,) * 7,
        out_shape=(
            jax.ShapeDtypeStruct((TILE, 768), bf),
            jax.ShapeDtypeStruct((TILE, 768), f32),
            jax.ShapeDtypeStruct((TILE, 768), bf),
            jax.ShapeDtypeStruct((2, 768, HALF), bf),
            jax.ShapeDtypeStruct((2, 4, 768, HALF), bf),
            jax.ShapeDtypeStruct((2, 8, HALF, HALF), bf),
            jax.ShapeDtypeStruct((16, 768), f32),
        ),
        scratch_shapes=[
            pltpu.VMEM((2, 768, HALF), bf),
            pltpu.VMEM((2, 4, 768, HALF), bf),
            pltpu.VMEM((2, 8, HALF, HALF), bf),
            pltpu.VMEM((TILE, 768), f32),
            pltpu.VMEM((TILE, 768), bf),
            pltpu.VMEM((768, TILE), bf),
            pltpu.VMEM((8, TILE, HALF), f32),
            pltpu.VMEM((8, HALF, TILE), bf),
            pltpu.VMEM((TILE, 768), f32),
            pltpu.SemaphoreType.DMA((3,)),
        ],
        compiler_params=pltpu.CompilerParams(vmem_limit_bytes=58 << 20),
    )(att, tokens, cotangent, rows, bias_in, first, second, third)


def body(
    tokens, w_qkv, bias_q, bias_v, w_out, bias_out, gain_one, shift_one, w_in, bias_in,
    w_down, bias_down, gain_two, shift_two, doc_lengths, cotangent,
):
    shard = lax.axis_index("shard")
    f32 = jnp.float32
    width = tokens.shape[1]

    vectors = (bias_q, bias_v, bias_out, gain_one, shift_one, bias_down, gain_two, shift_two)
    vec = jnp.concatenate(
        [
            jnp.stack(vectors).astype(f32),
            jnp.pad(bias_in.astype(f32).reshape(1, 24), ((0, 7), (0, 0))),
            jnp.zeros((8, 98), f32),
        ],
        axis=1,
    )
    cat = jnp.stack([jnp.concatenate([w_qkv, w_out], axis=1), w_in])
    lengths = doc_lengths.reshape(1, 128)
    first, second, third, rows, hidden_bias, window, kv, q_heads, o_heads, lse, attended = front(
        lengths, cat, w_down.reshape(3, 8, width), vec, tokens
    )
    first = first.reshape(2, 4, width, HALF)
    second = second.reshape(2, 4, width, HALF)
    third = third.reshape(2, 8, HALF, HALF)
    window = window.reshape(12, TILE, width)
    layer_out, d_one, d_att, dw_out, dw_in, dw_down, sums = mlp(
        attended, tokens, cotangent, rows, hidden_bias, first, second, third
    )
    sum_first, sum_in, sum_down, sum_vec, grad_tokens = back(
        lengths, q_heads, o_heads, lse, sums, d_att, kv, window, first,
        dw_out.reshape(2, 4, 4, 2, 3, 8, HALF), dw_in.reshape(2, *WIDE), dw_down.reshape(2, *TALL), d_one,
    )
    own = lax.dynamic_slice(sum_vec, (0, 6 * shard), (8, 6))
    own_in = lax.dynamic_slice(sum_vec[8:12].reshape(-1), (24 * shard,), (24,))
    return (
        layer_out, grad_tokens, sum_first[:, : 3 * width], own[0], own[1], sum_first[:, 3 * width :],
        own[2], own[3], own[4], sum_in, own_in, sum_down.reshape(24, width), own[5], own[6], own[7],
    )


def solution(mesh):
    both, own = P(("shard", "seq"), None), P("shard")
    rows = P("shard", None)
    return jax.shard_map(
        body,
        mesh=mesh,
        in_specs=(both, rows, own, own, rows, own, own, own, rows, own, rows, own, own, own, P(), both),
        out_specs=(both, both, rows, own, own, rows, own, own, own, rows, own, rows, own, own, own),
        check_vma=False,
    )
```

```python
import functools
import jax
import jax.numpy as jnp
from jax import lax
from jax.experimental import pallas as pl
from jax.experimental.pallas import tpu as pltpu
from jax.sharding import PartitionSpec as P

HEAD_DIM = 64
NORM_EPS = 1e-12
MESH = pl.DeviceIdType.MESH
ANY_SPACE = pl.BlockSpec(memory_space=pl.ANY)
IN_VMEM = pl.BlockSpec(memory_space=pltpu.VMEM)
LOG2E = 1.4426950408889634
TILE = 256
HALF = 384
BOTTOM = -1e30
EXTENT = {"x": 4, "y": 4, "z": 8}
ORDERS = (("z", "y", "x"), ("z", "y", "x"), ("z", "x", "y"))
X_FIRST, Y_FIRST = ("x", "y", "z"), ("y", "x", "z")
SUM_ORDERS = ((X_FIRST, X_FIRST, Y_FIRST), (X_FIRST, Y_FIRST, X_FIRST), (X_FIRST, X_FIRST, Y_FIRST))
OTHERS = {dim: range(1, size) for dim, size in EXTENT.items()}
HALVES = (((0, 256), (256, 128)), ((0, 128), (128, 256)), ((0, 256), (256, 128)))
STREAMS = (0, 1, 2)
WIDE = (2, 2, 4, 4, 2, 3, 8, HALF)
TALL = (4, 4, 2, 2, 2, 3, 8, HALF)


def place():
    s = lax.axis_index("shard")
    q = lax.axis_index("seq")
    return {
        "c": lax.rem(s, 2),
        "y": lax.rem(s // 2, 4),
        "x": s // 32,
        "z": lax.rem(s // 8, 4) * 2 + q,
    }


def device_at(at):
    return {
        "shard": ((at["x"] * 4 + at["z"] // 2) * 4 + at["y"]) * 2 + at["c"],
        "seq": lax.rem(at["z"], 2),
    }


def moved(at, **steps):
    new = dict(at)
    for dim, step in steps.items():
        size = 2 if dim == "c" else EXTENT[dim]
        new[dim] = lax.rem(at[dim] + step + size, size)
    return new


def stream_mates():
    s = lax.axis_index("shard")
    q = lax.axis_index("seq")
    partner = {"shard": s, "seq": 1 - q}
    after = {"shard": lax.rem(s + 2, 128), "seq": q}
    before = {"shard": lax.rem(s + 126, 128), "seq": q}
    return partner, before, after


def greet(targets):
    barrier = pltpu.get_barrier_semaphore()
    for target in targets:
        pl.semaphore_signal(barrier, inc=1, device_id=target, device_id_type=MESH)
    pl.semaphore_wait(barrier, len(targets))


def sending(src, dst, send, recv, target):
    return pltpu.make_async_remote_copy(
        src_ref=src, dst_ref=dst, send_sem=send, recv_sem=recv, device_id=target, device_id_type=MESH
    )


def neighbours(at):
    return [moved(at, **{d: step}) for d in ("x", "y", "z") for step in (1, -1)]


def octet_mates(me):
    across = dict(me)
    across["y"] = me["y"] + 1 - 2 * lax.rem(me["y"], 2)
    twin = moved(me, c=1)
    diagonal = dict(across)
    diagonal["c"] = twin["c"]
    return twin, across, diagonal


def span(index):
    return slice(None) if index is None else pl.ds(index, 1)


def picks_of(sets, gone=()):
    x, y, z = sets["x"], sets["y"], sets["z"]
    pick = {
        "x": x,
        "m": None if y is None else y // 2,
        "yp": None if y is None else lax.rem(y, 2),
        "zh": None if z is None else z // 2,
        "q": None if z is None else lax.rem(z, 2),
    }
    names = {"x": ("x",), "y": ("m", "yp"), "z": ("zh", "q")}
    for dim in gone:
        for name in names[dim]:
            pick[name] = 0
    return pick


WIDE_DIMS = ("yp", "q", "x", "zh", "m")
TALL_DIMS = ("x", "zh", "m", "yp", "q")
DIM_SIZE = {"yp": 2, "q": 2, "x": 4, "zh": 4, "m": 2}


def dims_of(k):
    return TALL_DIMS if k == 2 else WIDE_DIMS


def view(ref, k, part, sets, half=None, gone=(), lead=()):
    pick = picks_of(sets, gone)
    cut = (0, HALF) if half is None else HALVES[k][half]
    at = tuple(span(pick[d]) for d in dims_of(k))
    rows = () if part is None else (part,)
    return ref.at[(*lead, *at, *rows, slice(None), pl.ds(*cut))]


def find_docs(lengths, q_docs, k_docs):
    shard, seq = lax.axis_index("shard"), lax.axis_index("seq")
    stream_len = 128 * 2 * TILE
    row = lax.broadcasted_iota(jnp.int32, (128, 128), 0)
    column = lax.broadcasted_iota(jnp.int32, (128, 128), 1)
    wide = jnp.broadcast_to(lengths[...], (128, 128))
    starts_down = jnp.sum(jnp.where(column < row, wide, 0), axis=1, keepdims=True)
    lengths_down = jnp.sum(jnp.where(column == row, wide, 0), axis=1, keepdims=True)
    starts_across = jnp.sum(jnp.where(row < column, jnp.broadcast_to(lengths_down, (128, 128)), 0), axis=0, keepdims=True)
    origin = (shard // 2 - 1) * (4 * TILE)

    def tile(t, carry):
        at = origin + t * TILE + lax.broadcasted_iota(jnp.int32, (TILE, 1), 0)
        counted = jnp.sum((at >= starts_across).astype(jnp.int32), axis=1, keepdims=True) - 1
        k_docs[t] = jnp.where(at < stream_len, counted, stream_len)
        return carry

    lax.fori_loop(0, 12, tile, 0)
    for i in range(2):
        at = origin + (4 + seq + 2 * i) * TILE + lax.broadcasted_iota(jnp.int32, (1, TILE), 1)
        q_docs[i] = jnp.sum((starts_down <= at).astype(jnp.int32), axis=0, keepdims=True) - 1


def front_kernel(
    lengths, cat_ref, down_ref, vec_ref, tok_ref,
    first, second, third, rows_out, bias_in_out, window_out, kv_out, q_heads, o_heads, lse, attended,
    q_docs, k_docs,    land, stage, own, vecs, window, kv, w_heads, w_flat, top, total, acc,
    oct_s, oct_r, local, near_s, near_r, send, recv, core_s, core_r, vec_s, vec_r, tok_s, tok_r, keep, att_s, att_r,
):
    me = place()
    c, x, y, z = me["c"], me["x"], me["y"], me["z"]
    yp, q, m, zh = lax.rem(y, 2), lax.rem(z, 2), y // 2, z // 2
    outs = (first, second, third)
    twin, across, diagonal = octet_mates(me)
    twin_id = device_at(twin)
    partner, before, after = stream_mates()
    lines = [moved(me, **{d: o}) for d in EXTENT for o in OTHERS[d]]
    greet([device_at(a) for a in lines + [twin, diagonal]] + [before, after])

    def chunk_of(at):
        cols = (lax.rem(at["y"], 2) * 2 + q) * 768 + at["c"] * HALF
        return cat_ref.at[:, :, pl.ds(pl.multiple_of(cols, 128), HALF)]

    index = yp * 2 + c
    mates = (twin, across, diagonal)
    out = [
        sending(chunk_of(mate), land.at[:, index], oct_s.at[k], oct_r.at[k], device_at(mate))
        for k, mate in enumerate(mates)
    ]
    for cp in out:
        cp.start()
    kept = pltpu.make_async_copy(chunk_of(me), land.at[:, index], local.at[0])
    kept.start()
    gives = q == c
    down_out = sending(
        down_ref.at[:, :, pl.ds(pl.multiple_of((1 - c) * HALF, 128), HALF)], own.at[2], oct_s.at[3], oct_r.at[3], twin_id
    )
    down_kept = pltpu.make_async_copy(
        down_ref.at[:, :, pl.ds(pl.multiple_of(c * HALF, 128), HALF)], own.at[2], local.at[1]
    )

    @pl.when(gives)
    def _():
        down_out.start()
        down_kept.start()

    vec_kept = pltpu.make_async_copy(vec_ref, vecs.at[c, x, zh, y], local.at[2])
    vec_kept.start()

    sent = []

    def go(src, dst, send_sem, recv_sem, target):
        cp = sending(src, dst, send_sem, recv_sem, target)
        cp.start()
        sent.append(cp)

    def arrive(dst, send_sem, recv_sem, target):
        sending(dst, dst, send_sem, recv_sem, target).wait_recv()

    def tok_go(src, dst, at, target):
        go(src, dst, tok_s.at[at], tok_r.at[at], target)

    tok_kept = pltpu.make_async_copy(tok_ref, window.at[1, c, q], local.at[3])

    def tok_start():
        tok_kept.start()
        tok_go(tok_ref, window.at[1, c, q], 0, partner)
        tok_go(tok_ref, window.at[0, c, q], 1, after)
        tok_go(tok_ref, window.at[2, c, q], 2, before)
        tok_go(tok_ref, window.at[1, c, q], 3, twin_id)

    def tok_forward():
        theirs = window.at[1, c, 1 - q]
        arrive(theirs, tok_s.at[0], tok_r.at[0], partner)
        tok_go(theirs, window.at[0, c, 1 - q], 4, after)
        tok_go(theirs, window.at[2, c, 1 - q], 5, before)
        tok_go(theirs, window.at[1, c, 1 - q], 6, twin_id)

    def tok_share(h, first_slot, at):
        arrive(window.at[0, c, h], tok_s.at[first_slot], tok_r.at[first_slot], before)
        arrive(window.at[2, c, h], tok_s.at[first_slot + 1], tok_r.at[first_slot + 1], after)
        tok_go(window.at[0, c, h], window.at[0, c, h], at, twin_id)
        tok_go(window.at[2, c, h], window.at[2, c, h], at + 1, twin_id)

    vec_rounds = (("x", (1, 2, 3)), ("y", (1, 2, 3)), ("z", (2, 4, 6)), ("c", (1,)))

    def vec_copies(number, arriving):
        dim, steps = vec_rounds[number]
        done = [d for d, _ in vec_rounds[:number]]
        copies = []
        for k, step in enumerate(steps):
            source = moved(me, **{dim: (1 if dim == "c" else -step)}) if arriving else me
            pick = [None if d in done else (source["z"] // 2 if d == "z" else source[d]) for d in ("c", "x", "z", "y")]
            ref = vecs.at[tuple(span(p) for p in pick)]
            copies.append(
                sending(ref, ref, vec_s.at[number, k], vec_r.at[number, k], device_at(moved(me, **{dim: step})))
            )
        return copies

    def vec_start(number):
        for cp in vec_copies(number, False):
            cp.start()
            sent.append(cp)

    def vec_wait(number):
        for cp in vec_copies(number, True):
            cp.wait_recv()

    kept.wait()
    for k, mate in enumerate(mates):
        mate_index = lax.rem(mate["y"], 2) * 2 + mate["c"]
        arrive(land.at[:, mate_index], oct_s.at[k], oct_r.at[k], device_at(mate))
    for k in range(2):
        for owner in range(4):
            stage[pl.ds(6 * owner, 6), :] = land[k, owner].astype(jnp.float32)
        for part in range(3):
            own[k, part] = stage[pl.ds(8 * part, 8), :].astype(jnp.bfloat16)

    @pl.when(gives)
    def _():
        down_kept.wait()

    @pl.when(jnp.logical_not(gives))
    def _():
        down_out.wait_recv()

    homes = (first.at[c, yp, q, x, zh, m], second.at[c, yp, q, x, zh, m], third.at[c, x, zh, m, yp, q])
    flush = [pltpu.make_async_copy(own.at[k], homes[k], local.at[4 + k]) for k in STREAMS]
    for cp in flush:
        cp.start()
    twins = []

    def share(k, part, sets, half, slot):
        mine = view(outs[k], k, part, sets, half, (), (c,))
        theirs = view(outs[k], k, part, sets, half, (), (1 - c,))
        go(mine, mine, core_s.at[slot, k], core_r.at[slot, k], twin_id)
        twins.append((theirs, core_s.at[slot, k], core_r.at[slot, k]))

    def sets_at(part, phase, index):
        sets = {"x": x, "y": y, "z": z}
        for earlier in ORDERS[part][:phase]:
            sets[earlier] = None
        dim = ORDERS[part][phase]
        sets[dim] = lax.rem(index + EXTENT[dim], EXTENT[dim])
        return sets

    def near(k, part, phase, arriving):
        dim = ORDERS[part][phase]
        for o in OTHERS[dim]:
            sems = near_s.at[part, phase, o, k], near_r.at[part, phase, o, k]
            target = device_at(moved(me, **{dim: o}))
            if arriving:
                arrive(view(outs[k], k, part, sets_at(part, phase, me[dim] - o), None, (), (c,)), *sems, target)
            elif phase == 0:
                go(own.at[k, part], homes[k].at[part], *sems, target)
            else:
                ref = view(outs[k], k, part, sets_at(part, phase, me[dim]), None, (), (c,))
                go(ref, ref, *sems, target)

    def ring(k, part, step, arriving):
        dim = ORDERS[part][2]
        size = EXTENT[dim]
        for direction, sign in enumerate((1, -1)):
            sets = sets_at(part, 2, me[dim] - sign * (step if arriving else step - 1))
            half = direction if step == size // 2 else None
            ref = view(outs[k], k, part, sets, half, (), (c,))
            slot = part * 2 + step - 1
            sems = send.at[slot, direction, k], recv.at[slot, direction, k]
            target = device_at(moved(me, **{dim: sign}))
            if arriving:
                arrive(ref, *sems, target)
            else:
                go(ref, ref, *sems, target)

    def ring_share(k, part, step):
        dim = ORDERS[part][2]
        for direction, sign in enumerate((1, -1)):
            half = direction if step == EXTENT[dim] // 2 else None
            share(k, part, sets_at(part, 2, me[dim] - sign * step), half, 3 + (part * 2 + step - 1) * 2 + direction)

    parts = range(3)
    late = [(k, part) for k in (1, 2) for part in parts]
    for part in parts:
        near(0, part, 0, False)
    vec_kept.wait()
    vec_start(0)
    for k, part in late:
        near(k, part, 0, False)
    find_docs(lengths, q_docs, k_docs)
    for cp in flush:
        cp.wait()
    for part in parts:
        near(0, part, 0, True)
        near(0, part, 1, False)
    tok_start()
    vec_wait(0)
    vec_start(1)
    for part in parts:
        near(0, part, 1, True)
        ring(0, part, 1, False)
    for k, part in late:
        near(k, part, 0, True)
        near(k, part, 1, False)
    vec_wait(1)
    vec_start(2)
    tok_forward()
    for part in parts:
        ring(0, part, 1, True)
        ring(0, part, 2, False)
    vec_wait(2)
    vec_start(3)
    for k, part in late:
        near(k, part, 1, True)
        ring(k, part, 1, False)
    for k, part in late:
        share(k, part, sets_at(part, 2, me[ORDERS[part][2]]), None, part)
    vec_wait(3)
    for v in range(8):
        rows_out[v : v + 1] = jnp.zeros((1, 768), jnp.float32)
    lane = lax.broadcasted_iota(jnp.int32, (128, HALF), 0)
    line = lax.broadcasted_iota(jnp.int32, (512, HALF), 0)
    values = [vecs[owner_core].reshape(512, 128).astype(jnp.bfloat16) for owner_core in range(2)]
    for h in range(2):
        column = h * HALF + lax.broadcasted_iota(jnp.int32, (1, HALF), 1)
        cols = slice(h * HALF, (h + 1) * HALF)
        for owner_core in range(2):
            place_in = lax.rem(column, 12) - 6 * owner_core
            picked = dot32(values[owner_core], jnp.logical_and(lane == place_in, lane < 6).astype(jnp.bfloat16))
            for v in range(8):
                rows_out[v : v + 1, cols] += row_sum(jnp.where(line == column // 12 * 8 + v, picked, 0.0))

    def hidden_row(m, carry):
        column = m * HALF + lax.broadcasted_iota(jnp.int32, (1, HALF), 1)
        total = jnp.zeros((1, HALF), jnp.float32)
        for owner_core in range(2):
            place_in = lax.rem(column, 48) - 24 * owner_core
            inside = jnp.logical_and(place_in >= 0, place_in < 24)
            picked = dot32(values[owner_core], jnp.logical_and(lane == place_in + 6, inside).astype(jnp.bfloat16))
            total = total + row_sum(jnp.where(line == column // 48 * 8, picked, 0.0))
        bias_in_out[m] = total
        return carry

    lax.fori_loop(0, 8, hidden_row, 0)
    for part in parts:
        ring(0, part, 2, True)
    load = pltpu.make_async_copy(first.at[c, pl.ds(0, 2), pl.ds(0, 2)], w_heads, keep.at[1])
    load.start()
    go(first.at[c, 1, 1], first.at[c, 1, 1], core_s.at[0, 0], core_r.at[0, 0], twin_id)
    twins.append((first.at[1 - c, 1, 1], core_s.at[0, 0], core_r.at[0, 0]))

    own_half = pl.ds(pl.multiple_of(c * HALF, 128), HALF)
    bias = [rows_out[v : v + 1, own_half] for v in range(2)]
    arrive(window.at[1, 1 - c, q], tok_s.at[3], tok_r.at[3], twin_id)
    arrive(window.at[1, 1 - c, 1 - q], tok_s.at[6], tok_r.at[6], twin_id)
    tok_kept.wait()
    load.wait()

    def project_group(group):
        def one(n, carry):
            core, h = n // 2, lax.rem(n, 2)
            x_tile, t = window[group, core, h], group * 4 + n
            kv[0, t] = dot32(x_tile, weights(1)).astype(jnp.bfloat16)
            kv[1, t] = (dot32(x_tile, weights(2)) + bias[1]).astype(jnp.bfloat16)
            return carry

        lax.fori_loop(0, 4, one, 0)

    def flatten(i, carry):
        rows = pl.ds(pl.multiple_of(i * 192, 192), 192)
        for number in range(3):
            piece = w_heads[number // 2, number % 2, i].astype(jnp.float32)
            w_flat[number, rows] = piece.reshape(192, HALF).astype(jnp.bfloat16)
        return carry

    lax.fori_loop(0, 4, flatten, 0)

    def weights(number):
        return w_flat[number]

    low = lanes_low(TILE)
    scale = HEAD_DIM ** -0.5 * LOG2E

    def heads_front(pair, i, near_by):
        cols = slice(pair * 128, (pair + 1) * 128) if isinstance(pair, int) else pl.ds(pl.multiple_of(pair * 128, 128), 128)
        at = pair * 2 + i
        qs = q_heads[i, :, cols]
        none = jnp.zeros_like(qs)
        queries = (jnp.where(low, qs, none), jnp.where(low, none, qs))
        if near_by:
            top[at] = jnp.full((2, 1, TILE), BOTTOM, jnp.float32)
            total[at] = jnp.zeros((2, 1, TILE), jnp.float32)
            acc[at] = jnp.zeros((128, TILE), jnp.float32)

        def step(n, carry):
            u = q + 2 * i + n
            t = 4 + n if near_by else u + 4 * (u // 4)
            k, v = kv[0, t, :, cols], flipped(kv[1, t, :, cols])
            same = q_docs[i] == k_docs[t]
            scores = [jnp.where(same, across_lanes(k, queries[head]) * scale, BOTTOM) for head in range(2)]
            old = [top[at, head] for head in range(2)]
            new = [jnp.maximum(old[head], jnp.max(scores[head], axis=0, keepdims=True)) for head in range(2)]
            fade = [jnp.exp2(old[head] - new[head]) for head in range(2)]
            p = [jnp.exp2(scores[head] - new[head]) for head in range(2)]
            sums = [total[at, head] * fade[head] + jnp.sum(p[head], axis=0, keepdims=True) for head in range(2)]
            adds = [dot32(v[head * HEAD_DIM : (head + 1) * HEAD_DIM], p[head].astype(jnp.bfloat16)) for head in range(2)]
            for head in range(2):
                rows = slice(head * HEAD_DIM, (head + 1) * HEAD_DIM)
                acc[at, rows] = acc[at, rows] * fade[head] + adds[head]
                total[at, head] = sums[head]
                top[at, head] = new[head]
            return carry

        lax.fori_loop(0, 4 if near_by else 5, step, 0)
        if not near_by:
            for head in range(2):
                rows = slice(head * HEAD_DIM, (head + 1) * HEAD_DIM)
                acc[at, rows] = acc[at, rows] / total[at, head]
                lse[pair, i, head : head + 1] = top[at, head] + jnp.log2(total[at, head])
            o_heads[i, :, cols] = flipped(acc[at]).astype(jnp.bfloat16)

    def all_pairs(i, near_by):
        lax.fori_loop(0, 3, lambda pair, carry: (heads_front(pair, i, near_by), carry)[1], 0)

    for i in range(2):
        q_heads[i] = (dot32(window[1, i, q], weights(0)) + bias[0]).astype(jnp.bfloat16)
    project_group(1)
    all_pairs(0, True)
    tok_share(q, 1, 7)
    all_pairs(1, True)
    tok_share(1 - q, 4, 9)
    for part in parts:
        ring(1, part, 1, True)
        ring(1, part, 2, False)
    for h, at in ((q, 7), (1 - q, 9)):
        arrive(window.at[0, 1 - c, h], tok_s.at[at], tok_r.at[at], twin_id)
        arrive(window.at[2, 1 - c, h], tok_s.at[at + 1], tok_r.at[at + 1], twin_id)
    kept_window = pltpu.make_async_copy(window, window_out, keep.at[2])
    kept_window.start()
    project_group(0)
    for part in parts:
        ring(2, part, 1, True)
        ring(2, part, 2, False)
    project_group(2)
    kept_kv = pltpu.make_async_copy(kv, kv_out, keep.at[3])
    kept_kv.start()
    for part in parts:
        ring_share(1, part, 1)
    heads_front(0, 0, False)
    heads_front(1, 0, False)
    for part in parts:
        ring_share(2, part, 1)
    heads_front(2, 0, False)
    for part in parts:
        ring(1, part, 2, True)
        ring_share(1, part, 2)
    all_pairs(1, False)
    mine_cols, other_cols = (pl.ds(pl.multiple_of(a * HALF, 128), HALF) for a in (c, 1 - c))
    go(o_heads.at[1 - c], attended.at[:, mine_cols], att_s.at[0], att_r.at[0], twin_id)
    kept_att = pltpu.make_async_copy(o_heads.at[c], attended.at[:, mine_cols], keep.at[4])
    kept_att.start()
    for part in parts:
        ring(2, part, 2, True)
        ring_share(2, part, 2)
    for ref, send_sem, recv_sem in twins:
        arrive(ref, send_sem, recv_sem, twin_id)
    arrive(attended.at[:, other_cols], att_s.at[0], att_r.at[0], twin_id)
    for cp in (kept_window, kept_kv, kept_att):
        cp.wait()
    for cp in out + sent:
        cp.wait_send()

    @pl.when(gives)
    def _():
        down_out.wait_send()


def front(lengths, cat, down, vec, tokens):
    bf, f32, dma = jnp.bfloat16, jnp.float32, pltpu.SemaphoreType.DMA
    return pl.pallas_call(
        front_kernel,
        name="front",
        out_shape=(
            jax.ShapeDtypeStruct((2, *WIDE), bf),
            jax.ShapeDtypeStruct((2, *WIDE), bf),
            jax.ShapeDtypeStruct((2, *TALL), bf),
            jax.ShapeDtypeStruct((8, 768), f32),
            jax.ShapeDtypeStruct((8, 1, HALF), f32),
            jax.ShapeDtypeStruct((3, 2, 2, TILE, 768), bf),
            jax.ShapeDtypeStruct((2, 12, TILE, HALF), bf),
            jax.ShapeDtypeStruct((2, TILE, HALF), bf),
            jax.ShapeDtypeStruct((2, TILE, HALF), bf),
            jax.ShapeDtypeStruct((3, 2, 2, TILE), f32),
            jax.ShapeDtypeStruct((TILE, 768), bf),
        ),
        in_specs=[IN_VMEM] + [ANY_SPACE] * 4,
        out_specs=(ANY_SPACE,) * 3 + (IN_VMEM,) * 2 + (ANY_SPACE,) * 2 + (IN_VMEM,) * 4,
        scratch_shapes=[
            pltpu.VMEM((2, 1, TILE), jnp.int32),
            pltpu.VMEM((12, TILE, 1), jnp.int32),
            pltpu.VMEM((2, 4, 6, HALF), bf),
            pltpu.VMEM((24, HALF), f32),
            pltpu.VMEM((3, 3, 8, HALF), bf),
            pltpu.VMEM((2, 4, 4, 4, 8, 128), f32),
            pltpu.VMEM((3, 2, 2, TILE, 768), bf),
            pltpu.VMEM((2, 12, TILE, HALF), bf),
            pltpu.VMEM((2, 2, 4, 4, 2, 3, 8, HALF), bf),
            pltpu.VMEM((3, 768, HALF), bf),
            pltpu.VMEM((6, 2, 1, TILE), f32),
            pltpu.VMEM((6, 2, 1, TILE), f32),
            pltpu.VMEM((6, 128, TILE), f32),
            dma((4,)), dma((4,)), dma((7,)), dma((3, 2, 8, 3)), dma((3, 2, 8, 3)), dma((6, 2, 3)), dma((6, 2, 3)),
            dma((15, 3)), dma((15, 3)), dma((4, 3)), dma((4, 3)), dma((11,)), dma((11,)), dma((5,)), dma((1,)), dma((1,)),
        ],
        compiler_params=pltpu.CompilerParams(collective_id=1, has_side_effects=True, vmem_limit_bytes=62 << 20),
    )(lengths, cat, down, vec, tokens)


def back_kernel(*refs):
    (lengths, q_ref, o_ref, lse_ref, gv, d_att, kv_hbm, window_hbm, first, dwo, g1, g2, base) = refs[:13]
    (out0, out1, out2, out_v, out_tok) = refs[13:18]
    grads = (None, g1, g2)
    refs = refs[18:]
    acc, other, refs = refs[:3], refs[3:6], refs[6:]
    lands = {}
    for n, (part, phase, k) in enumerate((a, b, k) for a in range(3) for b in range(3) for k in STREAMS):
        lands[part, phase, k] = refs[n]
    refs = refs[27:]
    (
        stage, rows, tall_f, v_c, v_x, v_y, v_z, t_all, t_in, t_land, t_part, t_mate, t_base,
        kv, window, w_heads, dkv_all, dkv, dq_all, dq_acc, dw, q_rows, v_rows, q_docs, k_docs, do_ref,
        local, core_s, core_r, near_s, near_r, send, recv, fin_s, fin_r, t_s, t_r, vec_s, vec_r, tok_s, tok_r, tok_l, load, att_s, att_r,
    ) = refs
    me = place()
    c, x, y, z = me["c"], me["x"], me["y"], me["z"]
    yp, q, m, zh = lax.rem(y, 2), lax.rem(z, 2), y // 2, z // 2
    twin, across, diagonal = octet_mates(me)
    twin_id = device_at(twin)
    partner, before, after = stream_mates()

    def other_q(at):
        new = dict(at)
        new["z"] = at["z"] + 1 - 2 * lax.rem(at["z"], 2)
        return new

    ring_mates = [moved(me, **{d: k}) for d in ("x", "y", "z") for k in range(1, EXTENT[d])]
    mates = [twin, across, diagonal] + [other_q(a) for a in (me, twin, across, diagonal)]
    targets = ring_mates + [twin, diagonal] + [other_q(a) for a in (twin, across, diagonal)]
    greet([device_at(a) for a in targets] + [before, after])
    sent = []

    def go(src, dst, send_sem, recv_sem, target):
        cp = sending(src, dst, send_sem, recv_sem, target)
        cp.start()
        sent.append(cp)

    def arrive(dst, send_sem, recv_sem, target):
        sending(dst, dst, send_sem, recv_sem, target).wait_recv()

    def sets_of(k, part, phase, index):
        sets = {"x": x, "y": y, "z": z}
        order = SUM_ORDERS[k][part]
        for later in order[phase + 1:]:
            sets[later] = None
        sets[order[phase]] = lax.rem(index + 2 * EXTENT[order[phase]], EXTENT[order[phase]])
        return sets

    def add_region(k, part, sets, sources, half=None, gone=()):
        pick, from_pick = picks_of(sets), picks_of(sets, gone)
        dims = dims_of(k)
        inner = dims[3:] if k < 2 else dims[2:]
        outer = [d for d in dims if d not in inner and pick[d] is None]
        count = 1
        for d in outer:
            count *= DIM_SIZE[d]
        cut = pl.ds(*((0, HALF) if half is None else HALVES[k][half]))

        def one(i):
            at = {}
            for d in reversed(outer):
                at[d] = lax.rem(i, DIM_SIZE[d]) if count > 1 else 0
                i = i // DIM_SIZE[d]

            def index(picked):
                return tuple(
                    (at[d] if d in at else slice(None)) if picked[d] is None else pl.ds(picked[d], 1) if d in inner else picked[d]
                    for d in dims
                )

            to = (*index(pick), part, slice(None), cut)
            fr = (*index(from_pick), slice(None), cut)
            if len(sources) == 1:
                acc[k][to] = acc[k][to] + sources[0][fr]
            else:
                total = acc[k][to].astype(jnp.float32)
                for src in sources:
                    total = total + src[fr].astype(jnp.float32)
                acc[k][to] = total.astype(jnp.bfloat16)

        if count == 1:
            one(0)
        else:
            lax.fori_loop(0, count, lambda i, carry: (one(i), carry)[1], 0)

    def hop(k, part, n):
        return sets_of(k, part, 0, me[SUM_ORDERS[k][part][0]] + (2, 1, -1, 0)[n])

    own_copies = {}

    def cross(k, part, n):
        slot = part * 4 + n
        sets = hop(k, part, n)
        src = view(grads[k], k, part, sets, None, (), (1 - c,))
        go(src, view(other[k], k, part, sets), core_s.at[slot, k], core_r.at[slot, k], twin_id)
        kept = pltpu.make_async_copy(
            view(grads[k], k, part, sets, None, (), (c,)), view(acc[k], k, part, sets), local.at[slot, k]
        )
        kept.start()
        own_copies[k, part, n] = kept

    loads = [
        pltpu.make_async_copy(kv_hbm, kv, load.at[0]),
        pltpu.make_async_copy(first.at[c, pl.ds(0, 3)], w_heads, load.at[1]),
        pltpu.make_async_copy(window_hbm, window, load.at[2]),
        pltpu.make_async_copy(dwo.at[c], acc[0].at[1, 1], load.at[3]),
        pltpu.make_async_copy(base, t_base, load.at[4]),
    ]
    loads[0].start()
    own_half, other_half = (pl.ds(pl.multiple_of(a * HALF, 128), HALF) for a in (c, 1 - c))
    go(d_att.at[:, other_half], do_ref.at[c], att_s.at[0], att_r.at[0], twin_id)
    d_kept = pltpu.make_async_copy(d_att.at[:, own_half], do_ref.at[c], load.at[5])
    d_kept.start()
    for n in range(4):
        for k in (1, 2):
            for part in range(3):
                cross(k, part, n)

    for cp in loads[1:]:
        cp.start()
    go(dwo.at[1 - c], other[0], core_s.at[0, 0], core_r.at[0, 0], twin_id)

    vec_lands = (v_c, v_x, v_y, v_z)
    vec_dims = ("c", "x", "y", "z")

    def vec_start(number):
        dim, land = vec_dims[number], vec_lands[number]
        for k in range(1, land.shape[0]):
            mine = land.at[me[dim]]
            go(mine, mine, vec_s.at[number, k], vec_r.at[number, k], device_at(moved(me, **{dim: k})))

    def vec_finish(number):
        dim, land = vec_dims[number], vec_lands[number]
        size = land.shape[0]
        for k in range(1, size):
            theirs = land.at[lax.rem(me[dim] - k + size, size)]
            arrive(theirs, vec_s.at[number, k], vec_r.at[number, k], device_at(moved(me, **{dim: k})))
        total = land[0].astype(jnp.float32)
        for k in range(1, size):
            total = total + land[k].astype(jnp.float32)
        return total

    def row_blocks(fn):
        lax.fori_loop(0, TILE // 32, lambda r, carry: (fn(pl.ds(pl.multiple_of(r * 32, 32), 32)), carry)[1], 0)

    def tok_twin(group, at):
        go(t_all.at[1 - c, group], t_in.at[group], tok_s.at[at], tok_r.at[at], twin_id)

    def tok_edges():
        for n, (group, at) in enumerate(((0, 0), (2, 6))):
            arrive(t_in.at[group], tok_s.at[at], tok_r.at[at], twin_id)
        for n, h in enumerate((1 - q, q)):
            for group in (0, 2):
                def one(at):
                    t_all[c, group, h, at] = t_all[c, group, h, at] + t_in[group, h, at]
                row_blocks(one)
            go(t_all.at[c, 0, h], t_land.at[1, h], tok_s.at[1 + n], tok_r.at[1 + n], before)
            go(t_all.at[c, 2, h], t_land.at[0, h], tok_s.at[3 + n], tok_r.at[3 + n], after)

    def tok_total(h, at):
        f = jnp.float32
        return t_all[c, 1, h, at].astype(f) + t_in[1, h, at].astype(f) + t_land[0, h, at].astype(f) + t_land[1, h, at].astype(f)

    def tok_theirs():
        h = 1 - q
        arrive(t_in.at[1], tok_s.at[7], tok_r.at[7], twin_id)
        arrive(t_land.at[1, h], tok_s.at[1], tok_r.at[1], after)
        arrive(t_land.at[0, h], tok_s.at[3], tok_r.at[3], before)

        def one(at):
            t_part[at] = tok_total(h, at).astype(jnp.bfloat16)
        row_blocks(one)
        go(t_part, t_mate, tok_s.at[5], tok_r.at[5], partner)

    def tok_mine():
        arrive(t_land.at[1, q], tok_s.at[2], tok_r.at[2], after)
        arrive(t_land.at[0, q], tok_s.at[4], tok_r.at[4], before)
        arrive(t_mate, tok_s.at[5], tok_r.at[5], partner)
        loads[4].wait()

        def one(at):
            t_base[at] = tok_total(q, at) + t_mate[at].astype(jnp.float32) + t_base[at]
        row_blocks(one)
        done = pltpu.make_async_copy(t_base, out_tok, tok_l.at[0])
        done.start()
        return done

    def meet(k, part, n):
        slot = part * 4 + n
        own_copies[k, part, n].wait()
        sets = hop(k, part, n)
        arrive(view(other[k], k, part, sets), core_s.at[slot, k], core_r.at[slot, k], twin_id)
        add_region(k, part, sets, [other[k].at[(slice(None),) * 5 + (part,)]])

    def meet_out():
        loads[3].wait()
        arrive(other[0], core_s.at[0, 0], core_r.at[0, 0], twin_id)

        def one(i, carry):
            acc[0][1, 1, i] = acc[0][1, 1, i] + other[0][i]
            return carry

        lax.fori_loop(0, 4, one, 0)

    def ring(k, part, step, arriving):
        dim = SUM_ORDERS[k][part][0]
        ahead = 3 - step - (1 if arriving else 0)
        for direction, sign in enumerate((1, -1)):
            half = direction if step == 1 else None
            sets = sets_of(k, part, 0, me[dim] + sign * ahead)
            land = lands[part, 0, k].at[direction, step - 1]
            slot = part * 2 + step - 1
            sems = send.at[slot, direction, k], recv.at[slot, direction, k]
            target = device_at(moved(me, **{dim: sign}))
            here = view(land, k, None, sets, half, (dim,))
            if arriving:
                arrive(here, *sems, target)
                add_region(k, part, sets, [land], half, (dim,))
            else:
                go(view(acc[k], k, part, sets, half), here, *sems, target)

    def near(k, part, phase, arriving):
        order = SUM_ORDERS[k][part]
        dim, gone = order[phase], order[: phase + 1]
        mine = sets_of(k, part, phase, me[dim])
        sources = []
        for o in OTHERS[dim]:
            sems = near_s.at[part, phase - 1, o, k], near_r.at[part, phase - 1, o, k]
            target = device_at(moved(me, **{dim: o}))
            land = lands[part, phase, k].at[o - 1]
            here = view(land, k, None, mine, None, gone)
            if arriving:
                arrive(here, *sems, target)
                sources.append(land)
            else:
                go(view(acc[k], k, part, sets_of(k, part, phase, me[dim] + o)), here, *sems, target)
        if arriving:
            add_region(k, part, mine, sources, None, gone)

    def vec_next(n):
        total = vec_finish(n)
        if n < 3:
            vec_lands[n + 1][me[vec_dims[n + 1]]] = total.astype(jnp.bfloat16)
            vec_start(n + 1)
        else:
            out_v[...] = total

    low = lanes_low(TILE)
    scale = HEAD_DIM ** -0.5 * LOG2E
    picker = (
        lax.broadcasted_iota(jnp.int32, (8, 128), 0) == lax.broadcasted_iota(jnp.int32, (8, 128), 1) // HEAD_DIM
    ).astype(jnp.float32)

    def heads_back(pair, i, near_by):
        cols = slice(pair * 128, (pair + 1) * 128)
        place_at = pair * 2 + i
        qs, d_out = q_ref[i, :, cols], do_ref[i, :, cols]
        none = jnp.zeros_like(qs)
        q_heads = (jnp.where(low, qs, none), jnp.where(low, none, qs))
        do_heads = (jnp.where(low, d_out, none), jnp.where(low, none, d_out))
        prod = d_out.astype(jnp.float32) * o_ref[i, :, cols].astype(jnp.float32)
        deltas = lax.dot_general(
            picker, prod, (((1,), (1,)), ((), ())), precision=lax.Precision.HIGHEST, preferred_element_type=jnp.float32
        )
        if i == 0:
            dkv[...] = jnp.zeros_like(dkv)
        if not near_by:
            dq_acc[place_at] = jnp.zeros((128, TILE), jnp.float32)

        def step(n, carry):
            u = q + 2 * i + n
            t = 4 + n if near_by else u + 4 * (u // 4)
            slot = n if near_by else u
            k, v = kv[0, t, :, cols], kv[1, t, :, cols]
            k_flip = flipped(k)
            same = q_docs[i] == k_docs[t]
            heads = range(2)
            scores = [across_lanes(k, q_heads[h]) * scale for h in heads]
            dp = [across_lanes(v, do_heads[h]) for h in heads]
            p = [jnp.where(same, jnp.exp2(scores[h] - lse_ref[pair, i, h : h + 1]), 0.0) for h in heads]
            ds = [(p[h] * (dp[h] - deltas[h : h + 1])).astype(jnp.bfloat16) for h in heads]
            p_low = [p[h].astype(jnp.bfloat16) for h in heads]
            dq = [dot32(k_flip[h * HEAD_DIM : (h + 1) * HEAD_DIM], ds[h]) for h in heads]
            dk = [dot32(ds[h], q_heads[h]) for h in heads]
            dv = [dot32(p_low[h], do_heads[h]) for h in heads]
            for h in heads:
                lanes = slice(h * HEAD_DIM, (h + 1) * HEAD_DIM)
                dq_acc[place_at, lanes] = dq_acc[place_at, lanes] + dq[h]
            dkv[0, slot] = dkv[0, slot] + (dk[0] + dk[1])
            dkv[1, slot] = dkv[1, slot] + (dv[0] + dv[1])
            return carry

        lax.fori_loop(0, 4 if near_by else 5, step, 0)
        if near_by:
            dq_all[i, :, cols] = flipped(dq_acc[place_at] * HEAD_DIM ** -0.5).astype(jnp.bfloat16)
        if i == 1:
            def keep(u, carry):
                t = 4 + u if near_by else u + 4 * (u // 4)
                dkv_all[0, t, :, cols] = (dkv[0, u] * HEAD_DIM ** -0.5).astype(jnp.bfloat16)
                dkv_all[1, t, :, cols] = dkv[1, u].astype(jnp.bfloat16)
                return carry

            lax.fori_loop(0, 4 if near_by else 8, keep, 0)

    def tile_back(group, n):
        core, h = n // 2, lax.rem(n, 2)
        t = group * 4 + n
        x_flip = flipped(window[t])
        dk, dv = dkv_all[0, t], dkv_all[1, t]
        dw[1] += dot32(x_flip, dk)
        dw[2] += dot32(x_flip, dv)
        v_rows[...] = v_rows[...] + jnp.sum(dv.astype(jnp.float32), axis=0, keepdims=True)
        dx = across_lanes(dk, w_heads[1]) + across_lanes(dv, w_heads[2])
        t_all[core, group, h] = dx.astype(jnp.bfloat16)
        if group == 1:
            @pl.when(h == q)
            def _():
                dq = dq_all[core]
                dw[0] += dot32(x_flip, dq)
                q_rows[...] = q_rows[...] + jnp.sum(dq.astype(jnp.float32), axis=0, keepdims=True)
                t_all[core, group, h] = (dx + across_lanes(dq, w_heads[0])).astype(jnp.bfloat16)

    def tiles_back(group):
        lax.fori_loop(0, 4, lambda n, carry: (tile_back(group, n), carry)[1], 0)

    parts = range(3)
    late = [(k, part) for k in (1, 2) for part in parts]
    find_docs(lengths, q_docs, k_docs)
    for k, part in late:
        meet(k, part, 0)
        ring(k, part, 1, False)
    loads[0].wait()
    d_kept.wait()
    arrive(do_ref.at[1 - c], att_s.at[0], att_r.at[0], twin_id)
    heads_back(0, 0, False)
    for k, part in late:
        meet(k, part, 1)
        meet(k, part, 2)
    for part in parts:
        ring(1, part, 1, True)
        ring(1, part, 2, False)
    heads_back(0, 1, False)
    for part in parts:
        ring(2, part, 1, True)
        ring(2, part, 2, False)
    heads_back(1, 0, False)
    for k, part in late:
        meet(k, part, 3)
    meet_out()
    heads_back(1, 1, False)
    heads_back(2, 0, False)
    for part in parts:
        ring(1, part, 2, True)
        near(1, part, 1, False)
    heads_back(2, 1, False)
    loads[1].wait()
    loads[2].wait()
    dw[...] = jnp.zeros_like(dw)
    q_rows[...] = jnp.zeros_like(q_rows)
    v_rows[...] = jnp.zeros_like(v_rows)
    tiles_back(0)
    tok_twin(0, 0)
    tiles_back(2)
    tok_twin(2, 6)
    for part in parts:
        ring(2, part, 2, True)
        near(2, part, 1, False)
    heads_back(0, 0, True)
    heads_back(0, 1, True)
    for part in parts:
        near(1, part, 1, True)
        near(1, part, 2, False)
    heads_back(1, 0, True)
    heads_back(1, 1, True)
    for part in parts:
        near(2, part, 1, True)
        near(2, part, 2, False)
    heads_back(2, 0, True)
    heads_back(2, 1, True)
    for k, part in late:
        near(k, part, 2, True)
    tok_edges()
    tiles_back(1)
    tok_twin(1, 7)

    def grads_low(i, carry):
        rows_at = pl.ds(pl.multiple_of(i * 192, 192), 192)
        for number, (a, b) in enumerate(((0, 0), (0, 1), (1, 0))):
            acc[0][a, b, i] = dw[number, rows_at].reshape(4, 2, 3, 8, HALF).astype(jnp.bfloat16)
        return carry

    lax.fori_loop(0, 4, grads_low, 0)
    for part in parts:
        ring(0, part, 1, False)
    v_c[c] = gv[...]
    half_cols = pl.ds(pl.multiple_of(c * HALF, 128), HALF)
    v_c[c, 0:1, half_cols] = q_rows[...]
    v_c[c, 1:2, half_cols] = v_rows[...]
    vec_start(0)
    vec_next(0)
    for part in parts:
        ring(0, part, 1, True)
        ring(0, part, 2, False)
    vec_next(1)
    tok_theirs()
    for part in parts:
        ring(0, part, 2, True)
        near(0, part, 1, False)
    vec_next(2)
    for part in parts:
        near(0, part, 1, True)
        near(0, part, 2, False)
    vec_next(3)
    for part in parts:
        near(0, part, 2, True)

    for k in range(2):
        for part in range(3):
            stage[pl.ds(8 * part, 8), :] = acc[k][yp, q, x, zh, m, part].astype(jnp.float32)
        for owner in range(4):
            rows[k, owner] = stage[pl.ds(6 * owner, 6), :]
    for part in range(3):
        tall_f[part] = acc[2][x, zh, m, yp, q, part].astype(jnp.float32)

    def cols_at(at):
        return pl.ds(pl.multiple_of((lax.rem(at["y"], 2) * 2 + lax.rem(at["z"], 2)) * 768 + at["c"] * HALF, 128), HALF)

    def owner_of(at):
        return lax.rem(at["y"], 2) * 2 + at["c"]

    for k, out in enumerate((out0, out1)):
        for n, mate in enumerate(mates):
            go(rows.at[k, owner_of(mate)], out.at[:, cols_at(me)], fin_s.at[k, n], fin_r.at[k, n], device_at(mate))
    kept = [
        pltpu.make_async_copy(rows.at[k, owner_of(me)], out.at[:, cols_at(me)], fin_s.at[k, 7])
        for k, out in enumerate((out0, out1))
    ]
    for cp in kept:
        cp.start()
    stays = c == q
    half_at = [pl.ds(pl.multiple_of(a * HALF, 128), HALF) for a in (c, 1 - c)]
    t_self = pltpu.make_async_copy(tall_f, out2.at[:, :, half_at[0]], t_s.at[0])
    there_same, there_cross = device_at(other_q(me)), device_at(other_q(twin))
    t_twin = sending(tall_f, out2.at[:, :, half_at[0]], t_s.at[0], t_r.at[0], twin_id)
    t_same = sending(tall_f, out2.at[:, :, half_at[0]], t_s.at[1], t_r.at[1], there_same)
    t_cross = sending(tall_f, out2.at[:, :, half_at[0]], t_s.at[1], t_r.at[2], there_cross)

    @pl.when(stays)
    def _():
        t_self.start()
        t_same.start()

    @pl.when(jnp.logical_not(stays))
    def _():
        t_twin.start()
        t_cross.start()

    for k, out in enumerate((out0, out1)):
        for n, mate in enumerate(mates):
            arrive(out.at[:, cols_at(mate)], fin_s.at[k, n], fin_r.at[k, n], device_at(mate))

    @pl.when(stays)
    def _():
        arrive(out2.at[:, :, half_at[1]], t_s.at[0], t_r.at[0], twin_id)
        t_self.wait()
        t_same.wait_send()

    @pl.when(jnp.logical_not(stays))
    def _():
        arrive(out2.at[:, :, half_at[0]], t_s.at[1], t_r.at[1], there_same)
        arrive(out2.at[:, :, half_at[1]], t_s.at[1], t_r.at[2], there_cross)
        t_twin.wait_send()
        t_cross.wait_send()

    tok_mine().wait()
    for cp in kept:
        cp.wait()
    for cp in sent:
        cp.wait_send()


def back(lengths, q_heads, o_heads, lse, gv, d_att, kv, window, first, dwo, g1, g2, base):
    bf, f32, dma = jnp.bfloat16, jnp.float32, pltpu.SemaphoreType.DMA
    lands = []
    for part in range(3):
        for phase in range(3):
            for k in STREAMS:
                order = SUM_ORDERS[k][part]
                size = dict(DIM_SIZE)
                for dim, names in (("x", ("x",)), ("y", ("m", "yp")), ("z", ("zh", "q"))):
                    if dim in order[: phase + 1]:
                        for name in names:
                            size[name] = 1
                count = (2, 2) if phase == 0 else (EXTENT[order[phase]] - 1,)
                lands.append(pltpu.VMEM((*count, *(size[d] for d in dims_of(k)), 8, HALF), bf))
    whole = [pltpu.VMEM(WIDE, bf), pltpu.VMEM(TALL, bf)]
    return pl.pallas_call(
        back_kernel,
        name="back",
        out_shape=(
            jax.ShapeDtypeStruct((6, 3072), f32),
            jax.ShapeDtypeStruct((6, 3072), f32),
            jax.ShapeDtypeStruct((3, 8, 768), f32),
            jax.ShapeDtypeStruct((16, 768), f32),
            jax.ShapeDtypeStruct((TILE, 768), f32),
        ),
        in_specs=[IN_VMEM] * 5 + [ANY_SPACE] * 8,
        out_specs=(ANY_SPACE, ANY_SPACE, ANY_SPACE, IN_VMEM, ANY_SPACE),
        scratch_shapes=[
            pltpu.VMEM(WIDE, bf), *whole, pltpu.VMEM((4, 4, 2, 3, 8, HALF), bf), *whole, *lands,
            pltpu.VMEM((24, HALF), f32),
            pltpu.VMEM((2, 4, 6, HALF), f32),
            pltpu.VMEM((3, 8, HALF), f32),
            pltpu.VMEM((2, 16, 768), f32),
            pltpu.VMEM((4, 16, 768), bf),
            pltpu.VMEM((4, 16, 768), bf),
            pltpu.VMEM((8, 16, 768), bf),
            pltpu.VMEM((2, 3, 2, TILE, 768), bf),
            pltpu.VMEM((3, 2, TILE, 768), bf),
            pltpu.VMEM((2, 2, TILE, 768), bf),
            pltpu.VMEM((TILE, 768), bf),
            pltpu.VMEM((TILE, 768), bf),
            pltpu.VMEM((TILE, 768), f32),
            pltpu.VMEM((2, 12, TILE, HALF), bf),
            pltpu.VMEM((12, TILE, 768), bf),
            pltpu.VMEM((3, 768, HALF), bf),
            pltpu.VMEM((2, 12, TILE, HALF), bf),
            pltpu.VMEM((2, 8, TILE, 128), f32),
            pltpu.VMEM((2, TILE, HALF), bf),
            pltpu.VMEM((6, 128, TILE), f32),
            pltpu.VMEM((3, 768, HALF), f32),
            pltpu.VMEM((1, HALF), f32),
            pltpu.VMEM((1, HALF), f32),
            pltpu.VMEM((2, 1, TILE), jnp.int32),
            pltpu.VMEM((12, TILE, 1), jnp.int32),
            pltpu.VMEM((2, TILE, HALF), bf),
            dma((12, 3)), dma((12, 3)), dma((12, 3)), dma((3, 2, 8, 3)), dma((3, 2, 8, 3)), dma((6, 2, 3)), dma((6, 2, 3)),
            dma((2, 8)), dma((2, 7)),
            dma((2,)), dma((3,)), dma((4, 8)), dma((4, 8)), dma((8,)), dma((8,)), dma((1,)), dma((6,)), dma((1,)), dma((1,)),
        ],
        compiler_params=pltpu.CompilerParams(collective_id=2, has_side_effects=True, vmem_limit_bytes=63 << 20),
    )(lengths, q_heads, o_heads, lse, gv, d_att, kv, window, first, dwo, g1, g2, base)


def dot32(a, b):
    return jnp.dot(a, b, preferred_element_type=jnp.float32)


def lanes_low(rows):
    return lax.broadcasted_iota(jnp.int32, (rows, 128), 1) < HEAD_DIM


def across_lanes(a, b):
    return lax.dot_general(a, b, (((1,), (1,)), ((), ())), preferred_element_type=jnp.float32)


def flipped(a):
    return jnp.swapaxes(a, 0, 1)


def norm_parts(resid):
    centred = resid - jnp.mean(resid, axis=1, keepdims=True)
    inverse = lax.rsqrt(jnp.mean(centred * centred, axis=1, keepdims=True) + NORM_EPS)
    return centred * inverse, inverse


def norm_back(upstream, gain, n, inverse):
    e = upstream * gain
    return inverse * (e - jnp.mean(e, axis=1, keepdims=True) - n * jnp.mean(e * n, axis=1, keepdims=True))


def row_sum(a):
    return jnp.sum(a, axis=0, keepdims=True)


def mlp_kernel(
    att_ref, tok_ref, cot_ref, rows, bias_in, first, second, third,
    out_ref, d_one_ref, d_att_ref, dwo_ref, dw_in_ref, dw_down_ref, sums_ref,
    w_out, w_in, w_down, n_one, low, low_flip, slope, active, wide, sem,
):
    f32, bf = jnp.float32, jnp.bfloat16
    loads = [pltpu.make_async_copy(first.at[:, 3], w_out, sem.at[0])]
    loads += [pltpu.make_async_copy(second, w_in, sem.at[1]), pltpu.make_async_copy(third, w_down, sem.at[2])]
    for cp in loads:
        cp.start()

    def row(n):
        return rows[n : n + 1]

    halves = (slice(0, HALF), slice(HALF, 768))
    loads[0].wait()
    att = att_ref[...]
    for h in range(2):
        wide[:, halves[h]] = dot32(att, w_out[h])
    one, inverse_one = norm_parts(tok_ref[...].astype(f32) + (wide[...] + row(2)))
    n_one[...] = one
    normed = one * row(3) + row(4)
    low[...] = normed.astype(bf)
    low_flip[...] = flipped(low[...])
    wide[...] = normed + row(5)
    loads[1].wait()
    loads[2].wait()

    def up(m, carry):
        h = dot32(low[...], w_in[lax.rem(m, 2), m // 2]) + bias_in[m]
        cdf = 0.5 * (1.0 + lax.erf(h * 0.7071067811865476))
        slope[m] = cdf + h * jnp.exp(h * h * -0.5) * 0.3989422804014327
        a = (h * cdf).astype(bf)
        active[m] = flipped(a)
        for k in range(2):
            wide[:, halves[k]] += dot32(a, w_down[k, m])
        return carry

    lax.fori_loop(0, 8, up, 0)
    two, inverse_two = norm_parts(wide[...])
    out_ref[...] = (two * row(6) + row(7)).astype(bf)
    upstream = cot_ref[...].astype(f32)
    sums_ref[0:2] = jnp.zeros((2, 768), f32)
    sums_ref[12:16] = jnp.zeros((4, 768), f32)
    sums_ref[6:7] = row_sum(upstream * two)
    sums_ref[7:8] = row_sum(upstream)
    d_two = norm_back(upstream, row(6), two, inverse_two)
    sums_ref[5:6] = row_sum(d_two)
    d_low = d_two.astype(bf)
    wide[...] = d_two

    def down(m, carry):
        d_active = None
        for k in range(2):
            d_half = d_low[:, halves[k]]
            dw_down_ref[k, m] = dot32(active[m], d_half).astype(bf)
            part = across_lanes(d_half, w_down[k, m])
            d_active = part if d_active is None else d_active + part
        d_hidden = (d_active * slope[m]).astype(bf)
        sums_ref[pl.ds(8 + m // 2, 1), pl.ds(pl.multiple_of(lax.rem(m, 2) * HALF, 128), HALF)] = row_sum(d_hidden.astype(f32))
        dw_in_ref[lax.rem(m, 2), m // 2] = dot32(low_flip[...], d_hidden).astype(bf)
        wide[...] += across_lanes(d_hidden, w_in[lax.rem(m, 2), m // 2])
        return carry

    lax.fori_loop(0, 8, down, 0)
    d_normed = wide[...]
    one = n_one[...]
    sums_ref[3:4] = row_sum(d_normed * one)
    sums_ref[4:5] = row_sum(d_normed)
    d_one = norm_back(d_normed, row(3), one, inverse_one)
    d_one_ref[...] = d_one
    sums_ref[2:3] = row_sum(d_one)
    d_low = d_one.astype(bf)
    att_flip = flipped(att_ref[...])
    d_att = None
    for h in range(2):
        d_half = d_low[:, halves[h]]
        dwo_ref[h] = dot32(att_flip, d_half).astype(bf)
        part = across_lanes(d_half, w_out[h])
        d_att = part if d_att is None else d_att + part
    d_att_ref[...] = d_att.astype(bf)


def mlp(att, tokens, cotangent, rows, bias_in, first, second, third):
    f32, bf = jnp.float32, jnp.bfloat16
    return pl.pallas_call(
        mlp_kernel,
        name="mlp",
        in_specs=[IN_VMEM] * 5 + [ANY_SPACE] * 3,
        out_specs=(IN_VMEM,) * 7,
        out_shape=(
            jax.ShapeDtypeStruct((TILE, 768), bf),
            jax.ShapeDtypeStruct((TILE, 768), f32),
            jax.ShapeDtypeStruct((TILE, 768), bf),
            jax.ShapeDtypeStruct((2, 768, HALF), bf),
            jax.ShapeDtypeStruct((2, 4, 768, HALF), bf),
            jax.ShapeDtypeStruct((2, 8, HALF, HALF), bf),
            jax.ShapeDtypeStruct((16, 768), f32),
        ),
        scratch_shapes=[
            pltpu.VMEM((2, 768, HALF), bf),
            pltpu.VMEM((2, 4, 768, HALF), bf),
            pltpu.VMEM((2, 8, HALF, HALF), bf),
            pltpu.VMEM((TILE, 768), f32),
            pltpu.VMEM((TILE, 768), bf),
            pltpu.VMEM((768, TILE), bf),
            pltpu.VMEM((8, TILE, HALF), f32),
            pltpu.VMEM((8, HALF, TILE), bf),
            pltpu.VMEM((TILE, 768), f32),
            pltpu.SemaphoreType.DMA((3,)),
        ],
        compiler_params=pltpu.CompilerParams(vmem_limit_bytes=58 << 20),
    )(att, tokens, cotangent, rows, bias_in, first, second, third)


def body(
    tokens, w_qkv, bias_q, bias_v, w_out, bias_out, gain_one, shift_one, w_in, bias_in,
    w_down, bias_down, gain_two, shift_two, doc_lengths, cotangent,
):
    shard = lax.axis_index("shard")
    f32 = jnp.float32
    width = tokens.shape[1]

    vectors = (bias_q, bias_v, bias_out, gain_one, shift_one, bias_down, gain_two, shift_two)
    vec = jnp.concatenate(
        [
            jnp.stack(vectors).astype(f32),
            jnp.pad(bias_in.astype(f32).reshape(1, 24), ((0, 7), (0, 0))),
            jnp.zeros((8, 98), f32),
        ],
        axis=1,
    )
    cat = jnp.stack([jnp.concatenate([w_qkv, w_out], axis=1), w_in])
    lengths = doc_lengths.reshape(1, 128)
    first, second, third, rows, hidden_bias, window, kv, q_heads, o_heads, lse, attended = front(
        lengths, cat, w_down.reshape(3, 8, width), vec, tokens
    )
    first = first.reshape(2, 4, width, HALF)
    second = second.reshape(2, 4, width, HALF)
    third = third.reshape(2, 8, HALF, HALF)
    window = window.reshape(12, TILE, width)
    layer_out, d_one, d_att, dw_out, dw_in, dw_down, sums = mlp(
        attended, tokens, cotangent, rows, hidden_bias, first, second, third
    )
    sum_first, sum_in, sum_down, sum_vec, grad_tokens = back(
        lengths, q_heads, o_heads, lse, sums, d_att, kv, window, first,
        dw_out.reshape(2, 4, 4, 2, 3, 8, HALF), dw_in.reshape(2, *WIDE), dw_down.reshape(2, *TALL), d_one,
    )
    own = lax.dynamic_slice(sum_vec, (0, 6 * shard), (8, 6))
    own_in = lax.dynamic_slice(sum_vec[8:12].reshape(-1), (24 * shard,), (24,))
    return (
        layer_out, grad_tokens, sum_first[:, : 3 * width], own[0], own[1], sum_first[:, 3 * width :],
        own[2], own[3], own[4], sum_in, own_in, sum_down.reshape(24, width), own[5], own[6], own[7],
    )


def solution(mesh):
    both, own = P(("shard", "seq"), None), P("shard")
    rows = P("shard", None)
    return jax.shard_map(
        body,
        mesh=mesh,
        in_specs=(both, rows, own, own, rows, own, own, own, rows, own, rows, own, own, own, P(), both),
        out_specs=(both, both, rows, own, own, rows, own, own, own, rows, own, rows, own, own, own),
        check_vma=False,
    )
```

```python
import functools
import jax
import jax.numpy as jnp
from jax import lax
from jax.experimental import pallas as pl
from jax.experimental.pallas import tpu as pltpu
from jax.sharding import PartitionSpec as P

HEAD_DIM = 64
NORM_EPS = 1e-12
MESH = pl.DeviceIdType.MESH
ANY_SPACE = pl.BlockSpec(memory_space=pl.ANY)
IN_VMEM = pl.BlockSpec(memory_space=pltpu.VMEM)
LOG2E = 1.4426950408889634
TILE = 256
HALF = 384
BOTTOM = -1e30
EXTENT = {"x": 4, "y": 4, "z": 8}
ORDERS = (("z", "y", "x"), ("z", "y", "x"), ("z", "x", "y"))
X_FIRST, Y_FIRST = ("x", "y", "z"), ("y", "x", "z")
SUM_ORDERS = ((X_FIRST, X_FIRST, Y_FIRST), (X_FIRST, Y_FIRST, X_FIRST), (X_FIRST, X_FIRST, Y_FIRST))
OTHERS = {dim: range(1, size) for dim, size in EXTENT.items()}
HALVES = (((0, 256), (256, 128)), ((0, 128), (128, 256)), ((0, 256), (256, 128)))
STREAMS = (0, 1, 2)
WIDE = (2, 2, 4, 4, 2, 3, 8, HALF)
TALL = (4, 4, 2, 2, 2, 3, 8, HALF)


def place():
    s = lax.axis_index("shard")
    q = lax.axis_index("seq")
    return {
        "c": lax.rem(s, 2),
        "y": lax.rem(s // 2, 4),
        "x": s // 32,
        "z": lax.rem(s // 8, 4) * 2 + q,
    }


def device_at(at):
    return {
        "shard": ((at["x"] * 4 + at["z"] // 2) * 4 + at["y"]) * 2 + at["c"],
        "seq": lax.rem(at["z"], 2),
    }


def moved(at, **steps):
    new = dict(at)
    for dim, step in steps.items():
        size = 2 if dim == "c" else EXTENT[dim]
        new[dim] = lax.rem(at[dim] + step + size, size)
    return new


def stream_mates():
    s = lax.axis_index("shard")
    q = lax.axis_index("seq")
    partner = {"shard": s, "seq": 1 - q}
    after = {"shard": lax.rem(s + 2, 128), "seq": q}
    before = {"shard": lax.rem(s + 126, 128), "seq": q}
    return partner, before, after


def greet(targets):
    barrier = pltpu.get_barrier_semaphore()
    for target in targets:
        pl.semaphore_signal(barrier, inc=1, device_id=target, device_id_type=MESH)
    pl.semaphore_wait(barrier, len(targets))


def sending(src, dst, send, recv, target):
    return pltpu.make_async_remote_copy(
        src_ref=src, dst_ref=dst, send_sem=send, recv_sem=recv, device_id=target, device_id_type=MESH
    )


def neighbours(at):
    return [moved(at, **{d: step}) for d in ("x", "y", "z") for step in (1, -1)]


def octet_mates(me):
    across = dict(me)
    across["y"] = me["y"] + 1 - 2 * lax.rem(me["y"], 2)
    twin = moved(me, c=1)
    diagonal = dict(across)
    diagonal["c"] = twin["c"]
    return twin, across, diagonal


def span(index):
    return slice(None) if index is None else pl.ds(index, 1)


def picks_of(sets, gone=()):
    x, y, z = sets["x"], sets["y"], sets["z"]
    pick = {
        "x": x,
        "m": None if y is None else y // 2,
        "yp": None if y is None else lax.rem(y, 2),
        "zh": None if z is None else z // 2,
        "q": None if z is None else lax.rem(z, 2),
    }
    names = {"x": ("x",), "y": ("m", "yp"), "z": ("zh", "q")}
    for dim in gone:
        for name in names[dim]:
            pick[name] = 0
    return pick


WIDE_DIMS = ("yp", "q", "x", "zh", "m")
TALL_DIMS = ("x", "zh", "m", "yp", "q")
DIM_SIZE = {"yp": 2, "q": 2, "x": 4, "zh": 4, "m": 2}


def dims_of(k):
    return TALL_DIMS if k == 2 else WIDE_DIMS


def view(ref, k, part, sets, half=None, gone=(), lead=()):
    pick = picks_of(sets, gone)
    cut = (0, HALF) if half is None else HALVES[k][half]
    at = tuple(span(pick[d]) for d in dims_of(k))
    rows = () if part is None else (part,)
    return ref.at[(*lead, *at, *rows, slice(None), pl.ds(*cut))]


def find_docs(lengths, q_docs, k_docs):
    shard, seq = lax.axis_index("shard"), lax.axis_index("seq")
    stream_len = 128 * 2 * TILE
    row = lax.broadcasted_iota(jnp.int32, (128, 128), 0)
    column = lax.broadcasted_iota(jnp.int32, (128, 128), 1)
    wide = jnp.broadcast_to(lengths[...], (128, 128))
    starts_down = jnp.sum(jnp.where(column < row, wide, 0), axis=1, keepdims=True)
    lengths_down = jnp.sum(jnp.where(column == row, wide, 0), axis=1, keepdims=True)
    starts_across = jnp.sum(jnp.where(row < column, jnp.broadcast_to(lengths_down, (128, 128)), 0), axis=0, keepdims=True)
    origin = (shard // 2 - 1) * (4 * TILE)

    def tile(t, carry):
        at = origin + t * TILE + lax.broadcasted_iota(jnp.int32, (TILE, 1), 0)
        counted = jnp.sum((at >= starts_across).astype(jnp.int32), axis=1, keepdims=True) - 1
        k_docs[t] = jnp.where(at < stream_len, counted, stream_len)
        return carry

    lax.fori_loop(0, 12, tile, 0)
    for i in range(2):
        at = origin + (4 + seq + 2 * i) * TILE + lax.broadcasted_iota(jnp.int32, (1, TILE), 1)
        q_docs[i] = jnp.sum((starts_down <= at).astype(jnp.int32), axis=0, keepdims=True) - 1


def front_kernel(
    lengths, cat_ref, down_ref, vec_ref, tok_ref,
    first, second, third, rows_out, bias_in_out, window_out, kv_out, q_heads, o_heads, lse, attended,
    q_docs, k_docs,    land, stage, own, vecs, window, kv, w_heads, w_flat, top, total, acc,
    oct_s, oct_r, local, near_s, near_r, send, recv, core_s, core_r, vec_s, vec_r, tok_s, tok_r, keep, att_s, att_r,
):
    me = place()
    c, x, y, z = me["c"], me["x"], me["y"], me["z"]
    yp, q, m, zh = lax.rem(y, 2), lax.rem(z, 2), y // 2, z // 2
    outs = (first, second, third)
    twin, across, diagonal = octet_mates(me)
    twin_id = device_at(twin)
    partner, before, after = stream_mates()
    lines = [moved(me, **{d: o}) for d in EXTENT for o in OTHERS[d]]
    greet([device_at(a) for a in lines + [twin, diagonal]] + [before, after])

    def chunk_of(at):
        cols = (lax.rem(at["y"], 2) * 2 + q) * 768 + at["c"] * HALF
        return cat_ref.at[:, :, pl.ds(pl.multiple_of(cols, 128), HALF)]

    index = yp * 2 + c
    mates = (twin, across, diagonal)
    out = [
        sending(chunk_of(mate), land.at[:, index], oct_s.at[k], oct_r.at[k], device_at(mate))
        for k, mate in enumerate(mates)
    ]
    for cp in out:
        cp.start()
    kept = pltpu.make_async_copy(chunk_of(me), land.at[:, index], local.at[0])
    kept.start()
    gives = q == c
    down_out = sending(
        down_ref.at[:, :, pl.ds(pl.multiple_of((1 - c) * HALF, 128), HALF)], own.at[2], oct_s.at[3], oct_r.at[3], twin_id
    )
    down_kept = pltpu.make_async_copy(
        down_ref.at[:, :, pl.ds(pl.multiple_of(c * HALF, 128), HALF)], own.at[2], local.at[1]
    )

    @pl.when(gives)
    def _():
        down_out.start()
        down_kept.start()

    vec_kept = pltpu.make_async_copy(vec_ref, vecs.at[c, x, zh, y], local.at[2])
    vec_kept.start()

    sent = []

    def go(src, dst, send_sem, recv_sem, target):
        cp = sending(src, dst, send_sem, recv_sem, target)
        cp.start()
        sent.append(cp)

    def arrive(dst, send_sem, recv_sem, target):
        sending(dst, dst, send_sem, recv_sem, target).wait_recv()

    def tok_go(src, dst, at, target):
        go(src, dst, tok_s.at[at], tok_r.at[at], target)

    tok_kept = pltpu.make_async_copy(tok_ref, window.at[1, c, q], local.at[3])

    def tok_start():
        tok_kept.start()
        tok_go(tok_ref, window.at[1, c, q], 0, partner)
        tok_go(tok_ref, window.at[0, c, q], 1, after)
        tok_go(tok_ref, window.at[2, c, q], 2, before)
        tok_go(tok_ref, window.at[1, c, q], 3, twin_id)

    def tok_forward():
        theirs = window.at[1, c, 1 - q]
        arrive(theirs, tok_s.at[0], tok_r.at[0], partner)
        tok_go(theirs, window.at[0, c, 1 - q], 4, after)
        tok_go(theirs, window.at[2, c, 1 - q], 5, before)
        tok_go(theirs, window.at[1, c, 1 - q], 6, twin_id)

    def tok_share(h, first_slot, at):
        arrive(window.at[0, c, h], tok_s.at[first_slot], tok_r.at[first_slot], before)
        arrive(window.at[2, c, h], tok_s.at[first_slot + 1], tok_r.at[first_slot + 1], after)
        tok_go(window.at[0, c, h], window.at[0, c, h], at, twin_id)
        tok_go(window.at[2, c, h], window.at[2, c, h], at + 1, twin_id)

    vec_rounds = (("x", (1, 2, 3)), ("y", (1, 2, 3)), ("z", (2, 4, 6)), ("c", (1,)))

    def vec_copies(number, arriving):
        dim, steps = vec_rounds[number]
        done = [d for d, _ in vec_rounds[:number]]
        copies = []
        for k, step in enumerate(steps):
            source = moved(me, **{dim: (1 if dim == "c" else -step)}) if arriving else me
            pick = [None if d in done else (source["z"] // 2 if d == "z" else source[d]) for d in ("c", "x", "z", "y")]
            ref = vecs.at[tuple(span(p) for p in pick)]
            copies.append(
                sending(ref, ref, vec_s.at[number, k], vec_r.at[number, k], device_at(moved(me, **{dim: step})))
            )
        return copies

    def vec_start(number):
        for cp in vec_copies(number, False):
            cp.start()
            sent.append(cp)

    def vec_wait(number):
        for cp in vec_copies(number, True):
            cp.wait_recv()

    kept.wait()
    for k, mate in enumerate(mates):
        mate_index = lax.rem(mate["y"], 2) * 2 + mate["c"]
        arrive(land.at[:, mate_index], oct_s.at[k], oct_r.at[k], device_at(mate))
    for k in range(2):
        for owner in range(4):
            stage[pl.ds(6 * owner, 6), :] = land[k, owner].astype(jnp.float32)
        for part in range(3):
            own[k, part] = stage[pl.ds(8 * part, 8), :].astype(jnp.bfloat16)

    @pl.when(gives)
    def _():
        down_kept.wait()

    @pl.when(jnp.logical_not(gives))
    def _():
        down_out.wait_recv()

    homes = (first.at[c, yp, q, x, zh, m], second.at[c, yp, q, x, zh, m], third.at[c, x, zh, m, yp, q])
    flush = [pltpu.make_async_copy(own.at[k], homes[k], local.at[4 + k]) for k in STREAMS]
    for cp in flush:
        cp.start()
    twins = []

    def share(k, part, sets, half, slot):
        mine = view(outs[k], k, part, sets, half, (), (c,))
        theirs = view(outs[k], k, part, sets, half, (), (1 - c,))
        go(mine, mine, core_s.at[slot, k], core_r.at[slot, k], twin_id)
        twins.append((theirs, core_s.at[slot, k], core_r.at[slot, k]))

    def sets_at(part, phase, index):
        sets = {"x": x, "y": y, "z": z}
        for earlier in ORDERS[part][:phase]:
            sets[earlier] = None
        dim = ORDERS[part][phase]
        sets[dim] = lax.rem(index + EXTENT[dim], EXTENT[dim])
        return sets

    def near(k, part, phase, arriving):
        dim = ORDERS[part][phase]
        for o in OTHERS[dim]:
            sems = near_s.at[part, phase, o, k], near_r.at[part, phase, o, k]
            target = device_at(moved(me, **{dim: o}))
            if arriving:
                arrive(view(outs[k], k, part, sets_at(part, phase, me[dim] - o), None, (), (c,)), *sems, target)
            elif phase == 0:
                go(own.at[k, part], homes[k].at[part], *sems, target)
            else:
                ref = view(outs[k], k, part, sets_at(part, phase, me[dim]), None, (), (c,))
                go(ref, ref, *sems, target)

    def ring(k, part, step, arriving):
        dim = ORDERS[part][2]
        size = EXTENT[dim]
        for direction, sign in enumerate((1, -1)):
            sets = sets_at(part, 2, me[dim] - sign * (step if arriving else step - 1))
            half = direction if step == size // 2 else None
            ref = view(outs[k], k, part, sets, half, (), (c,))
            slot = part * 2 + step - 1
            sems = send.at[slot, direction, k], recv.at[slot, direction, k]
            target = device_at(moved(me, **{dim: sign}))
            if arriving:
                arrive(ref, *sems, target)
            else:
                go(ref, ref, *sems, target)

    def ring_share(k, part, step):
        dim = ORDERS[part][2]
        for direction, sign in enumerate((1, -1)):
            half = direction if step == EXTENT[dim] // 2 else None
            share(k, part, sets_at(part, 2, me[dim] - sign * step), half, 3 + (part * 2 + step - 1) * 2 + direction)

    parts = range(3)
    late = [(k, part) for k in (1, 2) for part in parts]
    for part in parts:
        near(0, part, 0, False)
    vec_kept.wait()
    vec_start(0)
    for k, part in late:
        near(k, part, 0, False)
    find_docs(lengths, q_docs, k_docs)
    for cp in flush:
        cp.wait()
    for part in parts:
        near(0, part, 0, True)
        near(0, part, 1, False)
    tok_start()
    vec_wait(0)
    vec_start(1)
    for part in parts:
        near(0, part, 1, True)
        ring(0, part, 1, False)
    for k, part in late:
        near(k, part, 0, True)
        near(k, part, 1, False)
    vec_wait(1)
    vec_start(2)
    tok_forward()
    for part in parts:
        ring(0, part, 1, True)
        ring(0, part, 2, False)
    vec_wait(2)
    vec_start(3)
    for k, part in late:
        near(k, part, 1, True)
        ring(k, part, 1, False)
    for k, part in late:
        share(k, part, sets_at(part, 2, me[ORDERS[part][2]]), None, part)
    vec_wait(3)
    for v in range(8):
        rows_out[v : v + 1] = jnp.zeros((1, 768), jnp.float32)
    lane = lax.broadcasted_iota(jnp.int32, (128, HALF), 0)
    line = lax.broadcasted_iota(jnp.int32, (512, HALF), 0)
    values = [vecs[owner_core].reshape(512, 128).astype(jnp.bfloat16) for owner_core in range(2)]
    for h in range(2):
        column = h * HALF + lax.broadcasted_iota(jnp.int32, (1, HALF), 1)
        cols = slice(h * HALF, (h + 1) * HALF)
        for owner_core in range(2):
            place_in = lax.rem(column, 12) - 6 * owner_core
            picked = dot32(values[owner_core], jnp.logical_and(lane == place_in, lane < 6).astype(jnp.bfloat16))
            for v in range(8):
                rows_out[v : v + 1, cols] += row_sum(jnp.where(line == column // 12 * 8 + v, picked, 0.0))

    def hidden_row(m, carry):
        column = m * HALF + lax.broadcasted_iota(jnp.int32, (1, HALF), 1)
        total = jnp.zeros((1, HALF), jnp.float32)
        for owner_core in range(2):
            place_in = lax.rem(column, 48) - 24 * owner_core
            inside = jnp.logical_and(place_in >= 0, place_in < 24)
            picked = dot32(values[owner_core], jnp.logical_and(lane == place_in + 6, inside).astype(jnp.bfloat16))
            total = total + row_sum(jnp.where(line == column // 48 * 8, picked, 0.0))
        bias_in_out[m] = total
        return carry

    lax.fori_loop(0, 8, hidden_row, 0)
    for part in parts:
        ring(0, part, 2, True)
    load = pltpu.make_async_copy(first.at[c, pl.ds(0, 2), pl.ds(0, 2)], w_heads, keep.at[1])
    load.start()
    go(first.at[c, 1, 1], first.at[c, 1, 1], core_s.at[0, 0], core_r.at[0, 0], twin_id)
    twins.append((first.at[1 - c, 1, 1], core_s.at[0, 0], core_r.at[0, 0]))

    own_half = pl.ds(pl.multiple_of(c * HALF, 128), HALF)
    bias = [rows_out[v : v + 1, own_half] for v in range(2)]
    arrive(window.at[1, 1 - c, q], tok_s.at[3], tok_r.at[3], twin_id)
    arrive(window.at[1, 1 - c, 1 - q], tok_s.at[6], tok_r.at[6], twin_id)
    tok_kept.wait()
    load.wait()

    def project_group(group):
        def one(n, carry):
            core, h = n // 2, lax.rem(n, 2)
            x_tile, t = window[group, core, h], group * 4 + n
            kv[0, t] = dot32(x_tile, weights(1)).astype(jnp.bfloat16)
            kv[1, t] = (dot32(x_tile, weights(2)) + bias[1]).astype(jnp.bfloat16)
            return carry

        lax.fori_loop(0, 4, one, 0)

    def flatten(i, carry):
        rows = pl.ds(pl.multiple_of(i * 192, 192), 192)
        for number in range(3):
            piece = w_heads[number // 2, number % 2, i].astype(jnp.float32)
            w_flat[number, rows] = piece.reshape(192, HALF).astype(jnp.bfloat16)
        return carry

    lax.fori_loop(0, 4, flatten, 0)

    def weights(number):
        return w_flat[number]

    low = lanes_low(TILE)
    scale = HEAD_DIM ** -0.5 * LOG2E

    def heads_front(pair, i, near_by):
        cols = slice(pair * 128, (pair + 1) * 128) if isinstance(pair, int) else pl.ds(pl.multiple_of(pair * 128, 128), 128)
        at = pair * 2 + i
        qs = q_heads[i, :, cols]
        none = jnp.zeros_like(qs)
        queries = (jnp.where(low, qs, none), jnp.where(low, none, qs))
        if near_by:
            top[at] = jnp.full((2, 1, TILE), BOTTOM, jnp.float32)
            total[at] = jnp.zeros((2, 1, TILE), jnp.float32)
            acc[at] = jnp.zeros((128, TILE), jnp.float32)

        def step(n, carry):
            u = q + 2 * i + n
            t = 4 + n if near_by else u + 4 * (u // 4)
            k, v = kv[0, t, :, cols], flipped(kv[1, t, :, cols])
            same = q_docs[i] == k_docs[t]
            scores = [jnp.where(same, across_lanes(k, queries[head]) * scale, BOTTOM) for head in range(2)]
            old = [top[at, head] for head in range(2)]
            new = [jnp.maximum(old[head], jnp.max(scores[head], axis=0, keepdims=True)) for head in range(2)]
            fade = [jnp.exp2(old[head] - new[head]) for head in range(2)]
            p = [jnp.exp2(scores[head] - new[head]) for head in range(2)]
            sums = [total[at, head] * fade[head] + jnp.sum(p[head], axis=0, keepdims=True) for head in range(2)]
            adds = [dot32(v[head * HEAD_DIM : (head + 1) * HEAD_DIM], p[head].astype(jnp.bfloat16)) for head in range(2)]
            for head in range(2):
                rows = slice(head * HEAD_DIM, (head + 1) * HEAD_DIM)
                acc[at, rows] = acc[at, rows] * fade[head] + adds[head]
                total[at, head] = sums[head]
                top[at, head] = new[head]
            return carry

        lax.fori_loop(0, 4 if near_by else 5, step, 0)
        if not near_by:
            for head in range(2):
                rows = slice(head * HEAD_DIM, (head + 1) * HEAD_DIM)
                acc[at, rows] = acc[at, rows] / total[at, head]
                lse[pair, i, head : head + 1] = top[at, head] + jnp.log2(total[at, head])
            o_heads[i, :, cols] = flipped(acc[at]).astype(jnp.bfloat16)

    def all_pairs(i, near_by):
        lax.fori_loop(0, 3, lambda pair, carry: (heads_front(pair, i, near_by), carry)[1], 0)

    for i in range(2):
        q_heads[i] = (dot32(window[1, i, q], weights(0)) + bias[0]).astype(jnp.bfloat16)
    project_group(1)
    all_pairs(0, True)
    tok_share(q, 1, 7)
    all_pairs(1, True)
    tok_share(1 - q, 4, 9)
    for part in parts:
        ring(1, part, 1, True)
        ring(1, part, 2, False)
    for h, at in ((q, 7), (1 - q, 9)):
        arrive(window.at[0, 1 - c, h], tok_s.at[at], tok_r.at[at], twin_id)
        arrive(window.at[2, 1 - c, h], tok_s.at[at + 1], tok_r.at[at + 1], twin_id)
    kept_window = pltpu.make_async_copy(window, window_out, keep.at[2])
    kept_window.start()
    project_group(0)
    for part in parts:
        ring(2, part, 1, True)
        ring(2, part, 2, False)
    project_group(2)
    kept_kv = pltpu.make_async_copy(kv, kv_out, keep.at[3])
    kept_kv.start()
    for part in parts:
        ring_share(1, part, 1)
    heads_front(0, 0, False)
    heads_front(1, 0, False)
    for part in parts:
        ring_share(2, part, 1)
    heads_front(2, 0, False)
    for part in parts:
        ring(1, part, 2, True)
        ring_share(1, part, 2)
    all_pairs(1, False)
    mine_cols, other_cols = (pl.ds(pl.multiple_of(a * HALF, 128), HALF) for a in (c, 1 - c))
    go(o_heads.at[1 - c], attended.at[:, mine_cols], att_s.at[0], att_r.at[0], twin_id)
    kept_att = pltpu.make_async_copy(o_heads.at[c], attended.at[:, mine_cols], keep.at[4])
    kept_att.start()
    for part in parts:
        ring(2, part, 2, True)
        ring_share(2, part, 2)
    for ref, send_sem, recv_sem in twins:
        arrive(ref, send_sem, recv_sem, twin_id)
    arrive(attended.at[:, other_cols], att_s.at[0], att_r.at[0], twin_id)
    for cp in (kept_window, kept_kv, kept_att):
        cp.wait()
    for cp in out + sent:
        cp.wait_send()

    @pl.when(gives)
    def _():
        down_out.wait_send()


def front(lengths, cat, down, vec, tokens):
    bf, f32, dma = jnp.bfloat16, jnp.float32, pltpu.SemaphoreType.DMA
    return pl.pallas_call(
        front_kernel,
        name="front",
        out_shape=(
            jax.ShapeDtypeStruct((2, *WIDE), bf),
            jax.ShapeDtypeStruct((2, *WIDE), bf),
            jax.ShapeDtypeStruct((2, *TALL), bf),
            jax.ShapeDtypeStruct((8, 768), f32),
            jax.ShapeDtypeStruct((8, 1, HALF), f32),
            jax.ShapeDtypeStruct((3, 2, 2, TILE, 768), bf),
            jax.ShapeDtypeStruct((2, 12, TILE, HALF), bf),
            jax.ShapeDtypeStruct((2, TILE, HALF), bf),
            jax.ShapeDtypeStruct((2, TILE, HALF), bf),
            jax.ShapeDtypeStruct((3, 2, 2, TILE), f32),
            jax.ShapeDtypeStruct((TILE, 768), bf),
        ),
        in_specs=[IN_VMEM] + [ANY_SPACE] * 4,
        out_specs=(ANY_SPACE,) * 3 + (IN_VMEM,) * 2 + (ANY_SPACE,) * 2 + (IN_VMEM,) * 4,
        scratch_shapes=[
            pltpu.VMEM((2, 1, TILE), jnp.int32),
            pltpu.VMEM((12, TILE, 1), jnp.int32),
            pltpu.VMEM((2, 4, 6, HALF), bf),
            pltpu.VMEM((24, HALF), f32),
            pltpu.VMEM((3, 3, 8, HALF), bf),
            pltpu.VMEM((2, 4, 4, 4, 8, 128), f32),
            pltpu.VMEM((3, 2, 2, TILE, 768), bf),
            pltpu.VMEM((2, 12, TILE, HALF), bf),
            pltpu.VMEM((2, 2, 4, 4, 2, 3, 8, HALF), bf),
            pltpu.VMEM((3, 768, HALF), bf),
            pltpu.VMEM((6, 2, 1, TILE), f32),
            pltpu.VMEM((6, 2, 1, TILE), f32),
            pltpu.VMEM((6, 128, TILE), f32),
            dma((4,)), dma((4,)), dma((7,)), dma((3, 2, 8, 3)), dma((3, 2, 8, 3)), dma((6, 2, 3)), dma((6, 2, 3)),
            dma((15, 3)), dma((15, 3)), dma((4, 3)), dma((4, 3)), dma((11,)), dma((11,)), dma((5,)), dma((1,)), dma((1,)),
        ],
        compiler_params=pltpu.CompilerParams(collective_id=1, has_side_effects=True, vmem_limit_bytes=62 << 20),
    )(lengths, cat, down, vec, tokens)


def back_kernel(*refs):
    (lengths, q_ref, o_ref, lse_ref, gv, d_att, kv_hbm, window_hbm, first, dwo, g1, g2, base) = refs[:13]
    (out0, out1, out2, out_v, out_tok) = refs[13:18]
    grads = (None, g1, g2)
    refs = refs[18:]
    acc, other, refs = refs[:3], refs[3:6], refs[6:]
    lands = {}
    for n, (part, phase, k) in enumerate((a, b, k) for a in range(3) for b in range(3) for k in STREAMS):
        lands[part, phase, k] = refs[n]
    refs = refs[27:]
    (
        stage, rows, tall_f, v_c, v_x, v_y, v_z, t_all, t_in, t_land, t_part, t_mate, t_base,
        kv, window, w_heads, dkv_all, dkv, dq_all, dq_acc, dw, q_rows, v_rows, q_docs, k_docs, do_ref,
        local, core_s, core_r, near_s, near_r, send, recv, fin_s, fin_r, t_s, t_r, vec_s, vec_r, tok_s, tok_r, tok_l, load, att_s, att_r,
    ) = refs
    me = place()
    c, x, y, z = me["c"], me["x"], me["y"], me["z"]
    yp, q, m, zh = lax.rem(y, 2), lax.rem(z, 2), y // 2, z // 2
    twin, across, diagonal = octet_mates(me)
    twin_id = device_at(twin)
    partner, before, after = stream_mates()

    def other_q(at):
        new = dict(at)
        new["z"] = at["z"] + 1 - 2 * lax.rem(at["z"], 2)
        return new

    ring_mates = [moved(me, **{d: k}) for d in ("x", "y", "z") for k in range(1, EXTENT[d])]
    mates = [twin, across, diagonal] + [other_q(a) for a in (me, twin, across, diagonal)]
    targets = ring_mates + [twin, diagonal] + [other_q(a) for a in (twin, across, diagonal)]
    greet([device_at(a) for a in targets] + [before, after])
    sent = []

    def go(src, dst, send_sem, recv_sem, target):
        cp = sending(src, dst, send_sem, recv_sem, target)
        cp.start()
        sent.append(cp)

    def arrive(dst, send_sem, recv_sem, target):
        sending(dst, dst, send_sem, recv_sem, target).wait_recv()

    def sets_of(k, part, phase, index):
        sets = {"x": x, "y": y, "z": z}
        order = SUM_ORDERS[k][part]
        for later in order[phase + 1:]:
            sets[later] = None
        sets[order[phase]] = lax.rem(index + 2 * EXTENT[order[phase]], EXTENT[order[phase]])
        return sets

    def add_region(k, part, sets, sources, half=None, gone=()):
        pick, from_pick = picks_of(sets), picks_of(sets, gone)
        dims = dims_of(k)
        inner = dims[3:] if k < 2 else dims[2:]
        outer = [d for d in dims if d not in inner and pick[d] is None]
        count = 1
        for d in outer:
            count *= DIM_SIZE[d]
        cut = pl.ds(*((0, HALF) if half is None else HALVES[k][half]))

        def one(i):
            at = {}
            for d in reversed(outer):
                at[d] = lax.rem(i, DIM_SIZE[d]) if count > 1 else 0
                i = i // DIM_SIZE[d]

            def index(picked):
                return tuple(
                    (at[d] if d in at else slice(None)) if picked[d] is None else pl.ds(picked[d], 1) if d in inner else picked[d]
                    for d in dims
                )

            to = (*index(pick), part, slice(None), cut)
            fr = (*index(from_pick), slice(None), cut)
            if len(sources) == 1:
                acc[k][to] = acc[k][to] + sources[0][fr]
            else:
                total = acc[k][to].astype(jnp.float32)
                for src in sources:
                    total = total + src[fr].astype(jnp.float32)
                acc[k][to] = total.astype(jnp.bfloat16)

        if count == 1:
            one(0)
        else:
            lax.fori_loop(0, count, lambda i, carry: (one(i), carry)[1], 0)

    def hop(k, part, n):
        return sets_of(k, part, 0, me[SUM_ORDERS[k][part][0]] + (2, 1, -1, 0)[n])

    own_copies = {}

    def cross(k, part, n):
        slot = part * 4 + n
        sets = hop(k, part, n)
        src = view(grads[k], k, part, sets, None, (), (1 - c,))
        go(src, view(other[k], k, part, sets), core_s.at[slot, k], core_r.at[slot, k], twin_id)
        kept = pltpu.make_async_copy(
            view(grads[k], k, part, sets, None, (), (c,)), view(acc[k], k, part, sets), local.at[slot, k]
        )
        kept.start()
        own_copies[k, part, n] = kept

    loads = [
        pltpu.make_async_copy(kv_hbm, kv, load.at[0]),
        pltpu.make_async_copy(first.at[c, pl.ds(0, 3)], w_heads, load.at[1]),
        pltpu.make_async_copy(window_hbm, window, load.at[2]),
        pltpu.make_async_copy(dwo.at[c], acc[0].at[1, 1], load.at[3]),
        pltpu.make_async_copy(base, t_base, load.at[4]),
    ]
    loads[0].start()
    own_half, other_half = (pl.ds(pl.multiple_of(a * HALF, 128), HALF) for a in (c, 1 - c))
    go(d_att.at[:, other_half], do_ref.at[c], att_s.at[0], att_r.at[0], twin_id)
    d_kept = pltpu.make_async_copy(d_att.at[:, own_half], do_ref.at[c], load.at[5])
    d_kept.start()
    for n in range(4):
        for k in (1, 2):
            for part in range(3):
                cross(k, part, n)

    for cp in loads[1:]:
        cp.start()
    go(dwo.at[1 - c], other[0], core_s.at[0, 0], core_r.at[0, 0], twin_id)

    vec_lands = (v_c, v_x, v_y, v_z)
    vec_dims = ("c", "x", "y", "z")

    def vec_start(number):
        dim, land = vec_dims[number], vec_lands[number]
        for k in range(1, land.shape[0]):
            mine = land.at[me[dim]]
            go(mine, mine, vec_s.at[number, k], vec_r.at[number, k], device_at(moved(me, **{dim: k})))

    def vec_finish(number):
        dim, land = vec_dims[number], vec_lands[number]
        size = land.shape[0]
        for k in range(1, size):
            theirs = land.at[lax.rem(me[dim] - k + size, size)]
            arrive(theirs, vec_s.at[number, k], vec_r.at[number, k], device_at(moved(me, **{dim: k})))
        total = land[0].astype(jnp.float32)
        for k in range(1, size):
            total = total + land[k].astype(jnp.float32)
        return total

    def row_blocks(fn):
        lax.fori_loop(0, TILE // 32, lambda r, carry: (fn(pl.ds(pl.multiple_of(r * 32, 32), 32)), carry)[1], 0)

    def tok_twin(group, at):
        go(t_all.at[1 - c, group], t_in.at[group], tok_s.at[at], tok_r.at[at], twin_id)

    def tok_edges():
        for n, (group, at) in enumerate(((0, 0), (2, 6))):
            arrive(t_in.at[group], tok_s.at[at], tok_r.at[at], twin_id)
        for n, h in enumerate((1 - q, q)):
            for group in (0, 2):
                def one(at):
                    t_all[c, group, h, at] = t_all[c, group, h, at] + t_in[group, h, at]
                row_blocks(one)
            go(t_all.at[c, 0, h], t_land.at[1, h], tok_s.at[1 + n], tok_r.at[1 + n], before)
            go(t_all.at[c, 2, h], t_land.at[0, h], tok_s.at[3 + n], tok_r.at[3 + n], after)

    def tok_total(h, at):
        f = jnp.float32
        return t_all[c, 1, h, at].astype(f) + t_in[1, h, at].astype(f) + t_land[0, h, at].astype(f) + t_land[1, h, at].astype(f)

    def tok_theirs():
        h = 1 - q
        arrive(t_in.at[1], tok_s.at[7], tok_r.at[7], twin_id)
        arrive(t_land.at[1, h], tok_s.at[1], tok_r.at[1], after)
        arrive(t_land.at[0, h], tok_s.at[3], tok_r.at[3], before)

        def one(at):
            t_part[at] = tok_total(h, at).astype(jnp.bfloat16)
        row_blocks(one)
        go(t_part, t_mate, tok_s.at[5], tok_r.at[5], partner)

    def tok_mine():
        arrive(t_land.at[1, q], tok_s.at[2], tok_r.at[2], after)
        arrive(t_land.at[0, q], tok_s.at[4], tok_r.at[4], before)
        arrive(t_mate, tok_s.at[5], tok_r.at[5], partner)
        loads[4].wait()

        def one(at):
            t_base[at] = tok_total(q, at) + t_mate[at].astype(jnp.float32) + t_base[at]
        row_blocks(one)
        done = pltpu.make_async_copy(t_base, out_tok, tok_l.at[0])
        done.start()
        return done

    def meet(k, part, n):
        slot = part * 4 + n
        own_copies[k, part, n].wait()
        sets = hop(k, part, n)
        arrive(view(other[k], k, part, sets), core_s.at[slot, k], core_r.at[slot, k], twin_id)
        add_region(k, part, sets, [other[k].at[(slice(None),) * 5 + (part,)]])

    def meet_out():
        loads[3].wait()
        arrive(other[0], core_s.at[0, 0], core_r.at[0, 0], twin_id)

        def one(i, carry):
            acc[0][1, 1, i] = acc[0][1, 1, i] + other[0][i]
            return carry

        lax.fori_loop(0, 4, one, 0)

    def ring(k, part, step, arriving):
        dim = SUM_ORDERS[k][part][0]
        ahead = 3 - step - (1 if arriving else 0)
        for direction, sign in enumerate((1, -1)):
            half = direction if step == 1 else None
            sets = sets_of(k, part, 0, me[dim] + sign * ahead)
            land = lands[part, 0, k].at[direction, step - 1]
            slot = part * 2 + step - 1
            sems = send.at[slot, direction, k], recv.at[slot, direction, k]
            target = device_at(moved(me, **{dim: sign}))
            here = view(land, k, None, sets, half, (dim,))
            if arriving:
                arrive(here, *sems, target)
                add_region(k, part, sets, [land], half, (dim,))
            else:
                go(view(acc[k], k, part, sets, half), here, *sems, target)

    def near(k, part, phase, arriving):
        order = SUM_ORDERS[k][part]
        dim, gone = order[phase], order[: phase + 1]
        mine = sets_of(k, part, phase, me[dim])
        sources = []
        for o in OTHERS[dim]:
            sems = near_s.at[part, phase - 1, o, k], near_r.at[part, phase - 1, o, k]
            target = device_at(moved(me, **{dim: o}))
            land = lands[part, phase, k].at[o - 1]
            here = view(land, k, None, mine, None, gone)
            if arriving:
                arrive(here, *sems, target)
                sources.append(land)
            else:
                go(view(acc[k], k, part, sets_of(k, part, phase, me[dim] + o)), here, *sems, target)
        if arriving:
            add_region(k, part, mine, sources, None, gone)

    def vec_next(n):
        total = vec_finish(n)
        if n < 3:
            vec_lands[n + 1][me[vec_dims[n + 1]]] = total.astype(jnp.bfloat16)
            vec_start(n + 1)
        else:
            out_v[...] = total

    low = lanes_low(TILE)
    scale = HEAD_DIM ** -0.5 * LOG2E
    picker = (
        lax.broadcasted_iota(jnp.int32, (8, 128), 0) == lax.broadcasted_iota(jnp.int32, (8, 128), 1) // HEAD_DIM
    ).astype(jnp.float32)

    def heads_back(pair, i, near_by):
        cols = slice(pair * 128, (pair + 1) * 128)
        place_at = pair * 2 + i
        qs, d_out = q_ref[i, :, cols], do_ref[i, :, cols]
        none = jnp.zeros_like(qs)
        q_heads = (jnp.where(low, qs, none), jnp.where(low, none, qs))
        do_heads = (jnp.where(low, d_out, none), jnp.where(low, none, d_out))
        prod = d_out.astype(jnp.float32) * o_ref[i, :, cols].astype(jnp.float32)
        deltas = lax.dot_general(
            picker, prod, (((1,), (1,)), ((), ())), precision=lax.Precision.HIGHEST, preferred_element_type=jnp.float32
        )
        if i == 0:
            dkv[...] = jnp.zeros_like(dkv)
        if not near_by:
            dq_acc[place_at] = jnp.zeros((128, TILE), jnp.float32)

        def step(n, carry):
            u = q + 2 * i + n
            t = 4 + n if near_by else u + 4 * (u // 4)
            slot = n if near_by else u
            k, v = kv[0, t, :, cols], kv[1, t, :, cols]
            k_flip = flipped(k)
            same = q_docs[i] == k_docs[t]
            heads = range(2)
            scores = [across_lanes(k, q_heads[h]) * scale for h in heads]
            dp = [across_lanes(v, do_heads[h]) for h in heads]
            p = [jnp.where(same, jnp.exp2(scores[h] - lse_ref[pair, i, h : h + 1]), 0.0) for h in heads]
            ds = [(p[h] * (dp[h] - deltas[h : h + 1])).astype(jnp.bfloat16) for h in heads]
            p_low = [p[h].astype(jnp.bfloat16) for h in heads]
            dq = [dot32(k_flip[h * HEAD_DIM : (h + 1) * HEAD_DIM], ds[h]) for h in heads]
            dk = [dot32(ds[h], q_heads[h]) for h in heads]
            dv = [dot32(p_low[h], do_heads[h]) for h in heads]
            for h in heads:
                lanes = slice(h * HEAD_DIM, (h + 1) * HEAD_DIM)
                dq_acc[place_at, lanes] = dq_acc[place_at, lanes] + dq[h]
            dkv[0, slot] = dkv[0, slot] + (dk[0] + dk[1])
            dkv[1, slot] = dkv[1, slot] + (dv[0] + dv[1])
            return carry

        lax.fori_loop(0, 4 if near_by else 5, step, 0)
        if near_by:
            dq_all[i, :, cols] = flipped(dq_acc[place_at] * HEAD_DIM ** -0.5).astype(jnp.bfloat16)
        if i == 1:
            def keep(u, carry):
                t = 4 + u if near_by else u + 4 * (u // 4)
                dkv_all[0, t, :, cols] = (dkv[0, u] * HEAD_DIM ** -0.5).astype(jnp.bfloat16)
                dkv_all[1, t, :, cols] = dkv[1, u].astype(jnp.bfloat16)
                return carry

            lax.fori_loop(0, 4 if near_by else 8, keep, 0)

    def tile_back(group, n):
        core, h = n // 2, lax.rem(n, 2)
        t = group * 4 + n
        x_flip = flipped(window[t])
        dk, dv = dkv_all[0, t], dkv_all[1, t]
        dw[1] += dot32(x_flip, dk)
        dw[2] += dot32(x_flip, dv)
        v_rows[...] = v_rows[...] + jnp.sum(dv.astype(jnp.float32), axis=0, keepdims=True)
        dx = across_lanes(dk, w_heads[1]) + across_lanes(dv, w_heads[2])
        t_all[core, group, h] = dx.astype(jnp.bfloat16)
        if group == 1:
            @pl.when(h == q)
            def _():
                dq = dq_all[core]
                dw[0] += dot32(x_flip, dq)
                q_rows[...] = q_rows[...] + jnp.sum(dq.astype(jnp.float32), axis=0, keepdims=True)
                t_all[core, group, h] = (dx + across_lanes(dq, w_heads[0])).astype(jnp.bfloat16)

    def tiles_back(group):
        lax.fori_loop(0, 4, lambda n, carry: (tile_back(group, n), carry)[1], 0)

    parts = range(3)
    late = [(k, part) for k in (1, 2) for part in parts]
    find_docs(lengths, q_docs, k_docs)
    for k, part in late:
        meet(k, part, 0)
        ring(k, part, 1, False)
    loads[0].wait()
    d_kept.wait()
    arrive(do_ref.at[1 - c], att_s.at[0], att_r.at[0], twin_id)
    heads_back(0, 0, False)
    for k, part in late:
        meet(k, part, 1)
        meet(k, part, 2)
    for part in parts:
        ring(1, part, 1, True)
        ring(1, part, 2, False)
    heads_back(0, 1, False)
    for part in parts:
        ring(2, part, 1, True)
        ring(2, part, 2, False)
    heads_back(1, 0, False)
    for k, part in late:
        meet(k, part, 3)
    meet_out()
    heads_back(1, 1, False)
    heads_back(2, 0, False)
    for part in parts:
        ring(1, part, 2, True)
        near(1, part, 1, False)
    heads_back(2, 1, False)
    loads[1].wait()
    loads[2].wait()
    dw[...] = jnp.zeros_like(dw)
    q_rows[...] = jnp.zeros_like(q_rows)
    v_rows[...] = jnp.zeros_like(v_rows)
    tiles_back(0)
    tok_twin(0, 0)
    tiles_back(2)
    tok_twin(2, 6)
    for part in parts:
        ring(2, part, 2, True)
        near(2, part, 1, False)
    heads_back(0, 0, True)
    heads_back(0, 1, True)
    for part in parts:
        near(1, part, 1, True)
        near(1, part, 2, False)
    heads_back(1, 0, True)
    heads_back(1, 1, True)
    for part in parts:
        near(2, part, 1, True)
        near(2, part, 2, False)
    heads_back(2, 0, True)
    heads_back(2, 1, True)
    for k, part in late:
        near(k, part, 2, True)
    tok_edges()
    tiles_back(1)
    tok_twin(1, 7)

    def grads_low(i, carry):
        rows_at = pl.ds(pl.multiple_of(i * 192, 192), 192)
        for number, (a, b) in enumerate(((0, 0), (0, 1), (1, 0))):
            acc[0][a, b, i] = dw[number, rows_at].reshape(4, 2, 3, 8, HALF).astype(jnp.bfloat16)
        return carry

    lax.fori_loop(0, 4, grads_low, 0)
    for part in parts:
        ring(0, part, 1, False)
    v_c[c] = gv[...]
    half_cols = pl.ds(pl.multiple_of(c * HALF, 128), HALF)
    v_c[c, 0:1, half_cols] = q_rows[...]
    v_c[c, 1:2, half_cols] = v_rows[...]
    vec_start(0)
    vec_next(0)
    for part in parts:
        ring(0, part, 1, True)
        ring(0, part, 2, False)
    vec_next(1)
    tok_theirs()
    for part in parts:
        ring(0, part, 2, True)
        near(0, part, 1, False)
    vec_next(2)
    for part in parts:
        near(0, part, 1, True)
        near(0, part, 2, False)
    vec_next(3)
    for part in parts:
        near(0, part, 2, True)

    for k in range(2):
        for part in range(3):
            stage[pl.ds(8 * part, 8), :] = acc[k][yp, q, x, zh, m, part].astype(jnp.float32)
        for owner in range(4):
            rows[k, owner] = stage[pl.ds(6 * owner, 6), :]
    for part in range(3):
        tall_f[part] = acc[2][x, zh, m, yp, q, part].astype(jnp.float32)

    def cols_at(at):
        return pl.ds(pl.multiple_of((lax.rem(at["y"], 2) * 2 + lax.rem(at["z"], 2)) * 768 + at["c"] * HALF, 128), HALF)

    def owner_of(at):
        return lax.rem(at["y"], 2) * 2 + at["c"]

    for k, out in enumerate((out0, out1)):
        for n, mate in enumerate(mates):
            go(rows.at[k, owner_of(mate)], out.at[:, cols_at(me)], fin_s.at[k, n], fin_r.at[k, n], device_at(mate))
    kept = [
        pltpu.make_async_copy(rows.at[k, owner_of(me)], out.at[:, cols_at(me)], fin_s.at[k, 7])
        for k, out in enumerate((out0, out1))
    ]
    for cp in kept:
        cp.start()
    stays = c == q
    half_at = [pl.ds(pl.multiple_of(a * HALF, 128), HALF) for a in (c, 1 - c)]
    t_self = pltpu.make_async_copy(tall_f, out2.at[:, :, half_at[0]], t_s.at[0])
    there_same, there_cross = device_at(other_q(me)), device_at(other_q(twin))
    t_twin = sending(tall_f, out2.at[:, :, half_at[0]], t_s.at[0], t_r.at[0], twin_id)
    t_same = sending(tall_f, out2.at[:, :, half_at[0]], t_s.at[1], t_r.at[1], there_same)
    t_cross = sending(tall_f, out2.at[:, :, half_at[0]], t_s.at[1], t_r.at[2], there_cross)

    @pl.when(stays)
    def _():
        t_self.start()
        t_same.start()

    @pl.when(jnp.logical_not(stays))
    def _():
        t_twin.start()
        t_cross.start()

    for k, out in enumerate((out0, out1)):
        for n, mate in enumerate(mates):
            arrive(out.at[:, cols_at(mate)], fin_s.at[k, n], fin_r.at[k, n], device_at(mate))

    @pl.when(stays)
    def _():
        arrive(out2.at[:, :, half_at[1]], t_s.at[0], t_r.at[0], twin_id)
        t_self.wait()
        t_same.wait_send()

    @pl.when(jnp.logical_not(stays))
    def _():
        arrive(out2.at[:, :, half_at[0]], t_s.at[1], t_r.at[1], there_same)
        arrive(out2.at[:, :, half_at[1]], t_s.at[1], t_r.at[2], there_cross)
        t_twin.wait_send()
        t_cross.wait_send()

    tok_mine().wait()
    for cp in kept:
        cp.wait()
    for cp in sent:
        cp.wait_send()


def back(lengths, q_heads, o_heads, lse, gv, d_att, kv, window, first, dwo, g1, g2, base):
    bf, f32, dma = jnp.bfloat16, jnp.float32, pltpu.SemaphoreType.DMA
    lands = []
    for part in range(3):
        for phase in range(3):
            for k in STREAMS:
                order = SUM_ORDERS[k][part]
                size = dict(DIM_SIZE)
                for dim, names in (("x", ("x",)), ("y", ("m", "yp")), ("z", ("zh", "q"))):
                    if dim in order[: phase + 1]:
                        for name in names:
                            size[name] = 1
                count = (2, 2) if phase == 0 else (EXTENT[order[phase]] - 1,)
                lands.append(pltpu.VMEM((*count, *(size[d] for d in dims_of(k)), 8, HALF), bf))
    whole = [pltpu.VMEM(WIDE, bf), pltpu.VMEM(TALL, bf)]
    return pl.pallas_call(
        back_kernel,
        name="back",
        out_shape=(
            jax.ShapeDtypeStruct((6, 3072), f32),
            jax.ShapeDtypeStruct((6, 3072), f32),
            jax.ShapeDtypeStruct((3, 8, 768), f32),
            jax.ShapeDtypeStruct((16, 768), f32),
            jax.ShapeDtypeStruct((TILE, 768), f32),
        ),
        in_specs=[IN_VMEM] * 5 + [ANY_SPACE] * 8,
        out_specs=(ANY_SPACE, ANY_SPACE, ANY_SPACE, IN_VMEM, ANY_SPACE),
        scratch_shapes=[
            pltpu.VMEM(WIDE, bf), *whole, pltpu.VMEM((4, 4, 2, 3, 8, HALF), bf), *whole, *lands,
            pltpu.VMEM((24, HALF), f32),
            pltpu.VMEM((2, 4, 6, HALF), f32),
            pltpu.VMEM((3, 8, HALF), f32),
            pltpu.VMEM((2, 16, 768), f32),
            pltpu.VMEM((4, 16, 768), bf),
            pltpu.VMEM((4, 16, 768), bf),
            pltpu.VMEM((8, 16, 768), bf),
            pltpu.VMEM((2, 3, 2, TILE, 768), bf),
            pltpu.VMEM((3, 2, TILE, 768), bf),
            pltpu.VMEM((2, 2, TILE, 768), bf),
            pltpu.VMEM((TILE, 768), bf),
            pltpu.VMEM((TILE, 768), bf),
            pltpu.VMEM((TILE, 768), f32),
            pltpu.VMEM((2, 12, TILE, HALF), bf),
            pltpu.VMEM((12, TILE, 768), bf),
            pltpu.VMEM((3, 768, HALF), bf),
            pltpu.VMEM((2, 12, TILE, HALF), bf),
            pltpu.VMEM((2, 8, TILE, 128), f32),
            pltpu.VMEM((2, TILE, HALF), bf),
            pltpu.VMEM((6, 128, TILE), f32),
            pltpu.VMEM((3, 768, HALF), f32),
            pltpu.VMEM((1, HALF), f32),
            pltpu.VMEM((1, HALF), f32),
            pltpu.VMEM((2, 1, TILE), jnp.int32),
            pltpu.VMEM((12, TILE, 1), jnp.int32),
            pltpu.VMEM((2, TILE, HALF), bf),
            dma((12, 3)), dma((12, 3)), dma((12, 3)), dma((3, 2, 8, 3)), dma((3, 2, 8, 3)), dma((6, 2, 3)), dma((6, 2, 3)),
            dma((2, 8)), dma((2, 7)),
            dma((2,)), dma((3,)), dma((4, 8)), dma((4, 8)), dma((8,)), dma((8,)), dma((1,)), dma((6,)), dma((1,)), dma((1,)),
        ],
        compiler_params=pltpu.CompilerParams(collective_id=2, has_side_effects=True, vmem_limit_bytes=63 << 20),
    )(lengths, q_heads, o_heads, lse, gv, d_att, kv, window, first, dwo, g1, g2, base)


def dot32(a, b):
    return jnp.dot(a, b, preferred_element_type=jnp.float32)


def lanes_low(rows):
    return lax.broadcasted_iota(jnp.int32, (rows, 128), 1) < HEAD_DIM


def across_lanes(a, b):
    return lax.dot_general(a, b, (((1,), (1,)), ((), ())), preferred_element_type=jnp.float32)


def flipped(a):
    return jnp.swapaxes(a, 0, 1)


def norm_parts(resid):
    centred = resid - jnp.mean(resid, axis=1, keepdims=True)
    inverse = lax.rsqrt(jnp.mean(centred * centred, axis=1, keepdims=True) + NORM_EPS)
    return centred * inverse, inverse


def norm_back(upstream, gain, n, inverse):
    e = upstream * gain
    return inverse * (e - jnp.mean(e, axis=1, keepdims=True) - n * jnp.mean(e * n, axis=1, keepdims=True))


def row_sum(a):
    return jnp.sum(a, axis=0, keepdims=True)


def mlp_kernel(
    att_ref, tok_ref, cot_ref, rows, bias_in, first, second, third,
    out_ref, d_one_ref, d_att_ref, dwo_ref, dw_in_out, dw_down_out, sums_ref,
    dw_in_ref, dw_down_ref, out_sem,    w_out, w_in, w_down, n_one, low, low_flip, slope, active, wide, sem,
):
    f32, bf = jnp.float32, jnp.bfloat16
    loads = [pltpu.make_async_copy(first.at[:, 3], w_out, sem.at[0])]
    loads += [pltpu.make_async_copy(second, w_in, sem.at[1]), pltpu.make_async_copy(third, w_down, sem.at[2])]
    for cp in loads:
        cp.start()

    def row(n):
        return rows[n : n + 1]

    halves = (slice(0, HALF), slice(HALF, 768))
    loads[0].wait()
    att = att_ref[...]
    for h in range(2):
        wide[:, halves[h]] = dot32(att, w_out[h])
    one, inverse_one = norm_parts(tok_ref[...].astype(f32) + (wide[...] + row(2)))
    n_one[...] = one
    normed = one * row(3) + row(4)
    low[...] = normed.astype(bf)
    low_flip[...] = flipped(low[...])
    wide[...] = normed + row(5)
    loads[1].wait()
    loads[2].wait()

    def up(m, carry):
        h = dot32(low[...], w_in[lax.rem(m, 2), m // 2]) + bias_in[m]
        cdf = 0.5 * (1.0 + lax.erf(h * 0.7071067811865476))
        slope[m] = cdf + h * jnp.exp(h * h * -0.5) * 0.3989422804014327
        a = (h * cdf).astype(bf)
        active[m] = flipped(a)
        for k in range(2):
            wide[:, halves[k]] += dot32(a, w_down[k, m])
        return carry

    lax.fori_loop(0, 8, up, 0)
    two, inverse_two = norm_parts(wide[...])
    out_ref[...] = (two * row(6) + row(7)).astype(bf)
    upstream = cot_ref[...].astype(f32)
    sums_ref[0:2] = jnp.zeros((2, 768), f32)
    sums_ref[12:16] = jnp.zeros((4, 768), f32)
    sums_ref[6:7] = row_sum(upstream * two)
    sums_ref[7:8] = row_sum(upstream)
    d_two = norm_back(upstream, row(6), two, inverse_two)
    sums_ref[5:6] = row_sum(d_two)
    d_low = d_two.astype(bf)
    wide[...] = d_two

    def down(m, carry):
        d_active = None
        for k in range(2):
            d_half = d_low[:, halves[k]]
            dw_down_ref[k, m] = dot32(active[m], d_half).astype(bf)
            part = across_lanes(d_half, w_down[k, m])
            d_active = part if d_active is None else d_active + part
        d_hidden = (d_active * slope[m]).astype(bf)
        sums_ref[pl.ds(8 + m // 2, 1), pl.ds(pl.multiple_of(lax.rem(m, 2) * HALF, 128), HALF)] = row_sum(d_hidden.astype(f32))
        dw_in_ref[lax.rem(m, 2), m // 2] = dot32(low_flip[...], d_hidden).astype(bf)
        for cp in leaving(m):
            cp.start()
        wide[...] += across_lanes(d_hidden, w_in[lax.rem(m, 2), m // 2])
        return carry

    def leaving(m):
        piece = lax.rem(m, 2), m // 2
        return [
            pltpu.make_async_copy(dw_in_ref.at[piece], dw_in_out.at[piece], out_sem.at[m, 0]),
            pltpu.make_async_copy(dw_down_ref.at[0, m], dw_down_out.at[0, m], out_sem.at[m, 1]),
            pltpu.make_async_copy(dw_down_ref.at[1, m], dw_down_out.at[1, m], out_sem.at[m, 2]),
        ]

    def left(m, carry):
        for cp in leaving(m):
            cp.wait()
        return carry

    lax.fori_loop(0, 8, down, 0)
    d_normed = wide[...]
    one = n_one[...]
    sums_ref[3:4] = row_sum(d_normed * one)
    sums_ref[4:5] = row_sum(d_normed)
    d_one = norm_back(d_normed, row(3), one, inverse_one)
    d_one_ref[...] = d_one
    sums_ref[2:3] = row_sum(d_one)
    d_low = d_one.astype(bf)
    att_flip = flipped(att_ref[...])
    d_att = None
    for h in range(2):
        d_half = d_low[:, halves[h]]
        dwo_ref[h] = dot32(att_flip, d_half).astype(bf)
        part = across_lanes(d_half, w_out[h])
        d_att = part if d_att is None else d_att + part
    d_att_ref[...] = d_att.astype(bf)
    lax.fori_loop(0, 8, left, 0)


def mlp(att, tokens, cotangent, rows, bias_in, first, second, third):
    f32, bf = jnp.float32, jnp.bfloat16
    return pl.pallas_call(
        mlp_kernel,
        name="mlp",
        in_specs=[IN_VMEM] * 5 + [ANY_SPACE] * 3,
        out_specs=(IN_VMEM,) * 4 + (ANY_SPACE,) * 2 + (IN_VMEM,),
        out_shape=(
            jax.ShapeDtypeStruct((TILE, 768), bf),
            jax.ShapeDtypeStruct((TILE, 768), f32),
            jax.ShapeDtypeStruct((TILE, 768), bf),
            jax.ShapeDtypeStruct((2, 768, HALF), bf),
            jax.ShapeDtypeStruct((2, 4, 768, HALF), bf),
            jax.ShapeDtypeStruct((2, 8, HALF, HALF), bf),
            jax.ShapeDtypeStruct((16, 768), f32),
        ),
        scratch_shapes=[
            pltpu.VMEM((2, 4, 768, HALF), bf),
            pltpu.VMEM((2, 8, HALF, HALF), bf),
            pltpu.SemaphoreType.DMA((8, 3)),
            pltpu.VMEM((2, 768, HALF), bf),
            pltpu.VMEM((2, 4, 768, HALF), bf),
            pltpu.VMEM((2, 8, HALF, HALF), bf),
            pltpu.VMEM((TILE, 768), f32),
            pltpu.VMEM((TILE, 768), bf),
            pltpu.VMEM((768, TILE), bf),
            pltpu.VMEM((8, TILE, HALF), f32),
            pltpu.VMEM((8, HALF, TILE), bf),
            pltpu.VMEM((TILE, 768), f32),
            pltpu.SemaphoreType.DMA((3,)),
        ],
        compiler_params=pltpu.CompilerParams(vmem_limit_bytes=58 << 20),
    )(att, tokens, cotangent, rows, bias_in, first, second, third)


def body(
    tokens, w_qkv, bias_q, bias_v, w_out, bias_out, gain_one, shift_one, w_in, bias_in,
    w_down, bias_down, gain_two, shift_two, doc_lengths, cotangent,
):
    shard = lax.axis_index("shard")
    f32 = jnp.float32
    width = tokens.shape[1]

    vectors = (bias_q, bias_v, bias_out, gain_one, shift_one, bias_down, gain_two, shift_two)
    vec = jnp.concatenate(
        [
            jnp.stack(vectors).astype(f32),
            jnp.pad(bias_in.astype(f32).reshape(1, 24), ((0, 7), (0, 0))),
            jnp.zeros((8, 98), f32),
        ],
        axis=1,
    )
    cat = jnp.stack([jnp.concatenate([w_qkv, w_out], axis=1), w_in])
    lengths = doc_lengths.reshape(1, 128)
    first, second, third, rows, hidden_bias, window, kv, q_heads, o_heads, lse, attended = front(
        lengths, cat, w_down.reshape(3, 8, width), vec, tokens
    )
    first = first.reshape(2, 4, width, HALF)
    second = second.reshape(2, 4, width, HALF)
    third = third.reshape(2, 8, HALF, HALF)
    window = window.reshape(12, TILE, width)
    layer_out, d_one, d_att, dw_out, dw_in, dw_down, sums = mlp(
        attended, tokens, cotangent, rows, hidden_bias, first, second, third
    )
    sum_first, sum_in, sum_down, sum_vec, grad_tokens = back(
        lengths, q_heads, o_heads, lse, sums, d_att, kv, window, first,
        dw_out.reshape(2, 4, 4, 2, 3, 8, HALF), dw_in.reshape(2, *WIDE), dw_down.reshape(2, *TALL), d_one,
    )
    own = lax.dynamic_slice(sum_vec, (0, 6 * shard), (8, 6))
    own_in = lax.dynamic_slice(sum_vec[8:12].reshape(-1), (24 * shard,), (24,))
    return (
        layer_out, grad_tokens, sum_first[:, : 3 * width], own[0], own[1], sum_first[:, 3 * width :],
        own[2], own[3], own[4], sum_in, own_in, sum_down.reshape(24, width), own[5], own[6], own[7],
    )


def solution(mesh):
    both, own = P(("shard", "seq"), None), P("shard")
    rows = P("shard", None)
    return jax.shard_map(
        body,
        mesh=mesh,
        in_specs=(both, rows, own, own, rows, own, own, own, rows, own, rows, own, own, own, P(), both),
        out_specs=(both, both, rows, own, own, rows, own, own, own, rows, own, rows, own, own, own),
        check_vma=False,
    )
```
